32 devices in a mesh: narrow: 2 (over x), wide: 16 (over z, y, core).
Axes of the slice: x: 2, y: 2, z: 4, core: 2. Of those that a mesh axis runs over, the one named last changes fastest.
Arguments:
- hidden_in: bfloat16 [8192, 768], P(('narrow', 'wide')), may hold values from -6 to 6
- masked: int32 [8192], P(('narrow', 'wide')), may hold values 0 or 1
- token_ids: int32 [8192], P(('narrow', 'wide')), may hold values from 0 to 4095
- token_table: bfloat16 [4096, 768], replicated, may hold values from -6 to 6
- qkv_weight: bfloat16 [768, 2304], P('wide'), may hold values from -0.21875 to 0.21875
- qv_bias: bfloat16 [1536], P('wide'), may hold values from -3 to 3
- out_weight: bfloat16 [768, 768], P('wide'), may hold values from -0.625 to 0.625
- out_bias: bfloat16 [768], P('wide'), may hold values from -2 to 2
- norm1_gain: bfloat16 [768], P('wide'), may hold values from 0.5 to 1.5
- norm1_bias: bfloat16 [768], P('wide'), may hold values from -2 to 2
- ffn_in_weight: bfloat16 [768, 6144], P('wide'), may hold values from -0.21875 to 0.21875
- ffn_in_bias: bfloat16 [6144], P('wide'), may hold values from -2 to 2
- ffn_out_weight: bfloat16 [3072, 768], P('wide'), may hold values from -0.109375 to 0.109375
- ffn_out_bias: bfloat16 [768], P('wide'), may hold values from -2 to 2
- norm2_gain: bfloat16 [768], P('wide'), may hold values from 0.5 to 1.5
- norm2_bias: bfloat16 [768], P('wide'), may hold values from -2 to 2
- out_cotangent: bfloat16 [8192, 768], P(('narrow', 'wide')), may hold values from -6 to 6
Outputs:
- layer_out: bfloat16 [8192, 768], P(('narrow', 'wide'))
- input_grad: float32 [8192, 768], P(('narrow', 'wide'))
- grad_qkv_weight: float32 [768, 2304], P('wide')
- grad_qv_bias: float32 [1536], P('wide')
- grad_out_weight: float32 [768, 768], P('wide')
- grad_out_bias: float32 [768], P('wide')
- grad_norm1_gain: float32 [768], P('wide')
- grad_norm1_bias: float32 [768], P('wide')
- grad_ffn_in_weight: float32 [768, 6144], P('wide')
- grad_ffn_in_bias: float32 [6144], P('wide')
- grad_ffn_out_weight: float32 [3072, 768], P('wide')
- grad_ffn_out_bias: float32 [768], P('wide')
- grad_norm2_gain: float32 [768], P('wide')
- grad_norm2_bias: float32 [768], P('wide')
The draws below stay inside these ranges and needn't reach their ends.
All inputs are finite; a program needn't handle non-finite values. No bound on the sum of `masked` on one device may be relied on, other than what follows from the above.
Results may differ from the reference program's by a relative error of at most 0.015.
Values may be sent and summed in bfloat16 or wider, within the bound.
No kernel may reach another device: no remote copies, remote signals or barrier semaphores. Data moves between devices by JAX's collectives and lax.ppermute only.
A program may use at most 256 MiB of HBM per device.

```python
import math
import jax
import jax.numpy as jnp
from jax import lax

D = 768
HEADS = 12
HEAD_DIM = 64
FF = 3072
VOCAB = 4096
SEQ = 128
TOKENS = 8192


def set_ends(values, rng, smallest, high):
    longest = values.shape.index(max(values.shape))
    spots = []
    for shift in (0, 1):
        where = [jax.random.randint(jax.random.fold_in(rng, axis), (), 0, length) for axis, length in enumerate(values.shape)]
        where[longest] = (where[longest] + shift) % values.shape[longest]
        spots.append(tuple(where))
    return values.at[spots[0]].set(smallest).at[spots[1]].set(high)


def block_scale(rng, shape, shards, low, top_value):
    level = 1.0
    for axis_at, blocks in shards:
        heights = jax.random.uniform(jax.random.fold_in(jax.random.fold_in(rng, 6), axis_at), (blocks,), jnp.float32, low / len(shards), top_value / len(shards))
        level = level * jnp.repeat(jnp.exp(heights), shape[axis_at] // blocks).reshape((-1,) + (1,) * (len(shape) - 1 - axis_at))
    return level


def noise(stream_key, shape, width, most, cuts=(), held_as=jnp.bfloat16):
    drawn = jax.random.normal(stream_key, shape, jnp.float32) * width
    if len(cuts) > 0:
        drawn = block_scale(stream_key, shape, cuts, -0.22, 0.18) * drawn
    return jnp.clip(drawn, min=-most, max=most).astype(held_as)


def setup_inputs(seed: int = 0) -> dict:
    key_of = jax.random.split(jax.random.key(seed), 18)
    return {
        "hidden_in": noise(key_of[0], (TOKENS, D), 1.0, 6.0, ((0, 32),)),
        "masked": set_ends((jax.random.randint(key_of[1], (TOKENS,), 0, 20) < 3).astype(jnp.int32), jax.random.fold_in(key_of[1], 1), 0, 1),
        "token_ids": set_ends(jax.random.randint(key_of[2], (TOKENS,), 0, VOCAB), jax.random.fold_in(key_of[2], 1), 0, VOCAB - 1).astype(jnp.int32),
        "token_table": noise(key_of[3], (VOCAB, D), 1.0, 6.0),
        "qkv_weight": noise(key_of[4], (D, 3 * D), D ** -0.5, 0.21875, ((0, 16),)),
        "qv_bias": noise(key_of[5], (2 * D,), 0.5, 3.0, ((0, 16),)),
        "out_weight": noise(key_of[6], (D, D), (D // 8) ** -0.5, 0.625, ((0, 16),)),
        "out_bias": noise(key_of[7], (D,), 0.3, 2.0, ((0, 16),)),
        "norm1_gain": jnp.clip(1.0 + 0.1 * jax.random.normal(key_of[8], (D,), jnp.float32), 0.5, 1.5).astype(jnp.bfloat16),
        "norm1_bias": noise(key_of[9], (D,), 0.3, 2.0, ((0, 16),)),
        "ffn_in_weight": noise(key_of[10], (D, 2 * FF), D ** -0.5, 0.21875, ((0, 16),)),
        "ffn_in_bias": noise(key_of[11], (2 * FF,), 0.3, 2.0, ((0, 16),)),
        "ffn_out_weight": noise(key_of[12], (FF, D), FF ** -0.5, 0.109375, ((0, 16),)),
        "ffn_out_bias": noise(key_of[13], (D,), 0.3, 2.0, ((0, 16),)),
        "norm2_gain": jnp.clip(1.0 + 0.1 * jax.random.normal(key_of[14], (D,), jnp.float32), 0.5, 1.5).astype(jnp.bfloat16),
        "norm2_bias": noise(key_of[15], (D,), 0.3, 2.0, ((0, 16),)),
        "out_cotangent": noise(key_of[16], (TOKENS, D), 1.0, 6.0, ((0, 32),)),
    }


EPS = 1e-12
PRECISE = lax.Precision.HIGHEST

@jax.custom_vjp
def low(v):
    return lax.optimization_barrier(v.astype(jnp.bfloat16)).astype(jnp.float32)

@jax.custom_vjp
def low_back(v):
    return v

def low_keep(v):
    return (low(v), None)

def low_pass(kept, grad):
    return (grad,)

def back_keep(v):
    return (v, None)

def back_low(kept, grad):
    return (low(grad),)
low.defvjp(low_keep, low_pass)
low_back.defvjp(back_keep, back_low)

def alibi_slopes(count):
    power = 2 ** int(math.floor(math.log2(count)))
    values = [2.0 ** (-8.0 * (number + 1) / power) for number in range(power)]
    if power < count:
        extra = [2.0 ** (-8.0 * (number + 1) / (2 * power)) for number in range(2 * power)]
        values = values + extra[0::2][:count - power]
    return values

def alibi_bias(count, length):
    slopes = jnp.array(alibi_slopes(count), jnp.float32)
    position = jnp.arange(length)
    distance = jnp.abs(position[:, None] - position[None, :]).astype(jnp.float32)
    return -slopes[:, None, None] * distance[None]

def layer_norm(values, gain, shift):
    average = lax.optimization_barrier(jnp.mean(values, -1, keepdims=True))
    center = values - average
    variance = lax.optimization_barrier(jnp.mean(center * center, -1, keepdims=True))
    return center * lax.rsqrt(variance + EPS) * gain + shift

def forward(params, inputs, replaced, chosen, alibi):
    qkv_weight, qv_bias, out_weight, out_bias, gain_one, shift_one, in_weight, in_bias, down_weight, down_bias, gain_two, shift_two = params
    start = jnp.where(chosen, replaced, inputs)
    row_count = start.shape[0]
    seq_count = row_count // SEQ
    qkv_shift = jnp.concatenate([qv_bias[:D], jnp.zeros_like(qv_bias[:D]), qv_bias[D:]])
    projected = low(low_back(jnp.dot(start, qkv_weight, precision=PRECISE) + qkv_shift))
    heads_view = projected.reshape(seq_count, SEQ, 3, HEADS, HEAD_DIM)
    queries = heads_view[:, :, 0]
    key_rows = heads_view[:, :, 1]
    value_rows = heads_view[:, :, 2]
    raw_scores = low_back(jnp.einsum('sqhd,skhd->shqk', queries, key_rows, precision=PRECISE))
    scores = raw_scores * HEAD_DIM ** (-0.5) + alibi[None]
    attn_probs = low(jax.nn.softmax(scores, axis=-1))
    context = jnp.einsum('shqk,skhd->sqhd', attn_probs, value_rows, precision=PRECISE)
    context = low(low_back(context.reshape(row_count, D)))
    attn = low_back(jnp.dot(context, out_weight, precision=PRECISE) + out_bias)
    hidden_one = low(layer_norm(start + attn, gain_one, shift_one))
    gate_up = low_back(jnp.dot(hidden_one, in_weight, precision=PRECISE) + in_bias)
    hidden_act = low(jax.nn.gelu(gate_up[:, :FF], approximate=False) * gate_up[:, FF:])
    branch = low_back(jnp.dot(hidden_act, down_weight, precision=PRECISE) + down_bias)
    return layer_norm(hidden_one + branch, gain_two, shift_two)

def reference(hidden_in, masked, token_ids, token_table, qkv_weight, qv_bias, out_weight, out_bias, norm1_gain, norm1_bias, ffn_in_weight, ffn_in_bias, ffn_out_weight, ffn_out_bias, norm2_gain, norm2_bias, out_cotangent):
    params = tuple((weight.astype(jnp.float32) for weight in (qkv_weight, qv_bias, out_weight, out_bias, norm1_gain, norm1_bias, ffn_in_weight, ffn_in_bias, ffn_out_weight, ffn_out_bias, norm2_gain, norm2_bias)))
    total_seqs = hidden_in.shape[0] // SEQ
    limit = max(1, 4096 // SEQ)
    per_group = 1
    for number in range(1, limit + 1):
        if total_seqs % number == 0:
            per_group = number
    groups = total_seqs // per_group
    row_count = per_group * SEQ
    alibi = alibi_bias(HEADS, SEQ)
    pieces = (hidden_in.reshape(groups, row_count, D), masked.reshape(groups, row_count), token_ids.reshape(groups, row_count), out_cotangent.reshape(groups, row_count, D))

    def group_step(totals, group):
        inputs, marks, chosen_ids, cotangent = group
        replaced = jnp.take(token_table, chosen_ids.astype(jnp.int32), axis=0).astype(jnp.float32)
        chosen = (marks > 0)[:, None]

        def layer_fn(weights, rows_in):
            return forward(weights, rows_in, replaced, chosen, alibi)
        result, pullback = jax.vjp(layer_fn, params, inputs.astype(jnp.float32))
        grads, grad_in = pullback(cotangent.astype(jnp.float32))
        totals = jax.tree.map(lambda first, second: first + second, totals, grads)
        return (totals, (result.astype(jnp.bfloat16), grad_in))
    initial = tuple((jnp.zeros_like(weight) for weight in params))
    totals, (results, grads_in) = lax.scan(group_step, initial, pieces)
    return (results.reshape(-1, D), grads_in.reshape(-1, D), totals[0], totals[1], totals[2], totals[3], totals[4], totals[5], totals[6], totals[7], totals[8], totals[9], totals[10], totals[11])
```

```python
import functools
import math

import jax
import jax.numpy as jnp
from jax import lax
from jax.experimental import pallas as pl
from jax.experimental.pallas import tpu as pltpu
from jax.sharding import PartitionSpec as P

D = 768
HEADS = 12
HEAD_DIM = 64
FF = 3072
SEQ = 128
EPS = 1e-12
AXES = ("narrow", "wide")
F32 = jnp.float32
BF16 = jnp.bfloat16


def alibi_slopes(count):
    power = 2 ** int(math.floor(math.log2(count)))
    values = [2.0 ** (-8.0 * (number + 1) / power) for number in range(power)]
    extra = [2.0 ** (-8.0 * (number + 1) / (2 * power)) for number in range(2 * power)]
    values = values + extra[0::2][: count - power]
    return values


def alibi_bias(count, length):
    slopes = jnp.array(alibi_slopes(count), F32)
    position = jnp.arange(length)
    distance = jnp.abs(position[:, None] - position[None, :]).astype(F32)
    return -slopes[:, None, None] * distance[None]


class Place:
    def __init__(self, narrow, wide):
        self.narrow = narrow
        self.wide = wide
        self.chips = wide // 2
        self.direct = narrow == 2 and wide == 16
        self.ny = 2 if self.direct else 1
        self.nz = self.chips // self.ny
        across = lax.axis_index("narrow")
        along = lax.axis_index("wide")
        self.x = across
        self.core = along % 2
        self.chip = along // 2
        self.y = self.chip % self.ny
        self.z = self.chip // self.ny

    def move(self, values, target):
        pairs = []
        for x in range(self.narrow):
            for z in range(self.nz):
                for y in range(self.ny):
                    for c in range(2):
                        tx, tz, ty, tc = target(x, z, y, c)
                        source = ((x * self.nz + z) * self.ny + y) * 2 + c
                        goal = ((tx * self.nz + tz) * self.ny + ty) * 2 + tc
                        pairs.append((source, goal))
        return lax.ppermute(values, AXES, pairs)

    def swap_core(self, values):
        return self.move(values, lambda x, z, y, c: (x, z, y, 1 - c))

    def swap_narrow(self, values):
        return self.move(values, lambda x, z, y, c: (1 - x, z, y, c))

    def first(self, values):
        return self.move(
            values, lambda x, z, y, c: (1 - x, z, y, c) if c == 0 else (x, z, 1 - y, c)
        )

    def second(self, values):
        return self.move(
            values, lambda x, z, y, c: (x, z, 1 - y, c) if c == 0 else (1 - x, z, y, c)
        )

    def along_z(self, values, step):
        return self.move(values, lambda x, z, y, c: (x, (z + step) % self.nz, y, c))

    def spots(self, sign):
        m = jnp.arange(4)[:, None]
        s = jnp.arange(4)[None, :]
        on_first = (m == 1) | (m == 3)
        on_second = (m == 2) | (m == 3)
        flip_x = jnp.where(self.core == 0, on_first, on_second).astype(jnp.int32)
        flip_y = jnp.where(self.core == 0, on_second, on_first).astype(jnp.int32)
        z = (self.z + sign * s) % self.nz
        y = jnp.bitwise_xor(self.y, flip_y)
        x = jnp.bitwise_xor(self.x, flip_x)
        return (((z * self.ny + y) * 2) + x).reshape(16).astype(jnp.int32)


def place_kernel(spots, *refs):
    sources, out, hold, arrive, leave = refs[:4], refs[4], refs[5], refs[6], refs[7]
    blocks = [(m, s, m * 4 + s) for m in range(4) for s in range(4)]
    come = [pltpu.make_async_copy(sources[m].at[s], hold.at[at], arrive.at[at]) for m, s, at in blocks]
    for copy in come:
        copy.start()
    go = []
    for _, _, at in blocks:
        come[at].wait()
        copy = pltpu.make_async_copy(hold.at[at], out.at[spots[at]], leave.at[at])
        copy.start()
        go.append(copy)
    for copy in go:
        copy.wait()


def pick_kernel(spots, source, *refs):
    outs, hold, arrive, leave = refs[:4], refs[4], refs[5], refs[6]
    blocks = [(m, s, m * 4 + s) for m in range(4) for s in range(4)]
    come = [
        pltpu.make_async_copy(source.at[spots[at]], hold.at[at], arrive.at[at]) for _, _, at in blocks
    ]
    for copy in come:
        copy.start()
    go = []
    for m, s, at in blocks:
        come[at].wait()
        copy = pltpu.make_async_copy(hold.at[at], outs[m].at[s], leave.at[at])
        copy.start()
        go.append(copy)
    for copy in go:
        copy.wait()


def staging(shape, dtype):
    return [
        pltpu.VMEM((16,) + shape, dtype),
        pltpu.SemaphoreType.DMA((16,)),
        pltpu.SemaphoreType.DMA((16,)),
    ]


ANYWHERE = pl.BlockSpec(memory_space=pl.ANY)
SCALARS = pl.BlockSpec(memory_space=pltpu.SMEM)


def chip_gather(piece, place):
    if not place.direct:
        both = lax.all_gather(piece, AXES, axis=0, tiled=False)
        both = both.reshape((place.narrow, place.chips, 2) + piece.shape)
        both = jnp.where(place.core == 0, both[:, :, 0], both[:, :, 1])
        return jnp.swapaxes(both, 0, 1).reshape((place.chips * 2,) + piece.shape)
    column = [piece] + [place.along_z(piece, step) for step in (1, 2, 3)]
    column = jnp.stack(column)
    one = place.first(column)
    two = place.second(column)
    three = place.second(one)
    return pl.pallas_call(
        place_kernel,
        in_specs=[SCALARS] + [ANYWHERE] * 4,
        out_specs=ANYWHERE,
        out_shape=jax.ShapeDtypeStruct((16,) + piece.shape, piece.dtype),
        scratch_shapes=staging(piece.shape, piece.dtype),
    )(place.spots(-1), column, one, two, three)


def chip_reduce(chunks, place):
    if not place.direct:
        order = chunks.reshape((place.chips, 2) + chunks.shape[1:])
        order = jnp.swapaxes(order, 0, 1)
        zeros = jnp.zeros_like(order)
        order = jnp.where(
            place.core == 0, jnp.stack([order, zeros], 2), jnp.stack([zeros, order], 2)
        )
        order = order.reshape((-1,) + chunks.shape[1:]).astype(F32)
        mine = lax.psum_scatter(order, AXES, scatter_dimension=0, tiled=True)[0]
    else:
        shape = jax.ShapeDtypeStruct((4,) + chunks.shape[1:], chunks.dtype)
        zero, one, two, three = pl.pallas_call(
            pick_kernel,
            in_specs=[SCALARS, ANYWHERE],
            out_specs=[ANYWHERE] * 4,
            out_shape=[shape] * 4,
            scratch_shapes=staging(chunks.shape[1:], chunks.dtype),
        )(place.spots(1), chunks)
        got_three = place.second(three)
        got_two = place.second(two)
        one = (one.astype(F32) + got_three.astype(F32)).astype(BF16)
        got_one = place.first(one)
        zero = (zero.astype(F32) + got_two.astype(F32) + got_one.astype(F32)).astype(BF16)
        mine = zero[0].astype(F32)
        for step in (1, 2, 3):
            mine = mine + place.along_z(zero[step], step).astype(F32)
    mine = mine.astype(BF16)
    other = place.swap_narrow(mine)
    return jnp.where(place.x == 0, jnp.stack([mine, other]), jnp.stack([other, mine]))


def by_core(place, values, axis):
    return jnp.where(
        place.core == 0,
        lax.index_in_dim(values, 0, axis, keepdims=False),
        lax.index_in_dim(values, 1, axis, keepdims=False),
    )


def normed(values):
    average = jnp.mean(values, -1, keepdims=True)
    center = values - average
    variance = jnp.mean(center * center, -1, keepdims=True)
    scale = lax.rsqrt(variance + EPS)
    return center * scale, scale


def norm_back(grad, unit, scale, gain):
    e = grad * gain
    return scale * (
        e - jnp.mean(e, -1, keepdims=True) - unit * jnp.mean(e * unit, -1, keepdims=True)
    )


def dot(a, b, da, db):
    return lax.dot_general(a, b, (((da,), (db,)), ((), ())), preferred_element_type=F32)


def attention_scores(queries, key_rows, alibi):
    raw = jnp.einsum("sqhd,skhd->shqk", queries, key_rows, preferred_element_type=F32)
    return raw * HEAD_DIM ** (-0.5) + alibi[None]


SMALL = ("qv", "ob", "g1", "b1", "ib", "db", "g2", "b2")


def pack_small(vectors):
    flat = jnp.concatenate(vectors, 1)
    n, width = flat.shape
    half = width // 2
    lanes = -(-half // 128) * 128
    both = flat.reshape(n, 2, half)
    both = jnp.pad(both, ((0, 0), (0, 0), (0, lanes - half)))
    return both.reshape(n, 2, lanes // 128, 128)


def unpack_small(lanes, widths):
    n = lanes.shape[0]
    half = sum(widths) // 2
    flat = lanes.reshape(n, 2, -1)[:, :, :half].reshape(n, 2 * half)
    ends = []
    at = 0
    for width in widths:
        ends.append(flat[:, at : at + width])
        at += width
    return ends


def with_small(rows, small):
    n, r, _ = rows.shape
    halves = jnp.swapaxes(rows.reshape(n, r, 2, 2 * D), 1, 2)
    small = jnp.pad(small, ((0, 0), (0, 0), (0, r - small.shape[2]), (0, 0)))
    return jnp.concatenate([halves, small.astype(rows.dtype)], 3)


def body(
    hidden_in,
    masked,
    token_ids,
    token_table,
    qkv_weight,
    qv_bias,
    out_weight,
    out_bias,
    norm1_gain,
    norm1_bias,
    ffn_in_weight,
    ffn_in_bias,
    ffn_out_weight,
    ffn_out_bias,
    norm2_gain,
    norm2_bias,
    out_cotangent,
):
    place = Place(lax.axis_size("narrow"), lax.axis_size("wide"))
    wide = place.wide
    chips = place.chips
    owned = qkv_weight.shape[0]
    units = ffn_out_weight.shape[0]
    rows = hidden_in.shape[0]
    seqs = rows // SEQ
    alibi = alibi_bias(HEADS, SEQ)

    small = (qv_bias, out_bias, norm1_gain, norm1_bias, ffn_in_bias, ffn_out_bias, norm2_gain, norm2_bias)
    widths = [v.shape[0] for v in small]
    small_rows = -(-(sum(widths) // 2) // 128)
    attn_rows = max(owned, small_rows)
    attn_own = with_small(
        jnp.concatenate([qkv_weight, out_weight], 1)[None], pack_small([v[None] for v in small])
    )[0]
    attn_piece = jnp.where(place.x == 0, attn_own[0], attn_own[1])
    attn_core = chip_gather(attn_piece, place)
    attn_other = place.swap_core(attn_core)
    attn_all = jnp.where(
        place.core == 0, jnp.stack([attn_core, attn_other]), jnp.stack([attn_other, attn_core])
    )
    attn_all = attn_all.reshape(2, chips, 2, owned, attn_core.shape[-1])
    attn_all = attn_all.transpose(1, 0, 3, 2, 4)
    wide_rows = attn_all[..., : 2 * D].reshape(wide * owned, 4 * D)
    full_qkv = wide_rows[:, : 3 * D]
    full_out = wide_rows[:, 3 * D :]
    small_all = attn_all[:, :, :small_rows, :, 2 * D :].transpose(0, 1, 3, 2, 4)
    small_all = unpack_small(small_all.reshape(wide, 2, small_rows, 128), widths)
    qv, ob, g1, b1, ib, db, g2, b2 = [v.reshape(-1).astype(F32) for v in small_all]

    in_blocks = ffn_in_weight.reshape(owned, 2, chips, 2, units)
    in_mine = by_core(place, in_blocks, 3).reshape(owned, FF)
    in_give = by_core(place, jnp.flip(in_blocks, 3), 3).reshape(owned, FF)
    in_got = place.swap_core(in_give)
    in_piece = jnp.where(place.x == place.core, in_mine, in_got)
    full_in = chip_gather(in_piece, place).reshape(D, FF)
    in_shift = by_core(place, ib.reshape(2, chips, 2, units), 2).reshape(FF)

    half_units = units // 2
    down_piece = jnp.where(place.x == 0, ffn_out_weight[:half_units], ffn_out_weight[half_units:])
    full_down = chip_gather(down_piece, place).reshape(FF // 2, D)

    chosen = (masked > 0)[:, None]
    start = jnp.where(chosen, jnp.take(token_table, token_ids, axis=0), hidden_in)
    qkv_shift = jnp.concatenate([qv[:D], jnp.zeros((D,), F32), qv[D:]])
    projected = (dot(start, full_qkv, 1, 0) + qkv_shift).astype(BF16)
    heads_view = projected.reshape(seqs, SEQ, 3, HEADS, HEAD_DIM)
    queries = heads_view[:, :, 0]
    key_rows = heads_view[:, :, 1]
    value_rows = heads_view[:, :, 2]
    scores = attention_scores(queries, key_rows, alibi)
    top_score = jnp.max(scores, -1, keepdims=True)
    expo = jnp.exp(scores - top_score)
    probs = expo / jnp.sum(expo, -1, keepdims=True)
    probs_low = probs.astype(BF16)
    context = jnp.einsum("shqk,skhd->sqhd", probs_low, value_rows, preferred_element_type=F32)
    context = context.reshape(rows, D).astype(BF16)
    first_sum = start.astype(F32) + dot(context, full_out, 1, 0) + ob
    unit_one, scale_one = normed(first_sum)
    hidden_one = (unit_one * g1 + b1).astype(BF16)
    hidden_chip = jnp.concatenate([hidden_one, place.swap_core(hidden_one)])
    gate_up = dot(hidden_chip, full_in, 1, 0) + in_shift
    gate = gate_up[:, : FF // 2]
    up = gate_up[:, FF // 2 :]
    cdf = 0.5 + 0.5 * lax.erf(gate * (0.5**0.5))
    gelu = gate * cdf
    slope = cdf + gate * jnp.exp(-0.5 * gate * gate) * ((2 * math.pi) ** -0.5)
    hidden_act = (gelu * up).astype(BF16)
    gelu_low = gelu.astype(BF16)
    slope_up = (slope * up).astype(BF16)
    partial = dot(hidden_act, full_down, 1, 0)
    branch = partial[:rows] + place.swap_core(partial[rows:]) + db
    unit_two, scale_two = normed(hidden_one.astype(F32) + branch)
    layer_out = (unit_two * g2 + b2).astype(BF16)

    cotangent = out_cotangent.astype(F32)
    grad_g2 = jnp.sum(cotangent * unit_two, 0)
    grad_b2 = jnp.sum(cotangent, 0)
    grad_second = norm_back(cotangent, unit_two, scale_two, g2)
    grad_branch = grad_second.astype(BF16)
    grad_db = jnp.sum(grad_branch.astype(F32), 0)
    grad_chip = jnp.concatenate([grad_branch, place.swap_core(grad_branch)])
    grad_down = dot(hidden_act, grad_chip, 0, 0).astype(BF16)
    down_sum = chip_reduce(grad_down.reshape(chips * 2, half_units, D), place)
    grad_hidden = dot(grad_chip, full_down, 1, 1)
    grad_gate_up = jnp.concatenate(
        [grad_hidden * slope_up.astype(F32), grad_hidden * gelu_low.astype(F32)], 1
    ).astype(BF16)
    grad_ib = jnp.sum(grad_gate_up.astype(F32), 0)
    grad_in = dot(hidden_chip, grad_gate_up, 0, 0).astype(BF16)
    in_sum = chip_reduce(grad_in.reshape(chips * 2, owned, FF), place)
    partial = dot(grad_gate_up, full_in, 1, 1)
    grad_hidden_one = grad_second + partial[:rows] + place.swap_core(partial[rows:])
    grad_g1 = jnp.sum(grad_hidden_one * unit_one, 0)
    grad_b1 = jnp.sum(grad_hidden_one, 0)
    grad_first = norm_back(grad_hidden_one, unit_one, scale_one, g1)
    grad_attn = grad_first.astype(BF16)
    grad_ob = jnp.sum(grad_attn.astype(F32), 0)
    grad_out = dot(context, grad_attn, 0, 0)
    grad_context = dot(grad_attn, full_out, 1, 1).astype(BF16)
    grad_context = grad_context.reshape(seqs, SEQ, HEADS, HEAD_DIM)
    grad_probs = jnp.einsum("sqhd,skhd->shqk", grad_context, value_rows, preferred_element_type=F32)
    grad_values = jnp.einsum("shqk,sqhd->skhd", probs_low, grad_context, preferred_element_type=F32)
    grad_scores = probs * (grad_probs - jnp.sum(probs * grad_probs, -1, keepdims=True))
    grad_raw = (grad_scores * HEAD_DIM ** (-0.5)).astype(BF16)
    grad_queries = jnp.einsum("shqk,skhd->sqhd", grad_raw, key_rows, preferred_element_type=F32)
    grad_keys = jnp.einsum("shqk,sqhd->skhd", grad_raw, queries, preferred_element_type=F32)
    grad_qkv = jnp.stack([grad_queries, grad_keys, grad_values], 2).reshape(rows, 3 * D).astype(BF16)
    grad_qv = jnp.concatenate(
        [
            jnp.sum(grad_qkv[:, :D].astype(F32), 0),
            jnp.sum(grad_qkv[:, 2 * D :].astype(F32), 0),
        ]
    )
    grad_start = grad_first + dot(grad_qkv, full_qkv, 1, 1)
    input_grad = jnp.where(chosen, 0.0, grad_start)

    grad_attn_rows = jnp.concatenate([dot(start, grad_qkv, 0, 0), grad_out], 1).astype(BF16)
    ib_blocks = grad_ib.reshape(2, chips, units)
    zero_blocks = jnp.zeros_like(ib_blocks)
    grad_ib = jnp.where(
        place.core == 0,
        jnp.stack([ib_blocks, zero_blocks], 2),
        jnp.stack([zero_blocks, ib_blocks], 2),
    )
    smalls = [grad_qv, grad_ob, grad_g1, grad_b1, grad_ib, grad_db, grad_g2, grad_b2]
    smalls = pack_small([v.reshape(wide, -1) for v in smalls])
    attn_chunks = with_small(grad_attn_rows.reshape(wide, owned, 4 * D), smalls)
    attn_chunks = attn_chunks.reshape((chips, 2) + attn_chunks.shape[1:])
    keep = by_core(place, attn_chunks, 1)
    give = by_core(place, jnp.flip(attn_chunks, 1), 1)
    keep = (keep.astype(F32) + place.swap_core(give).astype(F32)).astype(BF16)
    keep = keep.reshape((chips * 2,) + keep.shape[2:])
    attn_sum = chip_reduce(keep, place)

    attn_rows = jnp.swapaxes(attn_sum[..., : 2 * D], 0, 1).reshape(owned, 4 * D).astype(F32)
    small_sum = unpack_small(attn_sum[None, :, :small_rows, 2 * D :].astype(F32), widths)
    s_qv, s_ob, s_g1, s_b1, s_ib, s_db, s_g2, s_b2 = [v.reshape(-1) for v in small_sum]

    mine = jnp.where(place.core == 0, in_sum[0], in_sum[1])
    give = jnp.where(place.core == 0, in_sum[1], in_sum[0])
    got = place.swap_core(give)
    mine = mine.reshape(owned, 2, chips, units)
    got = got.reshape(owned, 2, chips, units)
    in_rows = jnp.where(place.core == 0, jnp.stack([mine, got], 3), jnp.stack([got, mine], 3))
    in_rows = in_rows.reshape(owned, 2 * FF).astype(F32)

    return (
        layer_out,
        input_grad,
        attn_rows[:, : 3 * D],
        s_qv,
        attn_rows[:, 3 * D :],
        s_ob,
        s_g1,
        s_b1,
        in_rows,
        s_ib,
        down_sum.reshape(units, D).astype(F32),
        s_db,
        s_g2,
        s_b2,
    )


def solution(mesh):
    rows = P(("narrow", "wide"), None)
    marks = P(("narrow", "wide"))
    matrix = P("wide", None)
    vector = P("wide")
    in_specs = (rows, marks, marks, P(), matrix, vector, matrix, vector, vector, vector)
    in_specs = in_specs + (matrix, vector, matrix, vector, vector, vector, rows)
    out_specs = (rows, rows, matrix, vector, matrix, vector, vector, vector)
    out_specs = out_specs + (matrix, vector, matrix, vector, vector, vector)
    return jax.shard_map(body, mesh=mesh, in_specs=in_specs, out_specs=out_specs, check_vma=False)
```

```python
import functools
import math

import jax
import jax.numpy as jnp
from jax import lax
from jax.experimental import pallas as pl
from jax.experimental.pallas import tpu as pltpu
from jax.sharding import PartitionSpec as P

D = 768
HEADS = 12
HEAD_DIM = 64
FF = 3072
SEQ = 128
EPS = 1e-12
AXES = ("narrow", "wide")
F32 = jnp.float32
BF16 = jnp.bfloat16


def alibi_slopes(count):
    power = 2 ** int(math.floor(math.log2(count)))
    values = [2.0 ** (-8.0 * (number + 1) / power) for number in range(power)]
    extra = [2.0 ** (-8.0 * (number + 1) / (2 * power)) for number in range(2 * power)]
    values = values + extra[0::2][: count - power]
    return values


class Place:
    def __init__(self, narrow, wide):
        self.narrow = narrow
        self.wide = wide
        self.chips = wide // 2
        self.direct = narrow == 2 and wide == 16
        self.ny = 2 if self.direct else 1
        self.nz = self.chips // self.ny
        across = lax.axis_index("narrow")
        along = lax.axis_index("wide")
        self.x = across
        self.core = along % 2
        self.chip = along // 2
        self.y = self.chip % self.ny
        self.z = self.chip // self.ny

    def move(self, values, target):
        pairs = []
        for x in range(self.narrow):
            for z in range(self.nz):
                for y in range(self.ny):
                    for c in range(2):
                        tx, tz, ty, tc = target(x, z, y, c)
                        source = ((x * self.nz + z) * self.ny + y) * 2 + c
                        goal = ((tx * self.nz + tz) * self.ny + ty) * 2 + tc
                        pairs.append((source, goal))
        return lax.ppermute(values, AXES, pairs)

    def swap_core(self, values):
        return self.move(values, lambda x, z, y, c: (x, z, y, 1 - c))

    def swap_narrow(self, values):
        return self.move(values, lambda x, z, y, c: (1 - x, z, y, c))

    def swap_y(self, values):
        return self.move(values, lambda x, z, y, c: (x, z, 1 - y, c))

    def first(self, values):
        return self.move(
            values, lambda x, z, y, c: (1 - x, z, y, c) if c == 0 else (x, z, 1 - y, c)
        )

    def second(self, values):
        return self.move(
            values, lambda x, z, y, c: (x, z, 1 - y, c) if c == 0 else (1 - x, z, y, c)
        )

    def diagonal(self, values):
        return self.move(values, lambda x, z, y, c: (1 - x, z, 1 - y, c))

    def along_z(self, values):
        lines = [
            [(z * self.ny + y) * 2 + c for z in range(self.nz)] for y in range(self.ny) for c in range(2)
        ]
        return lax.all_to_all(
            values, "wide", split_axis=0, concat_axis=0, axis_index_groups=lines, tiled=True
        )

    def spread_z(self, values):
        return self.along_z(jnp.broadcast_to(values[None], (self.nz,) + values.shape))

    def spots(self, core):
        if not self.direct:
            at = jnp.arange(16, dtype=jnp.int32)
            return at // 2, at % 2
        m = jnp.arange(16) // 4
        z = jnp.arange(16) % 4
        on_first = (m == 1) | (m == 3)
        on_second = (m == 2) | (m == 3)
        flip_x = jnp.where(core == 0, on_first, on_second).astype(jnp.int32)
        flip_y = jnp.where(core == 0, on_second, on_first).astype(jnp.int32)
        y = jnp.bitwise_xor(self.y, flip_y)
        x = jnp.bitwise_xor(self.x, flip_x)
        return (z * self.ny + y).astype(jnp.int32), x.astype(jnp.int32)

    def flat_spots(self):
        chip, half = self.spots(self.core)
        return chip * 2 + half

    def plane_spots(self, y_first):
        if not self.direct:
            return jnp.arange(8, dtype=jnp.int32)
        at = jnp.arange(8)
        flip, z = (at % 2, at // 2) if y_first else (at // 4, at % 4)
        return (z * self.ny + jnp.bitwise_xor(self.y, flip)).astype(jnp.int32)

    def row_spots(self, core):
        chip, half = self.spots(core)
        return jnp.stack([chip * 2 + core, half])


def place_kernel(spots, *refs):
    sources, out, hold, arrive, leave = refs[:4], refs[4], refs[5], refs[6], refs[7]
    blocks = [(m, s, m * 4 + s) for m in range(4) for s in range(4)]
    come = [pltpu.make_async_copy(sources[m].at[s], hold.at[at], arrive.at[at]) for m, s, at in blocks]
    for copy in come:
        copy.start()
    go = []
    for _, _, at in blocks:
        come[at].wait()
        copy = pltpu.make_async_copy(hold.at[at], out.at[spots[at]], leave.at[at])
        copy.start()
        go.append(copy)
    for copy in go:
        copy.wait()


ANYWHERE = pl.BlockSpec(memory_space=pl.ANY)
SCALARS = pl.BlockSpec(memory_space=pltpu.SMEM)
VECTORS = pl.BlockSpec(memory_space=pltpu.VMEM)
PAIRS = HEADS // 2
HALF = 2 * D
LANES = 128
WIDE = HALF + LANES


def dot(a, b, da, db):
    return lax.dot_general(a, b, (((da,), (db,)), ((), ())), preferred_element_type=F32)


def call(kernel, ins, outs, scratch, flops, moved, *operands):
    return pl.pallas_call(
        kernel,
        in_specs=ins,
        out_specs=[spec for spec, _, _ in outs],
        out_shape=[jax.ShapeDtypeStruct(shape, dtype) for _, shape, dtype in outs],
        scratch_shapes=scratch,
        cost_estimate=pl.CostEstimate(flops=flops, transcendentals=0, bytes_accessed=moved),
        compiler_params=pltpu.CompilerParams(vmem_limit_bytes=56 * 1024 * 1024),
    )(*operands)


def normed(values):
    average = jnp.mean(values, -1, keepdims=True)
    center = values - average
    variance = jnp.mean(center * center, -1, keepdims=True)
    scale = lax.rsqrt(variance + EPS)
    return center * scale, scale


def norm_back(grad, unit, scale, gain):
    e = grad * gain
    return scale * (
        e - jnp.mean(e, -1, keepdims=True) - unit * jnp.mean(e * unit, -1, keepdims=True)
    )


def split_heads(pair):
    low = lax.broadcasted_iota(jnp.int32, pair.shape, 1) < HEAD_DIM
    zero = jnp.zeros_like(pair)
    return jnp.concatenate([jnp.where(low, pair, zero), jnp.where(low, zero, pair)], 0)


def join_heads(stacked):
    rows = stacked.shape[0] // 2
    low = lax.broadcasted_iota(jnp.int32, (rows, LANES), 1) < HEAD_DIM
    return jnp.where(low, stacked[:rows], stacked[rows:])


def block_list(arrays):
    blocks = []
    for array in arrays:
        for i in range(array.shape[0]):
            if len(array.shape) == 4:
                blocks += [array.at[i, j] for j in range(array.shape[1])]
            else:
                blocks.append(array.at[i])
    return blocks


def fetch_rows(sources, spots, hold, sems):
    copies = []
    for at, block in enumerate(block_list(sources)):
        size = block.shape[0]
        to = pl.multiple_of(spots[at] * size, size)
        copies.append(pltpu.make_async_copy(block, hold.at[pl.ds(to, size)], sems.at[at]))
    for copy in copies:
        copy.start()
    return copies


def emit_rows(source, outs, spots, sems):
    copies = []
    for at, block in enumerate(block_list(outs)):
        size = block.shape[0]
        start = pl.multiple_of(spots[at] * size, size)
        copies.append(pltpu.make_async_copy(source.at[pl.ds(start, size)], block, sems.at[at]))
    for copy in copies:
        copy.start()
    for copy in copies:
        copy.wait()


def fetch_attn(mine, other, core, hold, sems):
    copies = []
    size = mine.shape[1]
    for side, source in enumerate((mine, other)):
        parity = core[0] if side == 0 else 1 - core[0]
        for chip in range(source.shape[0] // 2):
            row = pl.multiple_of((chip * 2 + parity) * size, size)
            for half in range(2):
                at = (chip * 2 + side) * 2 + half
                copies.append(
                    pltpu.make_async_copy(
                        source.at[chip * 2 + half],
                        hold.at[pl.ds(row, size), pl.ds(half * WIDE, WIDE)],
                        sems.at[at],
                    )
                )
    for copy in copies:
        copy.start()
    for copy in copies:
        copy.wait()


VALUE_AT = WIDE
OUT_AT = WIDE + D


def attn_forward_kernel(
    start, even, odd, core, bias, shift, context, probs, qkv, unit, scale, hidden, hold, sems
):
    fetch_attn(even, odd, core, hold, sems)
    rows = start.shape[0]
    begin = start[...]
    for part, at in enumerate((0, D, VALUE_AT)):
        made = dot(begin, hold[:, at : at + D], 1, 0)
        if part != 1:
            made = made + bias[part // 2 : part // 2 + 1, :]
        qkv[:, part * D : (part + 1) * D] = made.astype(BF16)
    distance = jnp.abs(
        lax.broadcasted_iota(jnp.int32, (SEQ, SEQ), 0) - lax.broadcasted_iota(jnp.int32, (SEQ, SEQ), 1)
    ).astype(F32)
    slopes = alibi_slopes(HEADS)
    for s in range(rows // SEQ):
        span = slice(s * SEQ, (s + 1) * SEQ)
        for pair in range(PAIRS):
            lane = pair * LANES
            queries = qkv[span, lane : lane + LANES]
            keys = qkv[span, D + lane : D + lane + LANES]
            values = qkv[span, 2 * D + lane : 2 * D + lane + LANES]
            raw = dot(split_heads(queries), keys, 1, 1)
            fall = jnp.concatenate([distance * slopes[2 * pair], distance * slopes[2 * pair + 1]], 0)
            scores = raw * HEAD_DIM ** (-0.5) - fall
            expo = jnp.exp(scores - jnp.max(scores, -1, keepdims=True))
            made = expo / jnp.sum(expo, -1, keepdims=True)
            probs[s, pair] = made
            joined = join_heads(dot(made.astype(BF16), values, 1, 0))
            context[span, lane : lane + LANES] = joined.astype(BF16)
    first_sum = begin.astype(F32) + dot(context[...], hold[:, OUT_AT : OUT_AT + D], 1, 0)
    made, factor = normed(first_sum + shift[0:1, :])
    unit[...] = made
    scale[...] = factor
    hidden[...] = (made * shift[1:2, :] + shift[2:3, :]).astype(BF16)


def ffn_in_kernel(
    mine, h1, theirs, spots, w0, w1, w2, w3, shift, act, gelu_out, slope_out, hold, sems
):
    copies = fetch_rows((w0, w1, w2, w3), spots, hold, sems)
    both = jnp.concatenate([mine[...], h1[...], theirs[...]], 0)
    for copy in copies:
        copy.wait()
    width = act.shape[1]
    block = 256
    for at in range(0, width, block):
        cols = slice(at, at + block)
        more = slice(width + at, width + at + block)
        gate = dot(both, hold[:, cols], 1, 0) + shift[:, cols]
        up = dot(both, hold[:, more], 1, 0) + shift[:, more]
        cdf = 0.5 + 0.5 * lax.erf(gate * (0.5**0.5))
        gelu = gate * cdf
        slope = cdf + gate * jnp.exp(-0.5 * gate * gate) * ((2 * math.pi) ** -0.5)
        act[:, cols] = (gelu * up).astype(BF16)
        gelu_out[:, cols] = gelu.astype(BF16)
        slope_out[:, cols] = (slope * up).astype(BF16)


def ffn_down_kernel(act, spots, w0, mine, near, theirs, hold, sems):
    copies = fetch_rows((w0,), spots, hold, sems)
    for copy in copies:
        copy.wait()
    rows = mine.shape[0]
    theirs[...] = dot(act[2 * rows :, :], hold[...], 1, 0).astype(BF16)
    near[...] = dot(act[rows : 2 * rows, :], hold[...], 1, 0)
    mine[...] = dot(act[:rows, :], hold[...], 1, 0)


def turn_kernel(mine, core, got, hidden, vectors, cotangent, layer_out, second, branch, sums):
    part = mine[...] + core[: mine.shape[0], :].astype(F32) + got[...].astype(F32)
    total = hidden[...].astype(F32) + (part + vectors[0:1, :])
    unit, scale = normed(total)
    layer_out[...] = (unit * vectors[1:2, :] + vectors[2:3, :]).astype(BF16)
    grad = cotangent[...].astype(F32)
    back = norm_back(grad, unit, scale, vectors[1:2, :])
    second[...] = back
    low = back.astype(BF16)
    branch[...] = low
    sums[0:1, :] = jnp.sum(low.astype(F32), 0, keepdims=True)
    sums[1:2, :] = jnp.sum(grad * unit, 0, keepdims=True)
    sums[2:3, :] = jnp.sum(grad, 0, keepdims=True)


def down_grad_kernel(act, mine, g1, theirs, spots, p0, p1, hold, sems):
    both = jnp.concatenate([mine[...], g1[...], theirs[...]], 0)
    hold[...] = dot(act[...], both, 0, 0).astype(BF16)
    emit_rows(hold, (p0, p1), spots, sems)


def back_kernel(
    mine, g1, theirs, gelu, slope, spots, w0, in_spots, u0, u1, u2, u3,
    back, sums, part, near, other, hold, in_hold, sems, in_sems,
):
    copies = fetch_rows((w0,), spots, hold, sems)
    in_copies = fetch_rows((u0, u1, u2, u3), in_spots, in_hold, in_sems)
    both = jnp.concatenate([mine[...], g1[...], theirs[...]], 0)
    for copy in copies:
        copy.wait()
    width = gelu.shape[1]
    block = 256
    for at in range(0, width, block):
        cols = slice(at, at + block)
        more = slice(width + at, width + at + block)
        grad = dot(both, hold[cols, :], 1, 1)
        for cut, factor in ((cols, slope), (more, gelu)):
            low = (grad * factor[:, cols].astype(F32)).astype(BF16)
            back[:, cut] = low
            sums[:, cut] = jnp.sum(low.astype(F32), 0, keepdims=True)
    for copy in in_copies:
        copy.wait()
    rows = part.shape[0]
    other[...] = dot(back[2 * rows :, :], in_hold[...], 1, 1).astype(BF16)
    near[...] = dot(back[rows : 2 * rows, :], in_hold[...], 1, 1)
    part[...] = dot(back[:rows, :], in_hold[...], 1, 1)


def in_grad_kernel(hidden, h1, hidden_other, back, goal, p0, p1, made, out_sems):
    inputs = jnp.concatenate([hidden[...], h1[...], hidden_other[...]], 0)
    made[...] = dot(inputs, back[...], 0, 0).astype(BF16)
    emit_rows(made, (p0, p1), goal, out_sems)


def attn_backward_kernel(
    second, mine, part, got, unit, scale, gain, keep, context, probs, qkv, even, odd, core,
    input_grad, grad_attn, grad_qkv, sums, hold, grad_context, sems,
):
    fetch_attn(even, odd, core, hold, sems)
    rows = second.shape[0]
    grad = second[...] + mine[...] + part[:rows, :].astype(F32) + got[...].astype(F32)
    made = unit[...]
    sums[0:1, :] = jnp.sum(grad * made, 0, keepdims=True)
    sums[1:2, :] = jnp.sum(grad, 0, keepdims=True)
    first = norm_back(grad, made, scale[...], gain[...])
    low = first.astype(BF16)
    grad_attn[...] = low
    sums[2:3, :] = jnp.sum(low.astype(F32), 0, keepdims=True)
    grad_context[...] = dot(low, hold[:, OUT_AT : OUT_AT + D], 1, 1).astype(BF16)
    for s in range(rows // SEQ):
        span = slice(s * SEQ, (s + 1) * SEQ)
        for pair in range(PAIRS):
            lane = pair * LANES
            queries = split_heads(qkv[span, lane : lane + LANES])
            keys = qkv[span, D + lane : D + lane + LANES]
            values = qkv[span, 2 * D + lane : 2 * D + lane + LANES]
            outer = split_heads(grad_context[span, lane : lane + LANES])
            weight = probs[s, pair]
            grad_probs = dot(outer, values, 1, 1)
            inner = jnp.sum(weight * grad_probs, -1, keepdims=True)
            grad_raw = (weight * (grad_probs - inner) * HEAD_DIM ** (-0.5)).astype(BF16)
            grad_queries = join_heads(dot(grad_raw, keys, 1, 0))
            grad_keys = dot(grad_raw, queries, 0, 0)
            grad_values = dot(weight.astype(BF16), outer, 0, 0)
            grad_qkv[span, lane : lane + LANES] = grad_queries.astype(BF16)
            grad_qkv[span, D + lane : D + lane + LANES] = grad_keys.astype(BF16)
            grad_qkv[span, 2 * D + lane : 2 * D + lane + LANES] = grad_values.astype(BF16)
    sums[3:4, :] = jnp.sum(grad_qkv[:, :D].astype(F32), 0, keepdims=True)
    sums[4:5, :] = jnp.sum(grad_qkv[:, 2 * D :].astype(F32), 0, keepdims=True)
    total = first
    for part, at in enumerate((0, D, VALUE_AT)):
        total = total + dot(grad_qkv[:, part * D : (part + 1) * D], hold[:, at : at + D], 1, 1)
    input_grad[...] = total * keep[...]


SMALL_ROWS = 16
BIAS_ROW = 8


def attn_grad_kernel(
    start, grad_qkv, context, grad_attn, sums, turn_sums, in_sums, quarter, mine, theirs, *refs
):
    keep, give, hold, sems = refs[:4], refs[4], refs[5], refs[6]
    begin = start[...]
    size = give.shape[1]
    owners = D // size
    hold[:, HALF:WIDE] = jnp.zeros((D, LANES), BF16)
    hold[:, WIDE + HALF : 2 * WIDE] = jnp.zeros((D, LANES), BF16)
    tall = lax.broadcasted_iota(jnp.int32, (4, 2 * size), 0) == quarter[0]
    vectors = ((sums, 2), (sums, 0), (sums, 1), (turn_sums, 0), (turn_sums, 1), (turn_sums, 2))
    for owner in range(owners):
        at = owner * size
        lane = (owner % (owners // 2)) * 2 * size
        row = 3 + owner // (owners // 2)
        bias = in_sums[:, owner * 2 * size : (owner + 1) * 2 * size]
        wide = [sums[row : row + 1, lane : lane + 2 * size]]
        narrow = [ref[i : i + 1, at : at + size] for ref, i in vectors]
        narrow = jnp.concatenate(narrow + [jnp.zeros((1, size), F32)], 0)
        narrow = jnp.concatenate([narrow, jnp.zeros_like(narrow)], 1)
        made = jnp.concatenate(
            wide + [narrow, jnp.where(tall, bias, 0.0), jnp.zeros((4, 2 * size), F32)], 0
        )
        hold[at : at + SMALL_ROWS, HALF : HALF + 2 * size] = made.astype(BF16)
    for part, at in enumerate((0, D, VALUE_AT)):
        hold[:, at : at + D] = dot(begin, grad_qkv[:, part * D : (part + 1) * D], 0, 0).astype(BF16)
    hold[:, OUT_AT : OUT_AT + D] = dot(context[...], grad_attn[...], 0, 0).astype(BF16)
    copies = []
    for side, spots in enumerate((theirs, mine)):
        for at in range(16):
            row = pl.multiple_of(spots[0, at] * size, size)
            lane = pl.multiple_of(spots[1, at] * WIDE, LANES)
            copies.append(
                pltpu.make_async_copy(
                    hold.at[pl.ds(row, size), pl.ds(lane, WIDE)],
                    give.at[at] if side == 0 else keep[at // 4].at[at % 4],
                    sems.at[side * 16 + at],
                )
            )
    for copy in copies:
        copy.start()
    for copy in copies:
        copy.wait()


def tie(*values):
    return lax.optimization_barrier(values)


def square_gather(column, place):
    one = place.first(column)
    return column, one, place.second(column), place.second(one)


def halves(place, mine):
    mine = mine.astype(BF16)
    other = place.swap_narrow(mine)
    return jnp.where(place.x == 0, jnp.stack([mine, other]), jnp.stack([other, mine]))


def square_sum(blocks, place):
    zero, one, two, three = blocks
    one = sum_of([one, place.second(three)]).astype(BF16)
    zero = sum_of([zero, place.second(two), place.first(one)]).astype(BF16)
    return place.along_z(zero)


def plane_all(piece, place):
    whole = lax.all_gather(piece, "wide", axis=0, tiled=False)
    whole = whole.reshape((place.chips, 2) + piece.shape)
    return by_core(place, whole, 1).reshape(8, -1, piece.shape[-1])


def plane_across(blocks, size, place):
    if place.direct:
        return [place.swap_y(values) for values in blocks[1:]]
    order = jnp.concatenate(blocks).reshape(place.chips, 1, size, blocks[0].shape[-1])
    zeros = jnp.zeros_like(order)
    order = jnp.where(
        place.core == 0, jnp.concatenate([order, zeros], 1), jnp.concatenate([zeros, order], 1)
    )
    order = order.reshape((-1,) + order.shape[2:]).astype(F32)
    return [lax.psum_scatter(order, "wide", scatter_dimension=0, tiled=True)]


def plane_along(near, far, place):
    if not place.direct:
        return far[0]
    return place.along_z(sum_of([near, far[0]]).astype(BF16))


def sum_of(parts):
    total = parts[0].astype(F32)
    for i in range(1, len(parts)):
        total = total + parts[i].astype(F32)
    return total


def by_core(place, values, axis):
    return jnp.where(
        place.core == 0,
        lax.index_in_dim(values, 0, axis, keepdims=False),
        lax.index_in_dim(values, 1, axis, keepdims=False),
    )


def by_narrow(place, values, axis):
    return jnp.where(
        place.x == 0,
        lax.index_in_dim(values, 0, axis, keepdims=False),
        lax.index_in_dim(values, 1, axis, keepdims=False),
    )


def quarter_sum(near, theirs, rows, place):
    got = place.swap_core(theirs)
    near = (near + got[rows:].astype(F32)).astype(BF16)
    return got, place.swap_narrow(near)


def pack_small(vectors):
    flat = jnp.concatenate(vectors, 1)
    n, width = flat.shape
    half = width // 2
    lanes = -(-half // LANES) * LANES
    both = flat.reshape(n, 2, half)
    both = jnp.pad(both, ((0, 0), (0, 0), (0, lanes - half)))
    return both.reshape(n, 2, lanes // LANES, LANES)


def unpack_small(lanes, widths):
    n = lanes.shape[0]
    half = sum(widths) // 2
    flat = lanes.reshape(n, 2, -1)[:, :, :half].reshape(n, 2 * half)
    parts = []
    at = 0
    for width in widths:
        parts.append(flat[:, at : at + width])
        at += width
    return parts


def with_small(rows, small):
    r = rows.shape[0]
    both = jnp.swapaxes(rows.reshape(r, 2, HALF), 0, 1)
    small = jnp.pad(small, ((0, 0), (0, r - small.shape[1]), (0, 0)))
    return jnp.concatenate([both, small.astype(rows.dtype)], 2)


def gather_attn(own, place):
    full = lax.all_gather(own, "wide", axis=0, tiled=False)
    lanes = full[..., HALF:]
    full = jnp.swapaxes(full, 1, 2).reshape(8, 2, D // 16, 2, WIDE)
    full = full.transpose(1, 0, 3, 2, 4).reshape(2, 16, D // 16, WIDE)
    mine = jnp.where(place.core == 0, full[0], full[1])
    return mine, jnp.where(place.core == 0, full[1], full[0]), lanes


def place_attn(blocks, place):
    shape = (16,) + blocks[0].shape[1:]
    mine = pl.pallas_call(
        place_kernel,
        in_specs=[SCALARS] + [ANYWHERE] * 4,
        out_specs=ANYWHERE,
        out_shape=jax.ShapeDtypeStruct(shape, BF16),
        scratch_shapes=[
            pltpu.VMEM(shape, BF16),
            pltpu.SemaphoreType.DMA((16,)),
            pltpu.SemaphoreType.DMA((16,)),
        ],
    )(place.flat_spots(), *blocks)
    other = place.swap_core(mine)
    near, far = mine[:, :SMALL_ROWS, HALF:], other[:, :SMALL_ROWS, HALF:]
    lanes = jnp.where(place.core == 0, jnp.stack([near, far], 1), jnp.stack([far, near], 1))
    lanes = lanes.reshape((place.chips, 2, 2) + lanes.shape[2:])
    lanes = jnp.swapaxes(lanes, 1, 2).reshape((place.wide, 2) + lanes.shape[3:])
    return mine, other, lanes


def reduce_attn(keep, give, owned, place):
    mine = jnp.stack(keep).reshape(8, 2, D // 16, WIDE)
    other = give.reshape(8, 2, D // 16, WIDE)
    full = jnp.where(place.core == 0, jnp.stack([mine, other], 1), jnp.stack([other, mine], 1))
    full = full.transpose(0, 1, 3, 2, 4).reshape(place.wide, owned, 2, WIDE)
    full = jnp.swapaxes(full, 1, 2).astype(F32)
    full = lax.psum_scatter(full, "wide", scatter_dimension=0, tiled=True)[0]
    return lax.psum(full, "narrow").astype(BF16)


def body(
    hidden_in,
    masked,
    token_ids,
    token_table,
    qkv_weight,
    qv_bias,
    out_weight,
    out_bias,
    norm1_gain,
    norm1_bias,
    ffn_in_weight,
    ffn_in_bias,
    ffn_out_weight,
    ffn_out_bias,
    norm2_gain,
    norm2_bias,
    out_cotangent,
):
    place = Place(lax.axis_size("narrow"), lax.axis_size("wide"))
    wide = place.wide
    chips = place.chips
    owned = qkv_weight.shape[0]
    units = ffn_out_weight.shape[0]
    rows = hidden_in.shape[0]
    seqs = rows // SEQ

    chosen = (masked > 0)[:, None]
    replaced, ffn_in_weight = tie(jnp.take(token_table, token_ids, axis=0), ffn_in_weight)
    start = jnp.where(chosen, replaced, hidden_in)

    small = (qv_bias, out_bias, norm1_gain, norm1_bias, ffn_in_bias, ffn_out_bias, norm2_gain, norm2_bias)
    widths = [v.shape[0] for v in small]
    small_rows = -(-(sum(widths) // 2) // LANES)
    attn_own = with_small(
        jnp.concatenate([qkv_weight, out_weight], 1), pack_small([v[None] for v in small])[0]
    )
    half_units = units // 2
    in_blocks = ffn_in_weight.reshape(owned, 2, chips, 2, 2, half_units)
    in_blocks = by_narrow(place, in_blocks, 4)
    in_mine = by_core(place, in_blocks, 3).reshape(owned, FF // 2)
    in_give = by_core(place, jnp.flip(in_blocks, 3), 3).reshape(owned, FF // 2)
    in_got = place.swap_core(in_give)
    in_piece = jnp.where(
        place.core == 0, jnp.concatenate([in_mine, in_got]), jnp.concatenate([in_got, in_mine])
    )
    down_piece = by_narrow(place, ffn_out_weight.reshape(2, half_units, D), 0)
    if place.direct:
        attn_column = place.spread_z(by_narrow(place, attn_own, 0))
        down_got = place.swap_y(down_piece)
        attn_column, down_got, in_piece, start = tie(attn_column, down_got, in_piece, start)
        in_column = place.spread_z(in_piece)
        attn_blocks = square_gather(attn_column, place)
        *attn_blocks, in_column, down_got = tie(*attn_blocks, in_column, down_got)
        in_first, in_last = in_column[:2], in_column[2:]
        in_weights = [in_first, in_last, place.swap_y(in_first), place.swap_y(in_last)]
        down_weights = place.spread_z(jnp.stack([down_piece, down_got]))
        even, odd, lanes = place_attn(attn_blocks, place)
    else:
        even, odd, lanes = gather_attn(attn_own, place)
        whole = plane_all(in_piece, place)
        in_weights = [whole[:2], whole[2:4], whole[4:6], whole[6:]]
        whole = plane_all(down_piece, place)
        down_weights = whole.reshape(4, 2, -1, D)
    lanes = unpack_small(lanes[:, :, :small_rows], widths)
    qv, ob, g1, b1, ib, db, g2, b2 = [v.reshape(1, -1).astype(F32) for v in lanes]
    in_shift = by_narrow(place, by_core(place, ib.reshape(2, chips, 2, 2, half_units), 2), 2)
    in_shift = in_shift.reshape(1, FF // 2)
    in_come = place.plane_spots(False)
    down_come = place.plane_spots(True)
    leave = place.plane_spots(False)
    block_rows, quarter = D // 8, FF // 4
    eight = pltpu.SemaphoreType.DMA((8,))
    sixteen = pltpu.SemaphoreType.DMA((16,))
    thirty_two = pltpu.SemaphoreType.DMA((32,))
    in_hold = pltpu.VMEM((D, 2 * quarter), BF16)
    down_hold = pltpu.VMEM((quarter, D), BF16)
    attn_hold = pltpu.VMEM((D, 2 * WIDE), BF16)
    V, A, S = VECTORS, ANYWHERE, SCALARS

    core = place.core.reshape(1).astype(jnp.int32)

    context, probs, qkv, unit, scale, hidden = call(
        attn_forward_kernel,
        [V, A, A, S, V, V],
        [
            (V, (rows, D), BF16),
            (V, (seqs, PAIRS, 2 * SEQ, SEQ), F32),
            (V, (rows, 3 * D), BF16),
            (V, (rows, D), F32),
            (V, (rows, 1), F32),
            (V, (rows, D), BF16),
        ],
        [attn_hold, thirty_two],
        rows * D * D * 10,
        10 << 20,
        start,
        even,
        odd,
        core,
        qv.reshape(2, D),
        jnp.concatenate([ob, g1, b1]),
    )
    hidden, in_weights[2] = tie(hidden, in_weights[2])
    hidden_near = place.swap_narrow(hidden)
    hidden_other = place.swap_core(jnp.concatenate([hidden, hidden_near]))
    hidden_other, down_weights = tie(hidden_other, down_weights)
    act, gelu, slope = call(
        ffn_in_kernel,
        [V, V, V, S, A, A, A, A, V],
        [(V, (4 * rows, quarter), BF16)] * 3,
        [in_hold, eight],
        rows * D * FF * 8,
        12 << 20,
        hidden,
        hidden_near,
        hidden_other,
        in_come,
        *in_weights,
        in_shift,
    )
    part, near, theirs = call(
        ffn_down_kernel,
        [V, S, A],
        [(V, (rows, D), F32), (V, (rows, D), F32), (V, (2 * rows, D), BF16)],
        [down_hold, eight],
        rows * D * FF * 2,
        6 << 20,
        act,
        down_come,
        down_weights,
    )
    core_got, got = quarter_sum(near, theirs, rows, place)
    layer_out, second, branch, turn_sums = call(
        turn_kernel,
        [V] * 6,
        [(V, (rows, D), BF16), (V, (rows, D), F32), (V, (rows, D), BF16), (V, (3, D), F32)],
        [],
        rows * D * 30,
        5 << 20,
        part,
        core_got,
        got,
        hidden,
        jnp.concatenate([db, g2, b2]),
        out_cotangent,
    )

    branch_near = place.swap_narrow(branch)
    branch_other = place.swap_core(jnp.concatenate([branch, branch_near]))
    back, in_sums, part, near, theirs = call(
        back_kernel,
        [V] * 5 + [S, A, S] + [A] * 4,
        [
            (V, (4 * rows, 2 * quarter), BF16),
            (V, (1, 2 * quarter), F32),
            (V, (rows, D), F32),
            (V, (rows, D), F32),
            (V, (2 * rows, D), BF16),
        ],
        [down_hold, in_hold, eight, eight],
        rows * D * FF * 8,
        18 << 20,
        branch,
        branch_near,
        branch_other,
        gelu,
        slope,
        down_come,
        down_weights,
        in_come,
        *in_weights,
    )
    theirs, act = tie(theirs, act)
    down_blocks = call(
        down_grad_kernel,
        [V, V, V, V, S],
        [(A, (4, block_rows, D), BF16)] * 2,
        [down_hold, eight],
        rows * D * FF * 2,
        6 << 20,
        act,
        branch,
        branch_near,
        branch_other,
        leave,
    )
    core_got = place.swap_core(theirs)
    near, back = tie((near + core_got[rows:].astype(F32)).astype(BF16), back)
    got = place.swap_narrow(near)
    in_blocks = call(
        in_grad_kernel,
        [V, V, V, V, S],
        [(A, (4, block_rows, 2 * quarter), BF16)] * 2,
        [in_hold, eight],
        rows * D * FF * 8,
        18 << 20,
        hidden,
        hidden_near,
        hidden_other,
        back,
        leave,
    )
    down_far = plane_across(down_blocks, half_units, place)
    got, *held = tie(got, *down_far, *in_blocks)
    down_far, in_blocks = held[:-2], held[-2:]
    in_far = plane_across(in_blocks, 2 * owned, place)
    down_parts = plane_along(down_blocks[0], down_far, place)
    keep_rows = jnp.broadcast_to(jnp.where(chosen, 0.0, 1.0), (rows, 1)).astype(F32)
    input_grad, grad_attn, grad_qkv, attn_sums = call(
        attn_backward_kernel,
        [V] * 11 + [A, A, S],
        [
            (V, (rows, D), F32),
            (V, (rows, D), BF16),
            (V, (rows, 3 * D), BF16),
            (V, (5, D), F32),
        ],
        [attn_hold, pltpu.VMEM((rows, D), BF16), thirty_two],
        rows * D * D * 12,
        14 << 20,
        second,
        part,
        core_got,
        got,
        unit,
        scale,
        g1,
        keep_rows,
        context,
        probs,
        qkv,
        even,
        odd,
        core,
    )
    grad_qkv, down_parts, *in_far = tie(grad_qkv, down_parts, *in_far)

    blocks = call(
        attn_grad_kernel,
        [V] * 7 + [S] * 3,
        [(A, (4, D // 16, WIDE), BF16)] * 4 + [(A, (16, D // 16, WIDE), BF16)],
        [attn_hold, thirty_two],
        rows * D * D * 8,
        8 << 20,
        start,
        grad_qkv,
        context,
        grad_attn,
        attn_sums,
        turn_sums,
        in_sums,
        (place.core * 2 + place.x).reshape(1).astype(jnp.int32),
        place.row_spots(place.core),
        place.row_spots(1 - place.core),
    )
    if place.direct:
        got = place.swap_core(blocks[4])
        keep = [sum_of([blocks[m], got[4 * m : 4 * m + 4]]).astype(BF16) for m in range(4)]
        attn_parts = square_sum(keep, place)
    in_sum = sum_of(plane_along(in_blocks[0], in_far, place)).astype(BF16).reshape(2, owned, 2 * quarter)
    mine = jnp.where(place.core == 0, in_sum[0], in_sum[1])
    give = jnp.where(place.core == 0, in_sum[1], in_sum[0])
    got = place.swap_core(give)
    pair = jnp.where(place.core == 0, jnp.stack([mine, got]), jnp.stack([got, mine]))
    in_rows = halves(place, pair).reshape(2, 2, owned, 2, chips, half_units)
    in_rows = in_rows.transpose(2, 3, 4, 1, 0, 5).reshape(owned, 2 * FF).astype(F32)
    down_rows = halves(place, sum_of(down_parts)).reshape(units, D).astype(F32)

    if place.direct:
        attn_half, in_rows, down_rows = tie(sum_of(attn_parts).astype(BF16), in_rows, down_rows)
        attn_sum = halves(place, attn_half)
        vectors = attn_sum[0, :SMALL_ROWS, HALF:].astype(F32)
        s_qv = vectors[0, : 2 * owned]
        s_ob, s_g1, s_b1, s_db, s_g2, s_b2 = [vectors[i, :owned] for i in range(1, 7)]
        s_ib = vectors[BIAS_ROW : BIAS_ROW + 4, : 2 * owned].reshape(-1)
    else:
        attn_sum = reduce_attn(blocks[:4], blocks[4], owned, place)
        ib_blocks = in_sums.reshape(2, chips, 1, 1, half_units)
        at_core = (jnp.arange(2) == place.core).astype(F32).reshape(1, 1, 2, 1, 1)
        at_narrow = (jnp.arange(2) == place.x).astype(F32).reshape(1, 1, 1, 2, 1)
        vectors = [attn_sums[3:5], attn_sums[2], attn_sums[0], attn_sums[1]]
        vectors = vectors + [ib_blocks * at_core * at_narrow, turn_sums[0], turn_sums[1], turn_sums[2]]
        vectors = jnp.concatenate([v.reshape(wide, -1) for v in vectors], 1)
        vectors = lax.psum(vectors, AXES)[lax.axis_index("wide")]
        ends = [sum(widths[: i + 1]) for i in range(len(widths) - 1)]
        s_qv, s_ob, s_g1, s_b1, s_ib, s_db, s_g2, s_b2 = jnp.split(vectors, ends)
    attn_rows = attn_sum[..., :HALF].astype(F32)
    full_qkv = jnp.concatenate([attn_rows[0], attn_rows[1, :, :D]], 1)

    return (
        layer_out,
        input_grad,
        full_qkv,
        s_qv,
        attn_rows[1, :, D:],
        s_ob,
        s_g1,
        s_b1,
        in_rows,
        s_ib,
        down_rows,
        s_db,
        s_g2,
        s_b2,
    )


def solution(mesh):
    rows = P(("narrow", "wide"), None)
    marks = P(("narrow", "wide"))
    matrix = P("wide", None)
    vector = P("wide")
    in_specs = (rows, marks, marks, P(), matrix, vector, matrix, vector, vector, vector)
    in_specs = in_specs + (matrix, vector, matrix, vector, vector, vector, rows)
    out_specs = (rows, rows, matrix, vector, matrix, vector, vector, vector)
    out_specs = out_specs + (matrix, vector, matrix, vector, vector, vector)
    return jax.shard_map(body, mesh=mesh, in_specs=in_specs, out_specs=out_specs, check_vma=False)
```

```python
import functools
import math

import jax
import jax.numpy as jnp
from jax import lax
from jax.experimental import pallas as pl
from jax.experimental.pallas import tpu as pltpu
from jax.sharding import PartitionSpec as P

D = 768
HEADS = 12
HEAD_DIM = 64
FF = 3072
SEQ = 128
EPS = 1e-12
AXES = ("narrow", "wide")
F32 = jnp.float32
BF16 = jnp.bfloat16


def alibi_slopes(count):
    power = 2 ** int(math.floor(math.log2(count)))
    values = [2.0 ** (-8.0 * (number + 1) / power) for number in range(power)]
    extra = [2.0 ** (-8.0 * (number + 1) / (2 * power)) for number in range(2 * power)]
    values = values + extra[0::2][: count - power]
    return values


class Place:
    def __init__(self, narrow, wide):
        self.narrow = narrow
        self.wide = wide
        self.chips = wide // 2
        self.direct = narrow == 2 and wide == 16
        self.ny = 2 if self.direct else 1
        self.nz = self.chips // self.ny
        across = lax.axis_index("narrow")
        along = lax.axis_index("wide")
        self.x = across
        self.core = along % 2
        self.chip = along // 2
        self.y = self.chip % self.ny
        self.z = self.chip // self.ny

    def move(self, values, target):
        pairs = []
        for x in range(self.narrow):
            for z in range(self.nz):
                for y in range(self.ny):
                    for c in range(2):
                        tx, tz, ty, tc = target(x, z, y, c)
                        source = ((x * self.nz + z) * self.ny + y) * 2 + c
                        goal = ((tx * self.nz + tz) * self.ny + ty) * 2 + tc
                        pairs.append((source, goal))
        return lax.ppermute(values, AXES, pairs)

    def swap_core(self, values):
        return self.move(values, lambda x, z, y, c: (x, z, y, 1 - c))

    def swap_narrow(self, values):
        return self.move(values, lambda x, z, y, c: (1 - x, z, y, c))

    def swap_y(self, values):
        return self.move(values, lambda x, z, y, c: (x, z, 1 - y, c))

    def first(self, values):
        return self.move(
            values, lambda x, z, y, c: (1 - x, z, y, c) if c == 0 else (x, z, 1 - y, c)
        )

    def second(self, values):
        return self.move(
            values, lambda x, z, y, c: (x, z, 1 - y, c) if c == 0 else (1 - x, z, y, c)
        )

    def diagonal(self, values):
        return self.move(values, lambda x, z, y, c: (1 - x, z, 1 - y, c))

    def along_z(self, values):
        lines = [
            [(z * self.ny + y) * 2 + c for z in range(self.nz)] for y in range(self.ny) for c in range(2)
        ]
        return lax.all_to_all(
            values, "wide", split_axis=0, concat_axis=0, axis_index_groups=lines, tiled=True
        )

    def column_z(self, values):
        column = [values]
        for step in range(1, self.nz):
            column.append(
                self.move(values, lambda x, z, y, c: (x, (z + step) % self.nz, y, c))
            )
        return column

    def spread_z(self, values):
        return self.along_z(jnp.broadcast_to(values[None], (self.nz,) + values.shape))

    def spots(self, core, steps):
        if not self.direct:
            at = jnp.arange(16, dtype=jnp.int32)
            return at // 2, at % 2
        m = jnp.arange(16) // 4
        z = (self.z - jnp.arange(16)) % 4 if steps else jnp.arange(16) % 4
        on_first = (m == 1) | (m == 3)
        on_second = (m == 2) | (m == 3)
        flip_x = jnp.where(core == 0, on_first, on_second).astype(jnp.int32)
        flip_y = jnp.where(core == 0, on_second, on_first).astype(jnp.int32)
        y = jnp.bitwise_xor(self.y, flip_y)
        x = jnp.bitwise_xor(self.x, flip_x)
        return (z * self.ny + y).astype(jnp.int32), x.astype(jnp.int32)

    def plane_spots(self, y_first):
        if not self.direct:
            return jnp.arange(8, dtype=jnp.int32)
        at = jnp.arange(8)
        flip, z = (at % 2, at // 2) if y_first else (at // 4, at % 4)
        return (z * self.ny + jnp.bitwise_xor(self.y, flip)).astype(jnp.int32)

    def row_spots(self, core, steps):
        chip, half = self.spots(core, steps)
        return jnp.stack([chip * 2 + core, half])


ANYWHERE = pl.BlockSpec(memory_space=pl.ANY)
IN_HBM = pl.BlockSpec(memory_space=pltpu.HBM)
KEPT = pl.BlockSpec(memory_space=pltpu.VMEM)
SCALARS = pl.BlockSpec(memory_space=pltpu.SMEM)
VECTORS = pl.BlockSpec(memory_space=pltpu.VMEM)
PAIRS = HEADS // 2
HALF = 2 * D
LANES = 128
WIDE = HALF + LANES


def dot(a, b, da, db):
    return lax.dot_general(a, b, (((da,), (db,)), ((), ())), preferred_element_type=F32)


BIG, SMALL = 36, 16


def call(kernel, ins, outs, scratch, flops, moved, *operands):
    operands = [
        pltpu.with_memory_space_constraint(operand, pltpu.HBM) if spec is IN_HBM or spec is KEPT else operand
        for spec, operand in zip(ins, operands, strict=True)
    ]
    windows = any(spec.block_shape is not None for spec in ins)
    return pl.pallas_call(
        kernel,
        grid=(1,) if windows else (),
        in_specs=ins,
        out_specs=[spec for spec, _, _ in outs],
        out_shape=[jax.ShapeDtypeStruct(shape, dtype) for _, shape, dtype in outs],
        scratch_shapes=scratch,
        cost_estimate=pl.CostEstimate(flops=flops, transcendentals=0, bytes_accessed=moved),
        compiler_params=pltpu.CompilerParams(vmem_limit_bytes=(BIG if kernel is attn_backward_kernel else SMALL) * 1024 * 1024),
    )(*operands)


def normed(values):
    average = jnp.mean(values, -1, keepdims=True)
    center = values - average
    variance = jnp.mean(center * center, -1, keepdims=True)
    scale = lax.rsqrt(variance + EPS)
    return center * scale, scale


def norm_back(grad, unit, scale, gain):
    e = grad * gain
    return scale * (
        e - jnp.mean(e, -1, keepdims=True) - unit * jnp.mean(e * unit, -1, keepdims=True)
    )


def split_heads(pair):
    low = lax.broadcasted_iota(jnp.int32, pair.shape, 1) < HEAD_DIM
    zero = jnp.zeros_like(pair)
    return jnp.concatenate([jnp.where(low, pair, zero), jnp.where(low, zero, pair)], 0)


def join_heads(stacked):
    rows = stacked.shape[0] // 2
    low = lax.broadcasted_iota(jnp.int32, (rows, LANES), 1) < HEAD_DIM
    return jnp.where(low, stacked[:rows], stacked[rows:])


def block_list(arrays):
    blocks = []
    for array in arrays:
        for i in range(array.shape[0]):
            if len(array.shape) == 4:
                blocks += [array.at[i, j] for j in range(array.shape[1])]
            else:
                blocks.append(array.at[i])
    return blocks


def fetch_rows(sources, spots, hold, sems):
    copies = []
    for at, block in enumerate(block_list(sources)):
        size = block.shape[0]
        to = pl.multiple_of(spots[at] * size, size)
        copies.append(pltpu.make_async_copy(block, hold.at[pl.ds(to, size)], sems.at[at]))
    for copy in copies:
        copy.start()
    return copies


def emit_rows(source, outs, spots, sems):
    copies = []
    for at, block in enumerate(block_list(outs)):
        size = block.shape[0]
        start = pl.multiple_of(spots[at] * size, size)
        copies.append(pltpu.make_async_copy(source.at[pl.ds(start, size)], block, sems.at[at]))
    for copy in copies:
        copy.start()
    for copy in copies:
        copy.wait()


def fetch_attn(blocks, spots, hold, sems):
    copies = []
    for at, block in enumerate(block_list(blocks)):
        size = block.shape[0]
        row = pl.multiple_of(spots[0, at] * size, size)
        lane = pl.multiple_of(spots[1, at] * WIDE, LANES)
        copies.append(
            pltpu.make_async_copy(
                block, hold.at[pl.ds(row, size), pl.ds(lane, WIDE)], sems.at[at]
            )
        )
    for copy in copies:
        copy.start()
    return copies


SMALL_ROWS = 16
BIAS_ROW = 8


def read_vectors(hold, quarter, vectors, in_shift):
    owners = 16
    size = D // owners
    tall = lax.broadcasted_iota(jnp.int32, (4, 2 * size), 0) == quarter[0]
    for owner in range(owners):
        at = owner * size
        lane = (owner % (owners // 2)) * 2 * size
        row = owner // (owners // 2)
        region = hold[at : at + SMALL_ROWS, HALF:WIDE].astype(F32)
        vectors[row : row + 1, lane : lane + 2 * size] = region[0:1, : 2 * size]
        vectors[2:8, at : at + size] = region[1:7, :size]
        bias = jnp.where(tall, region[BIAS_ROW : BIAS_ROW + 4, : 2 * size], 0.0)
        in_shift[:, owner * 2 * size : (owner + 1) * 2 * size] = jnp.sum(bias, 0, keepdims=True)


VALUE_AT = WIDE
OUT_AT = WIDE + D


def attn_forward_kernel(
    start, b0, b1, b2, b3, b4, b5, b6, b7, spots, quarter,
    context, probs, qkv, unit, scale, hidden, vectors, in_shift, hold, sems,
):
    for copy in fetch_attn((b0, b1, b2, b3, b4, b5, b6, b7), spots, hold, sems):
        copy.wait()
    read_vectors(hold, quarter, vectors, in_shift)
    rows = start.shape[0]
    begin = start[...]
    for part, at in enumerate((0, D, VALUE_AT)):
        made = dot(begin, hold[:, at : at + D], 1, 0)
        if part != 1:
            made = made + vectors[part // 2 : part // 2 + 1, :]
        qkv[:, part * D : (part + 1) * D] = made.astype(BF16)
    distance = jnp.abs(
        lax.broadcasted_iota(jnp.int32, (SEQ, SEQ), 0) - lax.broadcasted_iota(jnp.int32, (SEQ, SEQ), 1)
    ).astype(F32)
    slopes = alibi_slopes(HEADS)
    for s in range(rows // SEQ):
        span = slice(s * SEQ, (s + 1) * SEQ)
        for pair in range(PAIRS):
            lane = pair * LANES
            queries = qkv[span, lane : lane + LANES]
            keys = qkv[span, D + lane : D + lane + LANES]
            values = qkv[span, 2 * D + lane : 2 * D + lane + LANES]
            raw = dot(split_heads(queries), keys, 1, 1)
            fall = jnp.concatenate([distance * slopes[2 * pair], distance * slopes[2 * pair + 1]], 0)
            scores = raw * HEAD_DIM ** (-0.5) - fall
            expo = jnp.exp(scores - jnp.max(scores, -1, keepdims=True))
            made = expo / jnp.sum(expo, -1, keepdims=True)
            probs[s, pair] = made
            joined = join_heads(dot(made.astype(BF16), values, 1, 0))
            context[span, lane : lane + LANES] = joined.astype(BF16)
    first_sum = begin.astype(F32) + dot(context[...], hold[:, OUT_AT : OUT_AT + D], 1, 0)
    made, factor = normed(first_sum + vectors[2:3, :])
    unit[...] = made
    scale[...] = factor
    hidden[...] = (made * vectors[3:4, :] + vectors[4:5, :]).astype(BF16)


def by_sequence(values):
    return jnp.concatenate(
        [v[i : i + SEQ, :] for i in range(0, values[0].shape[0], SEQ) for v in values], 0
    )


def ffn_in_kernel(
    h0, h1, h2, h3, spots, w0, w1, w2, w3, shift, act, gelu_out, slope_out, hold, sems
):
    copies = fetch_rows((w0, w1, w2, w3), spots, hold, sems)
    both = by_sequence((h0, h1, h2, h3))
    for copy in copies:
        copy.wait()
    width = act.shape[1]
    block = 256
    for at in range(0, width, block):
        cols = slice(at, at + block)
        more = slice(width + at, width + at + block)
        gate = dot(both, hold[:, cols], 1, 0) + shift[:, cols]
        up = dot(both, hold[:, more], 1, 0) + shift[:, more]
        cdf = 0.5 + 0.5 * lax.erf(gate * (0.5**0.5))
        gelu = gate * cdf
        slope = cdf + gate * jnp.exp(-0.5 * gate * gate) * ((2 * math.pi) ** -0.5)
        act[:, cols] = (gelu * up).astype(BF16)
        gelu_out[:, cols] = gelu.astype(BF16)
        slope_out[:, cols] = (slope * up).astype(BF16)


def ffn_down_kernel(act, spots, w0, mine, near, theirs, hold, sems):
    copies = fetch_rows((w0,), spots, hold, sems)
    for copy in copies:
        copy.wait()
    rows = mine.shape[0]
    made = dot(act[...], hold[...], 1, 0)
    mine[...] = made[:rows]
    near[...] = made[rows : 2 * rows]
    theirs[...] = made[2 * rows :].astype(BF16)


def turn_kernel(mine, core, got, hidden, vectors, cotangent, layer_out, second, branch, sums):
    part = mine[...] + core[: mine.shape[0], :].astype(F32) + got[...].astype(F32)
    total = hidden[...].astype(F32) + (part + vectors[5:6, :])
    unit, scale = normed(total)
    layer_out[...] = (unit * vectors[6:7, :] + vectors[7:8, :]).astype(BF16)
    grad = cotangent[...].astype(F32)
    back = norm_back(grad, unit, scale, vectors[6:7, :])
    second[...] = back
    low = back.astype(BF16)
    branch[...] = low
    sums[0:1, :] = jnp.sum(low.astype(F32), 0, keepdims=True)
    sums[1:2, :] = jnp.sum(grad * unit, 0, keepdims=True)
    sums[2:3, :] = jnp.sum(grad, 0, keepdims=True)


def down_grad_kernel(act, g0, g1, g2, g3, g4, g5, g6, g7, spots, p0, p1, hold, sems):
    both = jnp.concatenate([g[...] for g in (g0, g1, g2, g3, g4, g5, g6, g7)], 0)
    hold[...] = dot(act[...], both, 0, 0).astype(BF16)
    emit_rows(hold, (p0, p1), spots, sems)


def back_kernel(
    g0, g1, g2, g3, g4, g5, g6, g7, gelu, slope, spots, w0, in_spots, u0, u1, u2, u3,
    back, sums, part, near, other, hold, in_hold, sems, in_sems,
):
    copies = fetch_rows((w0,), spots, hold, sems)
    in_copies = fetch_rows((u0, u1, u2, u3), in_spots, in_hold, in_sems)
    both = jnp.concatenate([g[...] for g in (g0, g1, g2, g3, g4, g5, g6, g7)], 0)
    for copy in copies:
        copy.wait()
    width = gelu.shape[1]
    block = 256
    for at in range(0, width, block):
        cols = slice(at, at + block)
        more = slice(width + at, width + at + block)
        grad = dot(both, hold[cols, :], 1, 1)
        for cut, factor in ((cols, slope), (more, gelu)):
            low = (grad * factor[:, cols].astype(F32)).astype(BF16)
            back[:, cut] = low
            sums[:, cut] = jnp.sum(low.astype(F32), 0, keepdims=True)
    for copy in in_copies:
        copy.wait()
    made = dot(back[...], in_hold[...], 1, 1)
    count = part.shape[0] // SEQ
    for i in range(count):
        at = 4 * SEQ * i
        here, there = slice(i * SEQ, (i + 1) * SEQ), slice((count + i) * SEQ, (count + i + 1) * SEQ)
        part[here, :] = made[at : at + SEQ]
        near[here, :] = made[at + SEQ : at + 2 * SEQ]
        other[here, :] = made[at + 2 * SEQ : at + 3 * SEQ].astype(BF16)
        other[there, :] = made[at + 3 * SEQ : at + 4 * SEQ].astype(BF16)


def in_grad_kernel(h0, h1, h2, h3, back, goal, p0, p1, made, out_sems):
    made[...] = dot(by_sequence((h0, h1, h2, h3)), back[...], 0, 0).astype(BF16)
    emit_rows(made, (p0, p1), goal, out_sems)


def attn_backward_kernel(
    s0, s1, mine, core, near, unit, scale, vectors, keep, context, probs, qkv,
    b0, b1, b2, b3, b4, b5, b6, b7, spots, start, turn0, turn1, in_sums, quarter, goal, other_goal,
    input_grad, sums, k0, k1, k2, k3, give,
    hold, grad_context, grad_attn, grad_qkv, made_hold, sems, out_sems,
):
    copies = fetch_attn((b0, b1, b2, b3, b4, b5, b6, b7), spots, hold, sems)
    rows = unit.shape[0]
    grad = jnp.concatenate([s0[...], s1[...]], 0) + mine[...]
    grad = grad + core[:rows, :].astype(F32) + near[...].astype(F32)
    made = unit[...]
    sums[0:1, :] = jnp.sum(grad * made, 0, keepdims=True)
    sums[1:2, :] = jnp.sum(grad, 0, keepdims=True)
    first = norm_back(grad, made, scale[...], vectors[3:4, :])
    low = first.astype(BF16)
    grad_attn[...] = low
    sums[2:3, :] = jnp.sum(low.astype(F32), 0, keepdims=True)
    for copy in copies:
        copy.wait()
    grad_context[...] = dot(low, hold[:, OUT_AT : OUT_AT + D], 1, 1).astype(BF16)
    for s in range(rows // SEQ):
        span = slice(s * SEQ, (s + 1) * SEQ)
        for pair in range(PAIRS):
            lane = pair * LANES
            queries = split_heads(qkv[span, lane : lane + LANES])
            keys = qkv[span, D + lane : D + lane + LANES]
            values = qkv[span, 2 * D + lane : 2 * D + lane + LANES]
            outer = split_heads(grad_context[span, lane : lane + LANES])
            weight = probs[s, pair]
            grad_probs = dot(outer, values, 1, 1)
            inner = jnp.sum(weight * grad_probs, -1, keepdims=True)
            grad_raw = (weight * (grad_probs - inner) * HEAD_DIM ** (-0.5)).astype(BF16)
            grad_queries = join_heads(dot(grad_raw, keys, 1, 0))
            grad_keys = dot(grad_raw, queries, 0, 0)
            grad_values = dot(weight.astype(BF16), outer, 0, 0)
            grad_qkv[span, lane : lane + LANES] = grad_queries.astype(BF16)
            grad_qkv[span, D + lane : D + lane + LANES] = grad_keys.astype(BF16)
            grad_qkv[span, 2 * D + lane : 2 * D + lane + LANES] = grad_values.astype(BF16)
    sums[3:4, :] = jnp.sum(grad_qkv[:, :D].astype(F32), 0, keepdims=True)
    sums[4:5, :] = jnp.sum(grad_qkv[:, 2 * D :].astype(F32), 0, keepdims=True)
    total = first
    for part, at in enumerate((0, D, VALUE_AT)):
        total = total + dot(grad_qkv[:, part * D : (part + 1) * D], hold[:, at : at + D], 1, 1)
    input_grad[...] = total * keep[...]
    attn_grad(
        start, grad_qkv, context, grad_attn, sums, turn0, turn1, in_sums, quarter, goal, other_goal,
        (k0, k1, k2, k3), give, made_hold, out_sems,
    )


def attn_grad(
    start, grad_qkv, context, grad_attn, sums, turn0, turn1, in_sums, quarter, mine, theirs, keep, give, hold, sems
):
    begin = start[...]
    size = give.shape[1]
    owners = D // size
    hold[:, HALF:WIDE] = jnp.zeros((D, LANES), BF16)
    hold[:, WIDE + HALF : 2 * WIDE] = jnp.zeros((D, LANES), BF16)
    tall = lax.broadcasted_iota(jnp.int32, (4, 2 * size), 0) == quarter[0]
    for owner in range(owners):
        at = owner * size
        lane = (owner % (owners // 2)) * 2 * size
        row = 3 + owner // (owners // 2)
        bias = in_sums[:, owner * 2 * size : (owner + 1) * 2 * size]
        wide = [sums[row : row + 1, lane : lane + 2 * size]]
        narrow = [sums[i : i + 1, at : at + size] for i in (2, 0, 1)]
        narrow.append(turn0[:, at : at + size] + turn1[:, at : at + size])
        narrow = jnp.concatenate(narrow + [jnp.zeros((1, size), F32)], 0)
        narrow = jnp.concatenate([narrow, jnp.zeros_like(narrow)], 1)
        made = jnp.concatenate(
            wide + [narrow, jnp.where(tall, bias, 0.0), jnp.zeros((4, 2 * size), F32)], 0
        )
        hold[at : at + SMALL_ROWS, HALF : HALF + 2 * size] = made.astype(BF16)
    for part, at in enumerate((0, D, VALUE_AT)):
        hold[:, at : at + D] = dot(begin, grad_qkv[:, part * D : (part + 1) * D], 0, 0).astype(BF16)
    hold[:, OUT_AT : OUT_AT + D] = dot(context[...], grad_attn[...], 0, 0).astype(BF16)
    copies = []
    for side, spots in enumerate((theirs, mine)):
        for at in range(16):
            row = pl.multiple_of(spots[0, at] * size, size)
            lane = pl.multiple_of(spots[1, at] * WIDE, LANES)
            copies.append(
                pltpu.make_async_copy(
                    hold.at[pl.ds(row, size), pl.ds(lane, WIDE)],
                    give.at[at] if side == 0 else keep[at // 4].at[at % 4],
                    sems.at[side * 16 + at],
                )
            )
    for copy in copies:
        copy.start()
    for copy in copies:
        copy.wait()


def block_at(i, step):
    return i, 0


def tie(*values):
    return lax.optimization_barrier(values)


def square_gather(column, place):
    one = place.first(column)
    return column, one, place.second(column), place.second(one)


def halves(place, mine):
    mine = mine.astype(BF16)
    other = place.swap_narrow(mine)
    return jnp.where(place.x == 0, jnp.stack([mine, other]), jnp.stack([other, mine]))


def square_sum(blocks, place):
    zero, one, two, three = blocks
    one = sum_of([one, place.second(three)]).astype(BF16)
    zero = sum_of([zero, place.second(two), place.first(one)]).astype(BF16)
    return place.along_z(zero)


def plane_all(piece, place):
    whole = lax.all_gather(piece, "wide", axis=0, tiled=False)
    whole = whole.reshape((place.chips, 2) + piece.shape)
    return by_core(place, whole, 1).reshape(8, -1, piece.shape[-1])


def plane_across(blocks, size, place):
    if place.direct:
        return [place.swap_y(values) for values in blocks[1:]]
    order = jnp.concatenate(blocks).reshape(place.chips, 1, size, blocks[0].shape[-1])
    zeros = jnp.zeros_like(order)
    order = jnp.where(
        place.core == 0, jnp.concatenate([order, zeros], 1), jnp.concatenate([zeros, order], 1)
    )
    order = order.reshape((-1,) + order.shape[2:]).astype(F32)
    return [lax.psum_scatter(order, "wide", scatter_dimension=0, tiled=True)]


def plane_along(near, far, place):
    if not place.direct:
        return far[0]
    return place.along_z(sum_of([near, far[0]]).astype(BF16))


def sum_of(parts):
    total = parts[0].astype(F32)
    for i in range(1, len(parts)):
        total = total + parts[i].astype(F32)
    return total


def by_core(place, values, axis):
    return jnp.where(
        place.core == 0,
        lax.index_in_dim(values, 0, axis, keepdims=False),
        lax.index_in_dim(values, 1, axis, keepdims=False),
    )


def by_narrow(place, values, axis):
    return jnp.where(
        place.x == 0,
        lax.index_in_dim(values, 0, axis, keepdims=False),
        lax.index_in_dim(values, 1, axis, keepdims=False),
    )


def quarter_sum(near, theirs, rows, place):
    got = place.swap_core(theirs)
    near = (near + got[rows:].astype(F32)).astype(BF16)
    return got, place.swap_narrow(near)


def with_small(rows, vectors, owned):
    both = jnp.swapaxes(rows.reshape(owned, 2, HALF), 0, 1)
    qv, ob, g1, b1, ib, db, g2, b2 = vectors
    width = 2 * owned
    narrow = jnp.stack([ob, g1, b1, db, g2, b2])
    narrow = jnp.pad(narrow, ((0, 1), (0, owned)))
    small = jnp.concatenate([qv[None], narrow, ib.reshape(4, width)])
    small = jnp.pad(small, ((0, owned - small.shape[0]), (0, LANES - width)))
    small = jnp.stack([small, jnp.zeros_like(small)])
    return jnp.concatenate([both, small], 2)


def gather_attn(rows, vectors, owned, place):
    full = lax.all_gather(rows, "wide", axis=0, tiled=True)
    parts = [lax.all_gather(v, "wide", axis=0, tiled=True) for v in vectors]
    size = D // 16
    parts = [v.reshape(16, -1) for v in parts]
    ib = parts[4].reshape(2, place.chips, 2, 2, -1).reshape(2, 8, -1, 2, 2, parts[4].size // (place.wide * 4))
    parts[4] = ib.transpose(0, 1, 3, 4, 2, 5).reshape(16, 4 * 2 * size)
    blocks = [
        with_small(full[i * size : (i + 1) * size], [v[i] for v in parts], size) for i in range(16)
    ]
    blocks = jnp.stack(blocks).reshape(8, 2, 2, size, WIDE)
    even, odd = [blocks[:, core].reshape(4, 4, size, WIDE) for core in range(2)]
    mine = jnp.where(place.core == 0, even, odd)
    other = jnp.where(place.core == 0, odd, even)
    return [mine[m] for m in range(4)] + [other[m] for m in range(4)]


def reduce_attn(keep, give, owned, place):
    mine = jnp.stack(keep).reshape(8, 2, D // 16, WIDE)
    other = give.reshape(8, 2, D // 16, WIDE)
    full = jnp.where(place.core == 0, jnp.stack([mine, other], 1), jnp.stack([other, mine], 1))
    full = full.transpose(0, 1, 3, 2, 4).reshape(place.wide, owned, 2, WIDE)
    full = jnp.swapaxes(full, 1, 2).astype(F32)
    full = lax.psum_scatter(full, "wide", scatter_dimension=0, tiled=True)[0]
    return lax.psum(full, "narrow").astype(BF16)


def body(
    hidden_in,
    masked,
    token_ids,
    token_table,
    qkv_weight,
    qv_bias,
    out_weight,
    out_bias,
    norm1_gain,
    norm1_bias,
    ffn_in_weight,
    ffn_in_bias,
    ffn_out_weight,
    ffn_out_bias,
    norm2_gain,
    norm2_bias,
    out_cotangent,
):
    place = Place(lax.axis_size("narrow"), lax.axis_size("wide"))
    wide = place.wide
    chips = place.chips
    owned = qkv_weight.shape[0]
    units = ffn_out_weight.shape[0]
    rows = hidden_in.shape[0]
    seqs = rows // SEQ

    chosen = (masked > 0)[:, None]
    replaced, ffn_in_weight = tie(jnp.take(token_table, token_ids, axis=0), ffn_in_weight)
    start = jnp.where(chosen, replaced, hidden_in)

    small = (qv_bias, out_bias, norm1_gain, norm1_bias, ffn_in_bias, ffn_out_bias, norm2_gain, norm2_bias)
    attn_own = jnp.concatenate([qkv_weight, out_weight], 1)
    half_units = units // 2
    in_blocks = ffn_in_weight.reshape(owned, 2, chips, 2, 2, half_units)
    in_blocks = by_narrow(place, in_blocks, 4)
    in_mine = by_core(place, in_blocks, 3).reshape(owned, FF // 2)
    in_give = by_core(place, jnp.flip(in_blocks, 3), 3).reshape(owned, FF // 2)
    in_got = place.swap_core(in_give)
    in_piece = jnp.where(
        place.core == 0, jnp.concatenate([in_mine, in_got]), jnp.concatenate([in_got, in_mine])
    )
    down_piece = by_narrow(place, ffn_out_weight.reshape(2, half_units, D), 0)
    if place.direct:
        attn_piece = by_narrow(place, with_small(attn_own, small, owned), 0)
        attn_column = place.column_z(attn_piece)
        down_got = place.swap_y(down_piece)
        *attn_column, down_got, in_piece, start = tie(*attn_column, down_got, in_piece, start)
        in_column = place.spread_z(in_piece)
        blocks = [jnp.stack(attn_column)]
        blocks = blocks + [place.first(blocks[0]), place.second(blocks[0])]
        others = [place.swap_core(values) for values in blocks]
        blocks.append(place.second(blocks[1]))
        *held, in_column, down_got = tie(*blocks, *others, in_column, down_got)
        attn_blocks = held + [place.swap_core(held[3])]
        in_first, in_last = in_column[:2], in_column[2:]
        in_weights = [in_first, in_last, place.swap_y(in_first), place.swap_y(in_last)]
        down_weights = place.spread_z(jnp.stack([down_piece, down_got]))
    else:
        attn_blocks = gather_attn(attn_own, small, owned, place)
        whole = plane_all(in_piece, place)
        in_weights = [whole[:2], whole[2:4], whole[4:6], whole[6:]]
        whole = plane_all(down_piece, place)
        down_weights = whole.reshape(4, 2, -1, D)
    attn_come = jnp.concatenate(
        [place.row_spots(place.core, True), place.row_spots(1 - place.core, True)], 1
    )
    in_come = place.plane_spots(False)
    down_come = place.plane_spots(True)
    leave = place.plane_spots(False)
    block_rows, quarter = D // 8, FF // 4
    eight = pltpu.SemaphoreType.DMA((8,))
    sixteen = pltpu.SemaphoreType.DMA((16,))
    thirty_two = pltpu.SemaphoreType.DMA((32,))
    in_hold = pltpu.VMEM((D, 2 * quarter), BF16)
    down_hold = pltpu.VMEM((quarter, D), BF16)
    attn_hold = pltpu.VMEM((D, 2 * WIDE), BF16)
    V, A, S, H, K = VECTORS, ANYWHERE, SCALARS, IN_HBM, KEPT

    quarter_at = (place.core * 2 + place.x).reshape(1).astype(jnp.int32)

    context, probs, qkv, unit, scale, hidden, vectors, in_shift = call(
        attn_forward_kernel,
        [V] + [H] * 8 + [S, S],
        [
            (V, (rows, D), BF16),
            (V, (seqs, PAIRS, 2 * SEQ, SEQ), F32),
            (V, (rows, 3 * D), BF16),
            (V, (rows, D), F32),
            (V, (rows, 1), F32),
            (V, (rows, D), BF16),
            (V, (8, D), F32),
            (V, (1, 2 * quarter), F32),
        ],
        [attn_hold, thirty_two],
        rows * D * D * 10,
        10 << 20,
        start,
        *attn_blocks,
        attn_come,
        quarter_at,
    )
    hidden, in_weights[2] = tie(hidden, in_weights[2])
    hidden_near = place.swap_narrow(hidden)
    hidden_core = place.swap_core(hidden)
    hidden_near, in_weights[3] = tie(hidden_near, in_weights[3])
    hidden_far = place.swap_core(hidden_near)
    hidden_far, down_weights = tie(hidden_far, down_weights)
    inputs = (hidden, hidden_near, hidden_core, hidden_far)
    act, gelu, slope = call(
        ffn_in_kernel,
        [V, V, V, V, S, H, H, H, H, V],
        [(V, (4 * rows, quarter), BF16)] * 3,
        [in_hold, eight],
        rows * D * FF * 8,
        12 << 20,
        *inputs,
        in_come,
        *in_weights,
        in_shift,
    )
    count = rows // SEQ
    parts = []
    for i in range(count):
        parts.append(
            call(
                ffn_down_kernel,
                [pl.BlockSpec((4 * SEQ, quarter), functools.partial(block_at, i)), S, H],
                [(V, (SEQ, D), F32), (V, (SEQ, D), F32), (V, (2 * SEQ, D), BF16)],
                [down_hold, eight],
                SEQ * D * FF * 2,
                6 << 20,
                act,
                down_come,
                down_weights,
            )
        )
    turned = []
    for i, (part, near, theirs) in enumerate(parts):
        core_got, got = quarter_sum(near, theirs, SEQ, place)
        row = pl.BlockSpec((SEQ, D), functools.partial(block_at, i))
        turned.append(
            call(
                turn_kernel,
                [V, V, V, row, V, row],
                [(V, (SEQ, D), BF16), (V, (SEQ, D), F32), (V, (SEQ, D), BF16), (V, (3, D), F32)],
                [],
                SEQ * D * 30,
                5 << 20,
                part,
                core_got,
                got,
                hidden,
                vectors,
                out_cotangent,
            )
        )
    layer_out = jnp.concatenate([made[0] for made in turned])

    gradients = []
    for made in turned:
        near = place.swap_narrow(made[2])
        gradients += [made[2], near, place.swap_core(made[2]), place.swap_core(near)]
    back, in_sums, part, near, theirs = call(
        back_kernel,
        [V] * 10 + [S, H, S] + [H] * 4,
        [
            (V, (4 * rows, 2 * quarter), BF16),
            (V, (1, 2 * quarter), F32),
            (V, (rows, D), F32),
            (V, (rows, D), F32),
            (V, (2 * rows, D), BF16),
        ],
        [down_hold, in_hold, eight, eight],
        rows * D * FF * 8,
        18 << 20,
        *gradients,
        gelu,
        slope,
        down_come,
        down_weights,
        in_come,
        *in_weights,
    )
    theirs, act = tie(theirs, act)
    down_blocks = call(
        down_grad_kernel,
        [V] * 9 + [S],
        [(A, (4, block_rows, D), BF16)] * 2,
        [down_hold, eight],
        rows * D * FF * 2,
        6 << 20,
        act,
        *gradients,
        leave,
    )
    core_got = place.swap_core(theirs)
    near, back = tie((near + core_got[rows:].astype(F32)).astype(BF16), back)
    got = place.swap_narrow(near)
    in_blocks = call(
        in_grad_kernel,
        [V] * 5 + [S],
        [(A, (4, block_rows, 2 * quarter), BF16)] * 2,
        [in_hold, eight],
        rows * D * FF * 8,
        18 << 20,
        *inputs,
        back,
        leave,
    )
    in_far = plane_across(in_blocks, 2 * owned, place)
    down_far = plane_across(down_blocks, half_units, place)
    got, *held = tie(got, *down_far, in_blocks[0])
    down_parts = plane_along(down_blocks[0], held[:-1], place)
    adds = [made[1] for made in turned] + [part, core_got, got]
    turn_sums = [made[3] for made in turned]
    keep_rows = jnp.broadcast_to(jnp.where(chosen, 0.0, 1.0), (rows, 1)).astype(F32)
    input_grad, attn_sums, *blocks = call(
        attn_backward_kernel,
        [K, K, V, V, V, K, V, V, V, K, K, K] + [H] * 8 + [S, K, V, V, V, S, S, S],
        [(V, (rows, D), F32), (V, (5, D), F32)]
        + [(A, (4, D // 16, WIDE), BF16)] * 4
        + [(A, (16, D // 16, WIDE), BF16)],
        [
            attn_hold,
            pltpu.VMEM((rows, D), BF16),
            pltpu.VMEM((rows, D), BF16),
            pltpu.VMEM((rows, 3 * D), BF16),
            attn_hold,
            thirty_two,
            thirty_two,
        ],
        rows * D * D * 20,
        22 << 20,
        *adds,
        unit,
        scale,
        vectors,
        keep_rows,
        context,
        probs,
        qkv,
        *attn_blocks,
        attn_come,
        start,
        *turn_sums,
        in_sums,
        quarter_at,
        place.row_spots(place.core, False),
        place.row_spots(1 - place.core, False),
    )
    give, down_parts, *in_far = tie(blocks[4], down_parts, *in_far)
    if place.direct:
        got = place.swap_core(give)
        keep = [sum_of([blocks[m], got[4 * m : 4 * m + 4]]).astype(BF16) for m in range(4)]
        attn_parts = square_sum(keep, place)
    in_sum = sum_of(plane_along(in_blocks[0], in_far, place)).astype(BF16).reshape(2, owned, 2 * quarter)
    mine = jnp.where(place.core == 0, in_sum[0], in_sum[1])
    give = jnp.where(place.core == 0, in_sum[1], in_sum[0])
    got = place.swap_core(give)
    pair = jnp.where(place.core == 0, jnp.stack([mine, got]), jnp.stack([got, mine]))
    in_rows = halves(place, pair).reshape(2, 2, owned, 2, chips, half_units)
    in_rows = in_rows.transpose(2, 3, 4, 1, 0, 5).reshape(owned, 2 * FF).astype(F32)
    down_rows = halves(place, sum_of(down_parts)).reshape(units, D).astype(F32)

    if place.direct:
        attn_half, in_rows, down_rows = tie(sum_of(attn_parts).astype(BF16), in_rows, down_rows)
        attn_sum = halves(place, attn_half)
        lanes = attn_sum[0, :SMALL_ROWS, HALF:].astype(F32)
        s_qv = lanes[0, : 2 * owned]
        s_ob, s_g1, s_b1, s_db, s_g2, s_b2 = [lanes[i, :owned] for i in range(1, 7)]
        s_ib = lanes[BIAS_ROW : BIAS_ROW + 4, : 2 * owned].reshape(-1)
    else:
        attn_sum = reduce_attn(blocks[:4], blocks[4], owned, place)
        turn_sums = sum_of(turn_sums)
        ib_blocks = in_sums.reshape(2, chips, 1, 1, half_units)
        at_core = (jnp.arange(2) == place.core).astype(F32).reshape(1, 1, 2, 1, 1)
        at_narrow = (jnp.arange(2) == place.x).astype(F32).reshape(1, 1, 1, 2, 1)
        sums = [attn_sums[3:5], attn_sums[2], attn_sums[0], attn_sums[1]]
        sums = sums + [ib_blocks * at_core * at_narrow, turn_sums[0], turn_sums[1], turn_sums[2]]
        widths = [v.size // wide for v in sums]
        sums = jnp.concatenate([v.reshape(wide, -1) for v in sums], 1)
        sums = lax.psum(sums, AXES)[lax.axis_index("wide")]
        ends = [sum(widths[: i + 1]) for i in range(len(widths) - 1)]
        s_qv, s_ob, s_g1, s_b1, s_ib, s_db, s_g2, s_b2 = jnp.split(sums, ends)
    attn_rows = attn_sum[..., :HALF].astype(F32)
    full_qkv = jnp.concatenate([attn_rows[0], attn_rows[1, :, :D]], 1)

    return (
        layer_out,
        input_grad,
        full_qkv,
        s_qv,
        attn_rows[1, :, D:],
        s_ob,
        s_g1,
        s_b1,
        in_rows,
        s_ib,
        down_rows,
        s_db,
        s_g2,
        s_b2,
    )


def solution(mesh):
    rows = P(("narrow", "wide"), None)
    marks = P(("narrow", "wide"))
    matrix = P("wide", None)
    vector = P("wide")
    in_specs = (rows, marks, marks, P(), matrix, vector, matrix, vector, vector, vector)
    in_specs = in_specs + (matrix, vector, matrix, vector, vector, vector, rows)
    out_specs = (rows, rows, matrix, vector, matrix, vector, vector, vector)
    out_specs = out_specs + (matrix, vector, matrix, vector, vector, vector)
    return jax.shard_map(body, mesh=mesh, in_specs=in_specs, out_specs=out_specs, check_vma=False)
```

```python
import functools
import math

import jax
import jax.numpy as jnp
from jax import lax
from jax.experimental import pallas as pl
from jax.experimental.pallas import tpu as pltpu
from jax.sharding import PartitionSpec as P

D = 768
HEADS = 12
HEAD_DIM = 64
FF = 3072
SEQ = 128
EPS = 1e-12
AXES = ("narrow", "wide")
F32 = jnp.float32
BF16 = jnp.bfloat16


def alibi_slopes(count):
    power = 2 ** int(math.floor(math.log2(count)))
    values = [2.0 ** (-8.0 * (number + 1) / power) for number in range(power)]
    extra = [2.0 ** (-8.0 * (number + 1) / (2 * power)) for number in range(2 * power)]
    values = values + extra[0::2][: count - power]
    return values


class Place:
    def __init__(self, narrow, wide):
        self.narrow = narrow
        self.wide = wide
        self.chips = wide // 2
        self.direct = narrow == 2 and wide == 16
        self.ny = 2 if self.direct else 1
        self.nz = self.chips // self.ny
        across = lax.axis_index("narrow")
        along = lax.axis_index("wide")
        self.x = across
        self.core = along % 2
        self.chip = along // 2
        self.y = self.chip % self.ny
        self.z = self.chip // self.ny

    def move(self, values, target):
        pairs = []
        for x in range(self.narrow):
            for z in range(self.nz):
                for y in range(self.ny):
                    for c in range(2):
                        tx, tz, ty, tc = target(x, z, y, c)
                        source = ((x * self.nz + z) * self.ny + y) * 2 + c
                        goal = ((tx * self.nz + tz) * self.ny + ty) * 2 + tc
                        pairs.append((source, goal))
        return lax.ppermute(values, AXES, pairs)

    def swap_core(self, values):
        return self.move(values, lambda x, z, y, c: (x, z, y, 1 - c))

    def swap_narrow(self, values):
        return self.move(values, lambda x, z, y, c: (1 - x, z, y, c))

    def swap_y(self, values):
        return self.move(values, lambda x, z, y, c: (x, z, 1 - y, c))

    def first(self, values):
        return self.move(
            values, lambda x, z, y, c: (1 - x, z, y, c) if c == 0 else (x, z, 1 - y, c)
        )

    def second(self, values):
        return self.move(
            values, lambda x, z, y, c: (x, z, 1 - y, c) if c == 0 else (1 - x, z, y, c)
        )

    def diagonal(self, values):
        return self.move(values, lambda x, z, y, c: (1 - x, z, 1 - y, c))

    def along_z(self, values):
        lines = [
            [(z * self.ny + y) * 2 + c for z in range(self.nz)] for y in range(self.ny) for c in range(2)
        ]
        return lax.all_to_all(
            values, "wide", split_axis=0, concat_axis=0, axis_index_groups=lines, tiled=True
        )

    def column_z(self, values):
        column = [values]
        for step in range(1, self.nz):
            column.append(
                self.move(values, lambda x, z, y, c: (x, (z + step) % self.nz, y, c))
            )
        return column

    def spread_z(self, values):
        return self.along_z(jnp.broadcast_to(values[None], (self.nz,) + values.shape))

    def spots(self, core, steps):
        if not self.direct:
            at = jnp.arange(16, dtype=jnp.int32)
            return at // 2, at % 2
        m = jnp.arange(16) // 4
        z = (self.z - jnp.arange(16)) % 4 if steps else jnp.arange(16) % 4
        on_first = (m == 1) | (m == 3)
        on_second = (m == 2) | (m == 3)
        flip_x = jnp.where(core == 0, on_first, on_second).astype(jnp.int32)
        flip_y = jnp.where(core == 0, on_second, on_first).astype(jnp.int32)
        y = jnp.bitwise_xor(self.y, flip_y)
        x = jnp.bitwise_xor(self.x, flip_x)
        return (z * self.ny + y).astype(jnp.int32), x.astype(jnp.int32)

    def plane_spots(self, y_first):
        if not self.direct:
            return jnp.arange(8, dtype=jnp.int32)
        at = jnp.arange(8)
        flip, z = (at % 2, at // 2) if y_first else (at // 4, at % 4)
        return (z * self.ny + jnp.bitwise_xor(self.y, flip)).astype(jnp.int32)

    def row_spots(self, core, steps):
        chip, half = self.spots(core, steps)
        return jnp.stack([chip * 2 + core, half])


ANYWHERE = pl.BlockSpec(memory_space=pl.ANY)
IN_HBM = pl.BlockSpec(memory_space=pltpu.HBM)
KEPT = pl.BlockSpec(memory_space=pltpu.VMEM)
SCALARS = pl.BlockSpec(memory_space=pltpu.SMEM)
VECTORS = pl.BlockSpec(memory_space=pltpu.VMEM)
PAIRS = HEADS // 2
HALF = 2 * D
LANES = 128
WIDE = HALF + LANES


def dot(a, b, da, db):
    return lax.dot_general(a, b, (((da,), (db,)), ((), ())), preferred_element_type=F32)


BIG, SMALL = 36, 16


def call(kernel, ins, outs, scratch, flops, moved, *operands):
    operands = [
        pltpu.with_memory_space_constraint(operand, pltpu.HBM) if spec is IN_HBM or spec is KEPT else operand
        for spec, operand in zip(ins, operands, strict=True)
    ]
    windows = any(spec.block_shape is not None for spec in ins)
    return pl.pallas_call(
        kernel,
        grid=(1,) if windows else (),
        in_specs=ins,
        out_specs=[spec for spec, _, _ in outs],
        out_shape=[
            pltpu.HBM(shape, dtype)
            if spec is IN_HBM or spec is KEPT
            else jax.ShapeDtypeStruct(shape, dtype)
            for spec, shape, dtype in outs
        ],
        scratch_shapes=scratch,
        cost_estimate=pl.CostEstimate(flops=flops, transcendentals=0, bytes_accessed=moved),
        compiler_params=pltpu.CompilerParams(vmem_limit_bytes=(BIG if kernel is attn_backward_kernel else SMALL) * 1024 * 1024),
    )(*operands)


def normed(values):
    average = jnp.mean(values, -1, keepdims=True)
    center = values - average
    variance = jnp.mean(center * center, -1, keepdims=True)
    scale = lax.rsqrt(variance + EPS)
    return center * scale, scale


def norm_back(grad, unit, scale, gain):
    e = grad * gain
    return scale * (
        e - jnp.mean(e, -1, keepdims=True) - unit * jnp.mean(e * unit, -1, keepdims=True)
    )


def split_heads(pair):
    low = lax.broadcasted_iota(jnp.int32, pair.shape, 1) < HEAD_DIM
    zero = jnp.zeros_like(pair)
    return jnp.concatenate([jnp.where(low, pair, zero), jnp.where(low, zero, pair)], 0)


def join_heads(stacked):
    rows = stacked.shape[0] // 2
    low = lax.broadcasted_iota(jnp.int32, (rows, LANES), 1) < HEAD_DIM
    return jnp.where(low, stacked[:rows], stacked[rows:])


def block_list(arrays):
    blocks = []
    for array in arrays:
        for i in range(array.shape[0]):
            if len(array.shape) == 4:
                blocks += [array.at[i, j] for j in range(array.shape[1])]
            else:
                blocks.append(array.at[i])
    return blocks


def fetch_rows(sources, spots, hold, sems):
    copies = []
    for at, block in enumerate(block_list(sources)):
        size = block.shape[0]
        to = pl.multiple_of(spots[at] * size, size)
        copies.append(pltpu.make_async_copy(block, hold.at[pl.ds(to, size)], sems.at[at]))
    for copy in copies:
        copy.start()
    return copies


def emit_rows(source, outs, spots, sems):
    copies = []
    for at, block in enumerate(block_list(outs)):
        size = block.shape[0]
        start = pl.multiple_of(spots[at] * size, size)
        copies.append(pltpu.make_async_copy(source.at[pl.ds(start, size)], block, sems.at[at]))
    for copy in copies:
        copy.start()
    for copy in copies:
        copy.wait()


def fetch_attn(blocks, spots, hold, sems):
    copies = []
    for at, block in enumerate(block_list(blocks)):
        size = block.shape[0]
        row = pl.multiple_of(spots[0, at] * size, size)
        lane = pl.multiple_of(spots[1, at] * WIDE, LANES)
        copies.append(
            pltpu.make_async_copy(
                block, hold.at[pl.ds(row, size), pl.ds(lane, WIDE)], sems.at[at]
            )
        )
    for copy in copies:
        copy.start()
    return copies


SMALL_ROWS = 16
BIAS_ROW = 8


def read_vectors(hold, quarter, vectors, in_shift):
    owners = 16
    size = D // owners
    tall = lax.broadcasted_iota(jnp.int32, (4, 2 * size), 0) == quarter[0]
    for owner in range(owners):
        at = owner * size
        lane = (owner % (owners // 2)) * 2 * size
        row = owner // (owners // 2)
        region = hold[at : at + SMALL_ROWS, HALF:WIDE].astype(F32)
        vectors[row : row + 1, lane : lane + 2 * size] = region[0:1, : 2 * size]
        vectors[2:8, at : at + size] = region[1:7, :size]
        bias = jnp.where(tall, region[BIAS_ROW : BIAS_ROW + 4, : 2 * size], 0.0)
        in_shift[:, owner * 2 * size : (owner + 1) * 2 * size] = jnp.sum(bias, 0, keepdims=True)


VALUE_AT = WIDE
OUT_AT = WIDE + D


def attn_forward_kernel(
    start, b0, b1, b2, b3, b4, b5, b6, b7, spots, quarter,
    context, probs, qkv, unit, scale, hidden, vectors, in_shift, hold, sems,
):
    for copy in fetch_attn((b0, b1, b2, b3, b4, b5, b6, b7), spots, hold, sems):
        copy.wait()
    read_vectors(hold, quarter, vectors, in_shift)
    rows = start.shape[0]
    begin = start[...]
    for part, at in enumerate((0, D, VALUE_AT)):
        made = dot(begin, hold[:, at : at + D], 1, 0)
        if part != 1:
            made = made + vectors[part // 2 : part // 2 + 1, :]
        qkv[:, part * D : (part + 1) * D] = made.astype(BF16)
    distance = jnp.abs(
        lax.broadcasted_iota(jnp.int32, (SEQ, SEQ), 0) - lax.broadcasted_iota(jnp.int32, (SEQ, SEQ), 1)
    ).astype(F32)
    slopes = alibi_slopes(HEADS)
    for s in range(rows // SEQ):
        span = slice(s * SEQ, (s + 1) * SEQ)
        for pair in range(PAIRS):
            lane = pair * LANES
            queries = qkv[span, lane : lane + LANES]
            keys = qkv[span, D + lane : D + lane + LANES]
            values = qkv[span, 2 * D + lane : 2 * D + lane + LANES]
            raw = dot(split_heads(queries), keys, 1, 1)
            fall = jnp.concatenate([distance * slopes[2 * pair], distance * slopes[2 * pair + 1]], 0)
            scores = raw * HEAD_DIM ** (-0.5) - fall
            expo = jnp.exp(scores - jnp.max(scores, -1, keepdims=True))
            made = expo / jnp.sum(expo, -1, keepdims=True)
            probs[s, pair] = made
            joined = join_heads(dot(made.astype(BF16), values, 1, 0))
            context[span, lane : lane + LANES] = joined.astype(BF16)
    first_sum = begin.astype(F32) + dot(context[...], hold[:, OUT_AT : OUT_AT + D], 1, 0)
    made, factor = normed(first_sum + vectors[2:3, :])
    unit[...] = made
    scale[...] = factor
    hidden[...] = (made * vectors[3:4, :] + vectors[4:5, :]).astype(BF16)


def by_sequence(values):
    return jnp.concatenate(
        [v[i : i + SEQ, :] for i in range(0, values[0].shape[0], SEQ) for v in values], 0
    )


def ffn_kernel(
    h0, h1, h2, h3, spots, w0, w1, w2, w3, shift, down_spots, down,
    act, gelu_out, slope_out, hold, down_hold, part0, near0, theirs0, part1, near1, theirs1,
    sems, down_sems,
):
    copies = fetch_rows((w0, w1, w2, w3), spots, hold, sems)
    down_copies = fetch_rows((down,), down_spots, down_hold, down_sems)
    both = by_sequence((h0, h1, h2, h3))
    for copy in copies:
        copy.wait()
    width = act.shape[1]
    block = 256
    for at in range(0, width, block):
        cols = slice(at, at + block)
        more = slice(width + at, width + at + block)
        gate = dot(both, hold[:, cols], 1, 0) + shift[:, cols]
        up = dot(both, hold[:, more], 1, 0) + shift[:, more]
        cdf = 0.5 + 0.5 * lax.erf(gate * (0.5**0.5))
        gelu = gate * cdf
        slope = cdf + gate * jnp.exp(-0.5 * gate * gate) * ((2 * math.pi) ** -0.5)
        act[:, cols] = (gelu * up).astype(BF16)
        gelu_out[:, cols] = gelu.astype(BF16)
        slope_out[:, cols] = (slope * up).astype(BF16)
    for copy in down_copies:
        copy.wait()
    for i, (part, near, theirs) in enumerate(((part0, near0, theirs0), (part1, near1, theirs1))):
        made = dot(act[i * 4 * SEQ : (i + 1) * 4 * SEQ, :], down_hold[...], 1, 0)
        part[...] = made[:SEQ]
        near[...] = made[SEQ : 2 * SEQ]
        theirs[...] = made[2 * SEQ :].astype(BF16)


def turn_kernel(mine, core, got, hidden, vectors, cotangent, layer_out, second, branch, sums):
    part = mine[...] + core[: mine.shape[0], :].astype(F32) + got[...].astype(F32)
    total = hidden[...].astype(F32) + (part + vectors[5:6, :])
    unit, scale = normed(total)
    layer_out[...] = (unit * vectors[6:7, :] + vectors[7:8, :]).astype(BF16)
    grad = cotangent[...].astype(F32)
    back = norm_back(grad, unit, scale, vectors[6:7, :])
    second[...] = back
    low = back.astype(BF16)
    branch[...] = low
    sums[0:1, :] = jnp.sum(low.astype(F32), 0, keepdims=True)
    sums[1:2, :] = jnp.sum(grad * unit, 0, keepdims=True)
    sums[2:3, :] = jnp.sum(grad, 0, keepdims=True)


def down_grad_kernel(act, g0, g1, g2, g3, g4, g5, g6, g7, spots, p0, p1, hold, sems):
    both = jnp.concatenate([g[...] for g in (g0, g1, g2, g3, g4, g5, g6, g7)], 0)
    hold[...] = dot(act[...], both, 0, 0).astype(BF16)
    emit_rows(hold, (p0, p1), spots, sems)


def back_kernel(
    g0, g1, g2, g3, g4, g5, g6, g7, gelu, slope, hold, in_hold, back, sums, part, near, other
):
    both = jnp.concatenate([g[...] for g in (g0, g1, g2, g3, g4, g5, g6, g7)], 0)
    width = gelu.shape[1]
    block = 256
    for at in range(0, width, block):
        cols = slice(at, at + block)
        more = slice(width + at, width + at + block)
        grad = dot(both, hold[cols, :], 1, 1)
        for cut, factor in ((cols, slope), (more, gelu)):
            low = (grad * factor[:, cols].astype(F32)).astype(BF16)
            back[:, cut] = low
            sums[:, cut] = jnp.sum(low.astype(F32), 0, keepdims=True)
    made = dot(back[...], in_hold[...], 1, 1)
    count = part.shape[0] // SEQ
    for i in range(count):
        at = 4 * SEQ * i
        here, there = slice(i * SEQ, (i + 1) * SEQ), slice((count + i) * SEQ, (count + i + 1) * SEQ)
        part[here, :] = made[at : at + SEQ]
        near[here, :] = made[at + SEQ : at + 2 * SEQ]
        other[here, :] = made[at + 2 * SEQ : at + 3 * SEQ].astype(BF16)
        other[there, :] = made[at + 3 * SEQ : at + 4 * SEQ].astype(BF16)


def in_grad_kernel(h0, h1, h2, h3, back, goal, p0, p1, made, out_sems):
    made[...] = dot(by_sequence((h0, h1, h2, h3)), back[...], 0, 0).astype(BF16)
    emit_rows(made, (p0, p1), goal, out_sems)


def attn_backward_kernel(
    s0, s1, mine, core, near, unit, scale, vectors, keep, context, probs, qkv,
    b0, b1, b2, b3, b4, b5, b6, b7, spots, start, turn0, turn1, in_sums, quarter, goal,
    input_grad, sums, k0, k1, k2, k3, give,
    hold, grad_context, grad_attn, grad_qkv, made_hold, sems, out_sems,
):
    copies = fetch_attn((b0, b1, b2, b3, b4, b5, b6, b7), spots, hold, sems)
    rows = unit.shape[0]
    grad = jnp.concatenate([s0[...], s1[...]], 0) + mine[...]
    grad = grad + core[:rows, :].astype(F32) + near[...].astype(F32)
    made = unit[...]
    sums[0:1, :] = jnp.sum(grad * made, 0, keepdims=True)
    sums[1:2, :] = jnp.sum(grad, 0, keepdims=True)
    first = norm_back(grad, made, scale[...], vectors[3:4, :])
    low = first.astype(BF16)
    grad_attn[...] = low
    sums[2:3, :] = jnp.sum(low.astype(F32), 0, keepdims=True)
    for copy in copies:
        copy.wait()
    grad_context[...] = dot(low, hold[:, OUT_AT : OUT_AT + D], 1, 1).astype(BF16)
    for s in range(rows // SEQ):
        span = slice(s * SEQ, (s + 1) * SEQ)
        for pair in range(PAIRS):
            lane = pair * LANES
            queries = split_heads(qkv[span, lane : lane + LANES])
            keys = qkv[span, D + lane : D + lane + LANES]
            values = qkv[span, 2 * D + lane : 2 * D + lane + LANES]
            outer = split_heads(grad_context[span, lane : lane + LANES])
            weight = probs[s, pair]
            grad_probs = dot(outer, values, 1, 1)
            inner = jnp.sum(weight * grad_probs, -1, keepdims=True)
            grad_raw = (weight * (grad_probs - inner) * HEAD_DIM ** (-0.5)).astype(BF16)
            grad_queries = join_heads(dot(grad_raw, keys, 1, 0))
            grad_keys = dot(grad_raw, queries, 0, 0)
            grad_values = dot(weight.astype(BF16), outer, 0, 0)
            grad_qkv[span, lane : lane + LANES] = grad_queries.astype(BF16)
            grad_qkv[span, D + lane : D + lane + LANES] = grad_keys.astype(BF16)
            grad_qkv[span, 2 * D + lane : 2 * D + lane + LANES] = grad_values.astype(BF16)
    sums[3:4, :] = jnp.sum(grad_qkv[:, :D].astype(F32), 0, keepdims=True)
    sums[4:5, :] = jnp.sum(grad_qkv[:, 2 * D :].astype(F32), 0, keepdims=True)
    total = first
    for part, at in enumerate((0, D, VALUE_AT)):
        total = total + dot(grad_qkv[:, part * D : (part + 1) * D], hold[:, at : at + D], 1, 1)
    input_grad[...] = total * keep[...]
    attn_grad(
        start, grad_qkv, context, grad_attn, sums, turn0, turn1, in_sums, quarter, goal,
        (k0, k1, k2, k3), give, made_hold, out_sems,
    )


def attn_grad(
    start, grad_qkv, context, grad_attn, sums, turn0, turn1, in_sums, quarter, goal, keep, give, hold, sems
):
    begin = start[...]
    size = give.shape[1]
    owners = D // size
    hold[:, HALF:WIDE] = jnp.zeros((D, LANES), BF16)
    hold[:, WIDE + HALF : 2 * WIDE] = jnp.zeros((D, LANES), BF16)
    tall = lax.broadcasted_iota(jnp.int32, (4, 2 * size), 0) == quarter[0]
    for owner in range(owners):
        at = owner * size
        lane = (owner % (owners // 2)) * 2 * size
        row = 3 + owner // (owners // 2)
        bias = in_sums[:, owner * 2 * size : (owner + 1) * 2 * size]
        wide = [sums[row : row + 1, lane : lane + 2 * size]]
        narrow = [sums[i : i + 1, at : at + size] for i in (2, 0, 1)]
        narrow.append(turn0[:, at : at + size] + turn1[:, at : at + size])
        narrow = jnp.concatenate(narrow + [jnp.zeros((1, size), F32)], 0)
        narrow = jnp.concatenate([narrow, jnp.zeros_like(narrow)], 1)
        made = jnp.concatenate(
            wide + [narrow, jnp.where(tall, bias, 0.0), jnp.zeros((4, 2 * size), F32)], 0
        )
        hold[at : at + SMALL_ROWS, HALF : HALF + 2 * size] = made.astype(BF16)
    for part, at in enumerate((0, D, VALUE_AT)):
        hold[:, at : at + D] = dot(begin, grad_qkv[:, part * D : (part + 1) * D], 0, 0).astype(BF16)
    hold[:, OUT_AT : OUT_AT + D] = dot(context[...], grad_attn[...], 0, 0).astype(BF16)
    copies = []
    for side in range(2):
        for at in range(16):
            row = pl.multiple_of(goal[1 - side, 0, at] * size, size)
            lane = pl.multiple_of(goal[1 - side, 1, at] * WIDE, LANES)
            copies.append(
                pltpu.make_async_copy(
                    hold.at[pl.ds(row, size), pl.ds(lane, WIDE)],
                    give.at[at] if side == 0 else keep[at // 4].at[at % 4],
                    sems.at[side * 16 + at],
                )
            )
    for copy in copies:
        copy.start()
    for copy in copies:
        copy.wait()


def block_at(i, step):
    return i, 0


def tie(*values):
    return lax.optimization_barrier(values)


def square_gather(column, place):
    one = place.first(column)
    return column, one, place.second(column), place.second(one)


def halves(place, mine):
    mine = mine.astype(BF16)
    other = place.swap_narrow(mine)
    return jnp.where(place.x == 0, jnp.stack([mine, other]), jnp.stack([other, mine]))


def square_sum(blocks, place):
    zero, one, two, three = blocks
    one = sum_of([one, place.second(three)]).astype(BF16)
    zero = sum_of([zero, place.second(two), place.first(one)]).astype(BF16)
    return place.along_z(zero)


def plane_all(piece, place):
    whole = lax.all_gather(piece, "wide", axis=0, tiled=False)
    whole = whole.reshape((place.chips, 2) + piece.shape)
    return by_core(place, whole, 1).reshape(8, -1, piece.shape[-1])


def plane_across(blocks, size, place):
    if place.direct:
        return [place.swap_y(values) for values in blocks[1:]]
    order = jnp.concatenate(blocks).reshape(place.chips, 1, size, blocks[0].shape[-1])
    zeros = jnp.zeros_like(order)
    order = jnp.where(
        place.core == 0, jnp.concatenate([order, zeros], 1), jnp.concatenate([zeros, order], 1)
    )
    order = order.reshape((-1,) + order.shape[2:]).astype(F32)
    return [lax.psum_scatter(order, "wide", scatter_dimension=0, tiled=True)]


def plane_along(near, far, place):
    if not place.direct:
        return far[0]
    return place.along_z(sum_of([near, far[0]]).astype(BF16))


def sum_of(parts):
    total = parts[0].astype(F32)
    for i in range(1, len(parts)):
        total = total + parts[i].astype(F32)
    return total


def by_core(place, values, axis):
    return jnp.where(
        place.core == 0,
        lax.index_in_dim(values, 0, axis, keepdims=False),
        lax.index_in_dim(values, 1, axis, keepdims=False),
    )


def by_narrow(place, values, axis):
    return jnp.where(
        place.x == 0,
        lax.index_in_dim(values, 0, axis, keepdims=False),
        lax.index_in_dim(values, 1, axis, keepdims=False),
    )


def quarter_sum(near, theirs, rows, place):
    got = place.swap_core(theirs)
    near = (near + got[rows:].astype(F32)).astype(BF16)
    return got, place.swap_narrow(near)


def with_small(rows, vectors, owned):
    both = jnp.swapaxes(rows.reshape(owned, 2, HALF), 0, 1)
    qv, ob, g1, b1, ib, db, g2, b2 = vectors
    width = 2 * owned
    narrow = jnp.stack([ob, g1, b1, db, g2, b2])
    narrow = jnp.pad(narrow, ((0, 1), (0, owned)))
    small = jnp.concatenate([qv[None], narrow, ib.reshape(4, width)])
    small = jnp.pad(small, ((0, owned - small.shape[0]), (0, LANES - width)))
    small = jnp.stack([small, jnp.zeros_like(small)])
    return jnp.concatenate([both, small], 2)


def gather_attn(rows, vectors, owned, place):
    full = lax.all_gather(rows, "wide", axis=0, tiled=True)
    parts = [lax.all_gather(v, "wide", axis=0, tiled=True) for v in vectors]
    size = D // 16
    parts = [v.reshape(16, -1) for v in parts]
    ib = parts[4].reshape(2, place.chips, 2, 2, -1).reshape(2, 8, -1, 2, 2, parts[4].size // (place.wide * 4))
    parts[4] = ib.transpose(0, 1, 3, 4, 2, 5).reshape(16, 4 * 2 * size)
    blocks = [
        with_small(full[i * size : (i + 1) * size], [v[i] for v in parts], size) for i in range(16)
    ]
    blocks = jnp.stack(blocks).reshape(8, 2, 2, size, WIDE)
    even, odd = [blocks[:, core].reshape(4, 4, size, WIDE) for core in range(2)]
    mine = jnp.where(place.core == 0, even, odd)
    other = jnp.where(place.core == 0, odd, even)
    return [mine[m] for m in range(4)] + [other[m] for m in range(4)]


def reduce_attn(keep, give, owned, place):
    mine = jnp.stack(keep).reshape(8, 2, D // 16, WIDE)
    other = give.reshape(8, 2, D // 16, WIDE)
    full = jnp.where(place.core == 0, jnp.stack([mine, other], 1), jnp.stack([other, mine], 1))
    full = full.transpose(0, 1, 3, 2, 4).reshape(place.wide, owned, 2, WIDE)
    full = jnp.swapaxes(full, 1, 2).astype(F32)
    full = lax.psum_scatter(full, "wide", scatter_dimension=0, tiled=True)[0]
    return lax.psum(full, "narrow").astype(BF16)


def body(
    hidden_in,
    masked,
    token_ids,
    token_table,
    qkv_weight,
    qv_bias,
    out_weight,
    out_bias,
    norm1_gain,
    norm1_bias,
    ffn_in_weight,
    ffn_in_bias,
    ffn_out_weight,
    ffn_out_bias,
    norm2_gain,
    norm2_bias,
    out_cotangent,
):
    place = Place(lax.axis_size("narrow"), lax.axis_size("wide"))
    wide = place.wide
    chips = place.chips
    owned = qkv_weight.shape[0]
    units = ffn_out_weight.shape[0]
    rows = hidden_in.shape[0]
    seqs = rows // SEQ

    chosen = (masked > 0)[:, None]
    replaced, ffn_in_weight = tie(jnp.take(token_table, token_ids, axis=0), ffn_in_weight)
    start = jnp.where(chosen, replaced, hidden_in)

    attn_come = jnp.concatenate(
        [place.row_spots(place.core, True), place.row_spots(1 - place.core, True)], 1
    )
    in_come = place.plane_spots(False)
    down_come = place.plane_spots(True)
    leave = place.plane_spots(False)
    attn_leave = jnp.stack([place.row_spots(place.core, False), place.row_spots(1 - place.core, False)])
    quarter_at = (place.core * 2 + place.x).reshape(1).astype(jnp.int32)

    small = (qv_bias, out_bias, norm1_gain, norm1_bias, ffn_in_bias, ffn_out_bias, norm2_gain, norm2_bias)
    attn_own = jnp.concatenate([qkv_weight, out_weight], 1)
    half_units = units // 2
    in_blocks = ffn_in_weight.reshape(owned, 2, chips, 2, 2, half_units)
    in_blocks = by_narrow(place, in_blocks, 4)
    in_mine = by_core(place, in_blocks, 3).reshape(owned, FF // 2)
    in_give = by_core(place, jnp.flip(in_blocks, 3), 3).reshape(owned, FF // 2)
    in_got = place.swap_core(in_give)
    in_piece = jnp.where(
        place.core == 0, jnp.concatenate([in_mine, in_got]), jnp.concatenate([in_got, in_mine])
    )
    down_piece = by_narrow(place, ffn_out_weight.reshape(2, half_units, D), 0)
    if place.direct:
        attn_piece = by_narrow(place, with_small(attn_own, small, owned), 0)
        attn_column = place.column_z(attn_piece)
        down_got = place.swap_y(down_piece)
        held = tie(
            *attn_column, down_got, in_piece, start, attn_come, in_come, down_come, leave, attn_leave
        )
        attn_column, held = held[:4], held[4:]
        down_got, in_piece, start, attn_come, in_come, down_come, leave, attn_leave = held
        in_column = place.spread_z(in_piece)
        blocks = [jnp.stack(attn_column)]
        blocks = blocks + [place.first(blocks[0]), place.second(blocks[0])]
        others = [place.swap_core(values) for values in blocks]
        blocks.append(place.second(blocks[1]))
        *held, in_column, down_got = tie(*blocks, *others, in_column, down_got)
        attn_blocks = held + [place.swap_core(held[3])]
        in_first, in_last = in_column[:2], in_column[2:]
        in_weights = [in_first, in_last, place.swap_y(in_first), place.swap_y(in_last)]
        down_weights = place.spread_z(jnp.stack([down_piece, down_got]))
    else:
        attn_blocks = gather_attn(attn_own, small, owned, place)
        whole = plane_all(in_piece, place)
        in_weights = [whole[:2], whole[2:4], whole[4:6], whole[6:]]
        whole = plane_all(down_piece, place)
        down_weights = whole.reshape(4, 2, -1, D)
    block_rows, quarter = D // 8, FF // 4
    eight = pltpu.SemaphoreType.DMA((8,))
    sixteen = pltpu.SemaphoreType.DMA((16,))
    thirty_two = pltpu.SemaphoreType.DMA((32,))
    in_hold = pltpu.VMEM((D, 2 * quarter), BF16)
    down_hold = pltpu.VMEM((quarter, D), BF16)
    attn_hold = pltpu.VMEM((D, 2 * WIDE), BF16)
    V, A, S, H, K = VECTORS, ANYWHERE, SCALARS, IN_HBM, KEPT

    context, probs, qkv, unit, scale, hidden, vectors, in_shift = call(
        attn_forward_kernel,
        [V] + [H] * 8 + [S, S],
        [
            (K, (rows, D), BF16),
            (K, (seqs, PAIRS, 2 * SEQ, SEQ), F32),
            (K, (rows, 3 * D), BF16),
            (K, (rows, D), F32),
            (K, (rows, 1), F32),
            (V, (rows, D), BF16),
            (K, (8, D), F32),
            (V, (1, 2 * quarter), F32),
        ],
        [attn_hold, thirty_two],
        rows * D * D * 10,
        10 << 20,
        start,
        *attn_blocks,
        attn_come,
        quarter_at,
    )
    hidden, in_weights[2] = tie(hidden, in_weights[2])
    hidden_near = place.swap_narrow(hidden)
    hidden_core = place.swap_core(hidden)
    hidden_near, in_weights[3] = tie(hidden_near, in_weights[3])
    hidden_far = place.swap_core(hidden_near)
    hidden_far, down_weights = tie(hidden_far, down_weights)
    inputs = (hidden, hidden_near, hidden_core, hidden_far)
    count = rows // SEQ
    part_shapes = [(V, (SEQ, D), F32), (V, (SEQ, D), F32), (V, (2 * SEQ, D), BF16)]
    act, gelu, slope, in_whole, down_whole, *parts = call(
        ffn_kernel,
        [V, V, V, V, S, H, H, H, H, V, S, H],
        [(V, (4 * rows, quarter), BF16)] * 3
        + [(V, (D, 2 * quarter), BF16), (V, (quarter, D), BF16)]
        + part_shapes * count,
        [eight, eight],
        rows * D * FF * 12,
        16 << 20,
        *inputs,
        in_come,
        *in_weights,
        in_shift,
        down_come,
        down_weights,
    )
    parts = [parts[3 * i : 3 * i + 3] for i in range(count)]
    turned = []
    for i, (part, near, theirs) in enumerate(parts):
        core_got, got = quarter_sum(near, theirs, SEQ, place)
        row = pl.BlockSpec((SEQ, D), functools.partial(block_at, i))
        turned.append(
            call(
                turn_kernel,
                [V, V, V, row, V, row],
                [(K, (SEQ, D), BF16), (K, (SEQ, D), F32), (V, (SEQ, D), BF16), (K, (3, D), F32)],
                [],
                SEQ * D * 30,
                5 << 20,
                part,
                core_got,
                got,
                hidden,
                vectors,
                out_cotangent,
            )
        )
    layer_out = jnp.concatenate([made[0] for made in turned])

    gradients = []
    for made in turned:
        near = place.swap_narrow(made[2])
        gradients += [made[2], near, place.swap_core(made[2]), place.swap_core(near)]
    back, in_sums, part, near, theirs = call(
        back_kernel,
        [V] * 12,
        [
            (V, (4 * rows, 2 * quarter), BF16),
            (K, (1, 2 * quarter), F32),
            (K, (rows, D), F32),
            (V, (rows, D), F32),
            (V, (2 * rows, D), BF16),
        ],
        [],
        rows * D * FF * 8,
        18 << 20,
        *gradients,
        gelu,
        slope,
        down_whole,
        in_whole,
    )
    theirs, act = tie(theirs, act)
    down_blocks = call(
        down_grad_kernel,
        [V] * 9 + [S],
        [(A, (4, block_rows, D), BF16)] * 2,
        [down_hold, eight],
        rows * D * FF * 2,
        6 << 20,
        act,
        *gradients,
        leave,
    )
    core_got = place.swap_core(theirs)
    near, back = tie((near + core_got[rows:].astype(F32)).astype(BF16), back)
    got = place.swap_narrow(near)
    in_blocks = call(
        in_grad_kernel,
        [V] * 5 + [S],
        [(A, (4, block_rows, 2 * quarter), BF16)] * 2,
        [in_hold, eight],
        rows * D * FF * 8,
        18 << 20,
        *inputs,
        back,
        leave,
    )
    in_far = plane_across(in_blocks, 2 * owned, place)
    down_far = plane_across(down_blocks, half_units, place)
    got, *held = tie(got, *down_far, in_blocks[0])
    down_parts = plane_along(down_blocks[0], held[:-1], place)
    adds = [made[1] for made in turned] + [part, core_got, got]
    turn_sums = [made[3] for made in turned]
    keep_rows = jnp.broadcast_to(jnp.where(chosen, 0.0, 1.0), (rows, 1)).astype(F32)
    input_grad, attn_sums, *blocks = call(
        attn_backward_kernel,
        [K, K, K, V, K, K, K, K, V, K, K, K] + [H] * 8 + [S, K, K, K, K, S, S],
        [(K, (rows, D), F32), (V, (5, D), F32)]
        + [(H, (4, D // 16, WIDE), BF16)] * 4
        + [(H, (16, D // 16, WIDE), BF16)],
        [
            attn_hold,
            pltpu.VMEM((rows, D), BF16),
            pltpu.VMEM((rows, D), BF16),
            pltpu.VMEM((rows, 3 * D), BF16),
            attn_hold,
            thirty_two,
            thirty_two,
        ],
        rows * D * D * 20,
        22 << 20,
        *adds,
        unit,
        scale,
        vectors,
        keep_rows,
        context,
        probs,
        qkv,
        *attn_blocks,
        attn_come,
        start,
        *turn_sums,
        in_sums,
        quarter_at,
        attn_leave,
    )
    give, down_parts, *in_far = tie(blocks[4], down_parts, *in_far)
    if place.direct:
        got = place.swap_core(give)
        keep = [sum_of([blocks[m], got[4 * m : 4 * m + 4]]).astype(BF16) for m in range(4)]
        attn_parts = square_sum(keep, place)
    in_sum = sum_of(plane_along(in_blocks[0], in_far, place)).astype(BF16).reshape(2, owned, 2 * quarter)
    mine = jnp.where(place.core == 0, in_sum[0], in_sum[1])
    give = jnp.where(place.core == 0, in_sum[1], in_sum[0])
    got = place.swap_core(give)
    pair = jnp.where(place.core == 0, jnp.stack([mine, got]), jnp.stack([got, mine]))
    in_rows = halves(place, pair).reshape(2, 2, owned, 2, chips, half_units)
    in_rows = in_rows.transpose(2, 3, 4, 1, 0, 5).reshape(owned, 2 * FF).astype(F32)
    down_rows = halves(place, sum_of(down_parts)).reshape(units, D).astype(F32)

    if place.direct:
        attn_half, in_rows, down_rows = tie(sum_of(attn_parts).astype(BF16), in_rows, down_rows)
        attn_sum = halves(place, attn_half)
        lanes = attn_sum[0, :SMALL_ROWS, HALF:].astype(F32)
        s_qv = lanes[0, : 2 * owned]
        s_ob, s_g1, s_b1, s_db, s_g2, s_b2 = [lanes[i, :owned] for i in range(1, 7)]
        s_ib = lanes[BIAS_ROW : BIAS_ROW + 4, : 2 * owned].reshape(-1)
    else:
        attn_sum = reduce_attn(blocks[:4], blocks[4], owned, place)
        turn_sums = sum_of(turn_sums)
        ib_blocks = in_sums.reshape(2, chips, 1, 1, half_units)
        at_core = (jnp.arange(2) == place.core).astype(F32).reshape(1, 1, 2, 1, 1)
        at_narrow = (jnp.arange(2) == place.x).astype(F32).reshape(1, 1, 1, 2, 1)
        sums = [attn_sums[3:5], attn_sums[2], attn_sums[0], attn_sums[1]]
        sums = sums + [ib_blocks * at_core * at_narrow, turn_sums[0], turn_sums[1], turn_sums[2]]
        widths = [v.size // wide for v in sums]
        sums = jnp.concatenate([v.reshape(wide, -1) for v in sums], 1)
        sums = lax.psum(sums, AXES)[lax.axis_index("wide")]
        ends = [sum(widths[: i + 1]) for i in range(len(widths) - 1)]
        s_qv, s_ob, s_g1, s_b1, s_ib, s_db, s_g2, s_b2 = jnp.split(sums, ends)
    attn_rows = attn_sum[..., :HALF].astype(F32)
    full_qkv = jnp.concatenate([attn_rows[0], attn_rows[1, :, :D]], 1)

    return (
        layer_out,
        input_grad,
        full_qkv,
        s_qv,
        attn_rows[1, :, D:],
        s_ob,
        s_g1,
        s_b1,
        in_rows,
        s_ib,
        down_rows,
        s_db,
        s_g2,
        s_b2,
    )


def solution(mesh):
    rows = P(("narrow", "wide"), None)
    marks = P(("narrow", "wide"))
    matrix = P("wide", None)
    vector = P("wide")
    in_specs = (rows, marks, marks, P(), matrix, vector, matrix, vector, vector, vector)
    in_specs = in_specs + (matrix, vector, matrix, vector, vector, vector, rows)
    out_specs = (rows, rows, matrix, vector, matrix, vector, vector, vector)
    out_specs = out_specs + (matrix, vector, matrix, vector, vector, vector)
    return jax.shard_map(body, mesh=mesh, in_specs=in_specs, out_specs=out_specs, check_vma=False)
```

```python
import functools
import math

import jax
import jax.numpy as jnp
from jax import lax
from jax.experimental import pallas as pl
from jax.experimental.pallas import tpu as pltpu
from jax.sharding import PartitionSpec as P

D = 768
HEADS = 12
HEAD_DIM = 64
FF = 3072
SEQ = 128
EPS = 1e-12
AXES = ("narrow", "wide")
F32 = jnp.float32
BF16 = jnp.bfloat16


def alibi_slopes(count):
    power = 2 ** int(math.floor(math.log2(count)))
    values = [2.0 ** (-8.0 * (number + 1) / power) for number in range(power)]
    extra = [2.0 ** (-8.0 * (number + 1) / (2 * power)) for number in range(2 * power)]
    values = values + extra[0::2][: count - power]
    return values


class Place:
    def __init__(self, narrow, wide):
        self.narrow = narrow
        self.wide = wide
        self.chips = wide // 2
        self.direct = narrow == 2 and wide == 16
        self.ny = 2 if self.direct else 1
        self.nz = self.chips // self.ny
        across = lax.axis_index("narrow")
        along = lax.axis_index("wide")
        self.x = across
        self.core = along % 2
        self.chip = along // 2
        self.y = self.chip % self.ny
        self.z = self.chip // self.ny

    def move(self, values, target):
        pairs = []
        for x in range(self.narrow):
            for z in range(self.nz):
                for y in range(self.ny):
                    for c in range(2):
                        tx, tz, ty, tc = target(x, z, y, c)
                        source = ((x * self.nz + z) * self.ny + y) * 2 + c
                        goal = ((tx * self.nz + tz) * self.ny + ty) * 2 + tc
                        pairs.append((source, goal))
        return lax.ppermute(values, AXES, pairs)

    def swap_core(self, values):
        return self.move(values, lambda x, z, y, c: (x, z, y, 1 - c))

    def swap_narrow(self, values):
        return self.move(values, lambda x, z, y, c: (1 - x, z, y, c))

    def swap_y(self, values):
        return self.move(values, lambda x, z, y, c: (x, z, 1 - y, c))

    def first(self, values):
        return self.move(
            values, lambda x, z, y, c: (1 - x, z, y, c) if c == 0 else (x, z, 1 - y, c)
        )

    def second(self, values):
        return self.move(
            values, lambda x, z, y, c: (x, z, 1 - y, c) if c == 0 else (1 - x, z, y, c)
        )

    def diagonal(self, values):
        return self.move(values, lambda x, z, y, c: (1 - x, z, 1 - y, c))

    def along_z(self, values):
        lines = [
            [(z * self.ny + y) * 2 + c for z in range(self.nz)] for y in range(self.ny) for c in range(2)
        ]
        return lax.all_to_all(
            values, "wide", split_axis=0, concat_axis=0, axis_index_groups=lines, tiled=True
        )

    def column_z(self, values):
        column = [values]
        for step in range(1, self.nz):
            column.append(
                self.move(values, lambda x, z, y, c: (x, (z + step) % self.nz, y, c))
            )
        return column

    def spread_z(self, values):
        return self.along_z(jnp.broadcast_to(values[None], (self.nz,) + values.shape))

    def spots(self, core, steps):
        if not self.direct:
            at = jnp.arange(16, dtype=jnp.int32)
            return at // 2, at % 2
        m = jnp.arange(16) // 4
        z = (self.z - jnp.arange(16)) % 4 if steps else jnp.arange(16) % 4
        on_first = (m == 1) | (m == 3)
        on_second = (m == 2) | (m == 3)
        flip_x = jnp.where(core == 0, on_first, on_second).astype(jnp.int32)
        flip_y = jnp.where(core == 0, on_second, on_first).astype(jnp.int32)
        y = jnp.bitwise_xor(self.y, flip_y)
        x = jnp.bitwise_xor(self.x, flip_x)
        return (z * self.ny + y).astype(jnp.int32), x.astype(jnp.int32)

    def step_spots(self):
        if not self.direct:
            return jnp.arange(8, dtype=jnp.int32)
        at = jnp.arange(8)
        z = (self.z - at // 2) % self.nz
        return (z * self.ny + jnp.bitwise_xor(self.y, at % 2)).astype(jnp.int32)

    def plane_spots(self, y_first):
        if not self.direct:
            return jnp.arange(8, dtype=jnp.int32)
        at = jnp.arange(8)
        flip, z = (at % 2, at // 2) if y_first else (at // 4, at % 4)
        return (z * self.ny + jnp.bitwise_xor(self.y, flip)).astype(jnp.int32)

    def row_spots(self, core, steps):
        chip, half = self.spots(core, steps)
        return jnp.stack([chip * 2 + core, half])


ANYWHERE = pl.BlockSpec(memory_space=pl.ANY)
IN_HBM = pl.BlockSpec(memory_space=pltpu.HBM)
KEPT = pl.BlockSpec(memory_space=pltpu.VMEM)
SCALARS = pl.BlockSpec(memory_space=pltpu.SMEM)
VECTORS = pl.BlockSpec(memory_space=pltpu.VMEM)
PAIRS = HEADS // 2
HALF = 2 * D
LANES = 128
WIDE = HALF + LANES


def dot(a, b, da, db):
    return lax.dot_general(a, b, (((da,), (db,)), ((), ())), preferred_element_type=F32)


BIG, SMALL = 36, 16


def call(kernel, ins, outs, scratch, flops, moved, *operands):
    operands = [
        pltpu.with_memory_space_constraint(operand, pltpu.HBM) if spec is IN_HBM or spec is KEPT else operand
        for spec, operand in zip(ins, operands, strict=True)
    ]
    windows = any(spec.block_shape is not None for spec in ins)
    return pl.pallas_call(
        kernel,
        grid=(1,) if windows else (),
        in_specs=ins,
        out_specs=[spec for spec, _, _ in outs],
        out_shape=[
            pltpu.HBM(shape, dtype)
            if spec is IN_HBM or spec is KEPT
            else jax.ShapeDtypeStruct(shape, dtype)
            for spec, shape, dtype in outs
        ],
        scratch_shapes=scratch,
        cost_estimate=pl.CostEstimate(flops=flops, transcendentals=0, bytes_accessed=moved),
        compiler_params=pltpu.CompilerParams(vmem_limit_bytes=(BIG if kernel is attn_backward_kernel else SMALL) * 1024 * 1024),
    )(*operands)


def normed(values):
    average = jnp.mean(values, -1, keepdims=True)
    center = values - average
    variance = jnp.mean(center * center, -1, keepdims=True)
    scale = lax.rsqrt(variance + EPS)
    return center * scale, scale


def norm_back(grad, unit, scale, gain):
    e = grad * gain
    return scale * (
        e - jnp.mean(e, -1, keepdims=True) - unit * jnp.mean(e * unit, -1, keepdims=True)
    )


def split_heads(pair):
    low = lax.broadcasted_iota(jnp.int32, pair.shape, 1) < HEAD_DIM
    zero = jnp.zeros_like(pair)
    return jnp.concatenate([jnp.where(low, pair, zero), jnp.where(low, zero, pair)], 0)


def join_heads(stacked):
    rows = stacked.shape[0] // 2
    low = lax.broadcasted_iota(jnp.int32, (rows, LANES), 1) < HEAD_DIM
    return jnp.where(low, stacked[:rows], stacked[rows:])


def block_list(arrays):
    blocks = []
    for array in arrays:
        for i in range(array.shape[0]):
            if len(array.shape) == 4:
                blocks += [array.at[i, j] for j in range(array.shape[1])]
            else:
                blocks.append(array.at[i])
    return blocks


def fetch_rows(sources, spots, hold, sems):
    copies = []
    for at, block in enumerate(block_list(sources)):
        size = block.shape[0]
        to = pl.multiple_of(spots[at] * size, size)
        copies.append(pltpu.make_async_copy(block, hold.at[pl.ds(to, size)], sems.at[at]))
    for copy in copies:
        copy.start()
    return copies


def emit_rows(source, outs, spots, sems):
    copies = []
    for at, block in enumerate(block_list(outs)):
        size = block.shape[0]
        start = pl.multiple_of(spots[at] * size, size)
        copies.append(pltpu.make_async_copy(source.at[pl.ds(start, size)], block, sems.at[at]))
    for copy in copies:
        copy.start()
    for copy in copies:
        copy.wait()


def fetch_attn(blocks, spots, hold, sems):
    copies = []
    for at, block in enumerate(block_list(blocks)):
        size = block.shape[0]
        row = pl.multiple_of(spots[0, at] * size, size)
        lane = pl.multiple_of(spots[1, at] * WIDE, LANES)
        copies.append(
            pltpu.make_async_copy(
                block, hold.at[pl.ds(row, size), pl.ds(lane, WIDE)], sems.at[at]
            )
        )
    for copy in copies:
        copy.start()
    return copies


SMALL_ROWS = 16
BIAS_ROW = 8


def read_vectors(hold, quarter, vectors, in_shift):
    owners = 16
    size = D // owners
    tall = lax.broadcasted_iota(jnp.int32, (4, 2 * size), 0) == quarter[0]
    for owner in range(owners):
        at = owner * size
        lane = (owner % (owners // 2)) * 2 * size
        row = owner // (owners // 2)
        region = hold[at : at + SMALL_ROWS, HALF:WIDE].astype(F32)
        vectors[row : row + 1, lane : lane + 2 * size] = region[0:1, : 2 * size]
        vectors[2:8, at : at + size] = region[1:7, :size]
        bias = jnp.where(tall, region[BIAS_ROW : BIAS_ROW + 4, : 2 * size], 0.0)
        in_shift[:, owner * 2 * size : (owner + 1) * 2 * size] = jnp.sum(bias, 0, keepdims=True)


VALUE_AT = WIDE
OUT_AT = WIDE + D


def attn_forward_kernel(
    start, b0, b1, b2, b3, b4, b5, b6, b7, spots, quarter,
    context, probs, qkv, unit, scale, hidden, vectors, in_shift, hold, sems,
):
    for copy in fetch_attn((b0, b1, b2, b3, b4, b5, b6, b7), spots, hold, sems):
        copy.wait()
    read_vectors(hold, quarter, vectors, in_shift)
    rows = start.shape[0]
    begin = start[...]
    for part, at in enumerate((0, D, VALUE_AT)):
        made = dot(begin, hold[:, at : at + D], 1, 0)
        if part != 1:
            made = made + vectors[part // 2 : part // 2 + 1, :]
        qkv[:, part * D : (part + 1) * D] = made.astype(BF16)
    distance = jnp.abs(
        lax.broadcasted_iota(jnp.int32, (SEQ, SEQ), 0) - lax.broadcasted_iota(jnp.int32, (SEQ, SEQ), 1)
    ).astype(F32)
    slopes = alibi_slopes(HEADS)
    for s in range(rows // SEQ):
        span = slice(s * SEQ, (s + 1) * SEQ)
        for pair in range(PAIRS):
            lane = pair * LANES
            queries = qkv[span, lane : lane + LANES]
            keys = qkv[span, D + lane : D + lane + LANES]
            values = qkv[span, 2 * D + lane : 2 * D + lane + LANES]
            raw = dot(split_heads(queries), keys, 1, 1)
            fall = jnp.concatenate([distance * slopes[2 * pair], distance * slopes[2 * pair + 1]], 0)
            scores = raw * HEAD_DIM ** (-0.5) - fall
            expo = jnp.exp(scores - jnp.max(scores, -1, keepdims=True))
            made = expo / jnp.sum(expo, -1, keepdims=True)
            probs[s, pair] = made
            joined = join_heads(dot(made.astype(BF16), values, 1, 0))
            context[span, lane : lane + LANES] = joined.astype(BF16)
    first_sum = begin.astype(F32) + dot(context[...], hold[:, OUT_AT : OUT_AT + D], 1, 0)
    made, factor = normed(first_sum + vectors[2:3, :])
    unit[...] = made
    scale[...] = factor
    hidden[...] = (made * vectors[3:4, :] + vectors[4:5, :]).astype(BF16)


def by_sequence(values):
    return jnp.concatenate(
        [v[i : i + SEQ, :] for i in range(0, values[0].shape[0], SEQ) for v in values], 0
    )


def ffn_kernel(
    h0, h1, h2, h3, spots, w0, w1, w2, w3, shift, down_spots, d0, d1, d2, d3,
    act, gelu_out, slope_out, hold, down_hold, part0, near0, theirs0, part1, near1, theirs1,
    sems, down_sems,
):
    copies = fetch_rows((w0, w1, w2, w3), spots, hold, sems)
    down_copies = fetch_rows((d0, d1, d2, d3), down_spots, down_hold, down_sems)
    both = by_sequence((h0, h1, h2, h3))
    for copy in copies:
        copy.wait()
    width = act.shape[1]
    block = 256
    for at in range(0, width, block):
        cols = slice(at, at + block)
        more = slice(width + at, width + at + block)
        gate = dot(both, hold[:, cols], 1, 0) + shift[:, cols]
        up = dot(both, hold[:, more], 1, 0) + shift[:, more]
        cdf = 0.5 + 0.5 * lax.erf(gate * (0.5**0.5))
        gelu = gate * cdf
        slope = cdf + gate * jnp.exp(-0.5 * gate * gate) * ((2 * math.pi) ** -0.5)
        act[:, cols] = (gelu * up).astype(BF16)
        gelu_out[:, cols] = gelu.astype(BF16)
        slope_out[:, cols] = (slope * up).astype(BF16)
    for copy in down_copies:
        copy.wait()
    for i, (part, near, theirs) in enumerate(((part0, near0, theirs0), (part1, near1, theirs1))):
        made = dot(act[i * 4 * SEQ : (i + 1) * 4 * SEQ, :], down_hold[...], 1, 0)
        part[...] = made[:SEQ]
        near[...] = made[SEQ : 2 * SEQ]
        theirs[...] = made[2 * SEQ :].astype(BF16)


def turn_kernel(mine, core, got, hidden, vectors, cotangent, layer_out, second, branch, sums):
    part = mine[...] + core[: mine.shape[0], :].astype(F32) + got[...].astype(F32)
    total = hidden[...].astype(F32) + (part + vectors[5:6, :])
    unit, scale = normed(total)
    layer_out[...] = (unit * vectors[6:7, :] + vectors[7:8, :]).astype(BF16)
    grad = cotangent[...].astype(F32)
    back = norm_back(grad, unit, scale, vectors[6:7, :])
    second[...] = back
    low = back.astype(BF16)
    branch[...] = low
    sums[0:1, :] = jnp.sum(low.astype(F32), 0, keepdims=True)
    sums[1:2, :] = jnp.sum(grad * unit, 0, keepdims=True)
    sums[2:3, :] = jnp.sum(grad, 0, keepdims=True)


def down_grad_kernel(act, g0, g1, g2, g3, g4, g5, g6, g7, spots, p0, p1, hold, sems):
    both = jnp.concatenate([g[...] for g in (g0, g1, g2, g3, g4, g5, g6, g7)], 0)
    hold[...] = dot(act[...], both, 0, 0).astype(BF16)
    emit_rows(hold, (p0, p1), spots, sems)


def back_kernel(
    g0, g1, g2, g3, g4, g5, g6, g7, gelu, slope, hold, in_hold, back, sums, part, near, other
):
    both = jnp.concatenate([g[...] for g in (g0, g1, g2, g3, g4, g5, g6, g7)], 0)
    width = gelu.shape[1]
    block = 256
    for at in range(0, width, block):
        cols = slice(at, at + block)
        more = slice(width + at, width + at + block)
        grad = dot(both, hold[cols, :], 1, 1)
        for cut, factor in ((cols, slope), (more, gelu)):
            low = (grad * factor[:, cols].astype(F32)).astype(BF16)
            back[:, cut] = low
            sums[:, cut] = jnp.sum(low.astype(F32), 0, keepdims=True)
    made = dot(back[...], in_hold[...], 1, 1)
    count = part.shape[0] // SEQ
    for i in range(count):
        at = 4 * SEQ * i
        here, there = slice(i * SEQ, (i + 1) * SEQ), slice((count + i) * SEQ, (count + i + 1) * SEQ)
        part[here, :] = made[at : at + SEQ]
        near[here, :] = made[at + SEQ : at + 2 * SEQ]
        other[here, :] = made[at + 2 * SEQ : at + 3 * SEQ].astype(BF16)
        other[there, :] = made[at + 3 * SEQ : at + 4 * SEQ].astype(BF16)


def in_grad_kernel(h0, h1, h2, h3, back, goal, p0, p1, made, out_sems):
    made[...] = dot(by_sequence((h0, h1, h2, h3)), back[...], 0, 0).astype(BF16)
    emit_rows(made, (p0, p1), goal, out_sems)


def attn_backward_kernel(
    s0, s1, mine, core, near, unit, scale, vectors, keep, context, probs, qkv,
    b0, b1, b2, b3, b4, b5, b6, b7, spots, start, turn0, turn1, in_sums, quarter, goal,
    input_grad, sums, k0, k1, k2, k3, give,
    hold, grad_context, grad_attn, grad_qkv, made_hold, sems, out_sems,
):
    copies = fetch_attn((b0, b1, b2, b3, b4, b5, b6, b7), spots, hold, sems)
    rows = unit.shape[0]
    grad = jnp.concatenate([s0[...], s1[...]], 0) + mine[...]
    grad = grad + core[:rows, :].astype(F32) + near[...].astype(F32)
    made = unit[...]
    sums[0:1, :] = jnp.sum(grad * made, 0, keepdims=True)
    sums[1:2, :] = jnp.sum(grad, 0, keepdims=True)
    first = norm_back(grad, made, scale[...], vectors[3:4, :])
    low = first.astype(BF16)
    grad_attn[...] = low
    sums[2:3, :] = jnp.sum(low.astype(F32), 0, keepdims=True)
    for copy in copies:
        copy.wait()
    grad_context[...] = dot(low, hold[:, OUT_AT : OUT_AT + D], 1, 1).astype(BF16)
    for s in range(rows // SEQ):
        span = slice(s * SEQ, (s + 1) * SEQ)
        for pair in range(PAIRS):
            lane = pair * LANES
            queries = split_heads(qkv[span, lane : lane + LANES])
            keys = qkv[span, D + lane : D + lane + LANES]
            values = qkv[span, 2 * D + lane : 2 * D + lane + LANES]
            outer = split_heads(grad_context[span, lane : lane + LANES])
            weight = probs[s, pair]
            grad_probs = dot(outer, values, 1, 1)
            inner = jnp.sum(weight * grad_probs, -1, keepdims=True)
            grad_raw = (weight * (grad_probs - inner) * HEAD_DIM ** (-0.5)).astype(BF16)
            grad_queries = join_heads(dot(grad_raw, keys, 1, 0))
            grad_keys = dot(grad_raw, queries, 0, 0)
            grad_values = dot(weight.astype(BF16), outer, 0, 0)
            grad_qkv[span, lane : lane + LANES] = grad_queries.astype(BF16)
            grad_qkv[span, D + lane : D + lane + LANES] = grad_keys.astype(BF16)
            grad_qkv[span, 2 * D + lane : 2 * D + lane + LANES] = grad_values.astype(BF16)
    sums[3:4, :] = jnp.sum(grad_qkv[:, :D].astype(F32), 0, keepdims=True)
    sums[4:5, :] = jnp.sum(grad_qkv[:, 2 * D :].astype(F32), 0, keepdims=True)
    total = first
    for part, at in enumerate((0, D, VALUE_AT)):
        total = total + dot(grad_qkv[:, part * D : (part + 1) * D], hold[:, at : at + D], 1, 1)
    input_grad[...] = total * keep[...]
    attn_grad(
        start, grad_qkv, context, grad_attn, sums, turn0, turn1, in_sums, quarter, goal,
        (k0, k1, k2, k3), give, made_hold, out_sems,
    )


def attn_grad(
    start, grad_qkv, context, grad_attn, sums, turn0, turn1, in_sums, quarter, goal, keep, give, hold, sems
):
    begin = start[...]
    size = give.shape[1]
    owners = D // size
    hold[:, HALF:WIDE] = jnp.zeros((D, LANES), BF16)
    hold[:, WIDE + HALF : 2 * WIDE] = jnp.zeros((D, LANES), BF16)
    tall = lax.broadcasted_iota(jnp.int32, (4, 2 * size), 0) == quarter[0]
    for owner in range(owners):
        at = owner * size
        lane = (owner % (owners // 2)) * 2 * size
        row = 3 + owner // (owners // 2)
        bias = in_sums[:, owner * 2 * size : (owner + 1) * 2 * size]
        wide = [sums[row : row + 1, lane : lane + 2 * size]]
        narrow = [sums[i : i + 1, at : at + size] for i in (2, 0, 1)]
        narrow.append(turn0[:, at : at + size] + turn1[:, at : at + size])
        narrow = jnp.concatenate(narrow + [jnp.zeros((1, size), F32)], 0)
        narrow = jnp.concatenate([narrow, jnp.zeros_like(narrow)], 1)
        made = jnp.concatenate(
            wide + [narrow, jnp.where(tall, bias, 0.0), jnp.zeros((4, 2 * size), F32)], 0
        )
        hold[at : at + SMALL_ROWS, HALF : HALF + 2 * size] = made.astype(BF16)
    for part, at in enumerate((0, D, VALUE_AT)):
        hold[:, at : at + D] = dot(begin, grad_qkv[:, part * D : (part + 1) * D], 0, 0).astype(BF16)
    hold[:, OUT_AT : OUT_AT + D] = dot(context[...], grad_attn[...], 0, 0).astype(BF16)
    copies = []
    for side in range(2):
        for at in range(16):
            row = pl.multiple_of(goal[1 - side, 0, at] * size, size)
            lane = pl.multiple_of(goal[1 - side, 1, at] * WIDE, LANES)
            copies.append(
                pltpu.make_async_copy(
                    hold.at[pl.ds(row, size), pl.ds(lane, WIDE)],
                    give.at[at] if side == 0 else keep[at // 4].at[at % 4],
                    sems.at[side * 16 + at],
                )
            )
    for copy in copies:
        copy.start()
    for copy in copies:
        copy.wait()


def block_at(i, step):
    return i, 0


def tie(*values):
    return lax.optimization_barrier(values)


def square_gather(column, place):
    one = place.first(column)
    return column, one, place.second(column), place.second(one)


def halves(place, mine):
    mine = mine.astype(BF16)
    other = place.swap_narrow(mine)
    return jnp.where(place.x == 0, jnp.stack([mine, other]), jnp.stack([other, mine]))


def square_sum(blocks, place):
    zero, one, two, three = blocks
    one = sum_of([one, place.second(three)]).astype(BF16)
    zero = sum_of([zero, place.second(two), place.first(one)]).astype(BF16)
    return place.along_z(zero)


def plane_all(piece, place):
    whole = lax.all_gather(piece, "wide", axis=0, tiled=False)
    whole = whole.reshape((place.chips, 2) + piece.shape)
    return by_core(place, whole, 1).reshape(8, -1, piece.shape[-1])


def plane_across(blocks, size, place):
    if place.direct:
        return [place.swap_y(values) for values in blocks[1:]]
    order = jnp.concatenate(blocks).reshape(place.chips, 1, size, blocks[0].shape[-1])
    zeros = jnp.zeros_like(order)
    order = jnp.where(
        place.core == 0, jnp.concatenate([order, zeros], 1), jnp.concatenate([zeros, order], 1)
    )
    order = order.reshape((-1,) + order.shape[2:]).astype(F32)
    return [lax.psum_scatter(order, "wide", scatter_dimension=0, tiled=True)]


def plane_along(near, far, place):
    if not place.direct:
        return far[0]
    return place.along_z(sum_of([near, far[0]]).astype(BF16))


def sum_of(parts):
    total = parts[0].astype(F32)
    for i in range(1, len(parts)):
        total = total + parts[i].astype(F32)
    return total


def by_core(place, values, axis):
    return jnp.where(
        place.core == 0,
        lax.index_in_dim(values, 0, axis, keepdims=False),
        lax.index_in_dim(values, 1, axis, keepdims=False),
    )


def by_narrow(place, values, axis):
    return jnp.where(
        place.x == 0,
        lax.index_in_dim(values, 0, axis, keepdims=False),
        lax.index_in_dim(values, 1, axis, keepdims=False),
    )


def quarter_sum(near, theirs, rows, place):
    got = place.swap_core(theirs)
    near = (near + got[rows:].astype(F32)).astype(BF16)
    return got, place.swap_narrow(near)


def with_small(rows, vectors, owned):
    both = jnp.swapaxes(rows.reshape(owned, 2, HALF), 0, 1)
    qv, ob, g1, b1, ib, db, g2, b2 = vectors
    width = 2 * owned
    narrow = jnp.stack([ob, g1, b1, db, g2, b2])
    narrow = jnp.pad(narrow, ((0, 1), (0, owned)))
    small = jnp.concatenate([qv[None], narrow, ib.reshape(4, width)])
    small = jnp.pad(small, ((0, owned - small.shape[0]), (0, LANES - width)))
    small = jnp.stack([small, jnp.zeros_like(small)])
    return jnp.concatenate([both, small], 2)


def gather_attn(rows, vectors, owned, place):
    full = lax.all_gather(rows, "wide", axis=0, tiled=True)
    parts = [lax.all_gather(v, "wide", axis=0, tiled=True) for v in vectors]
    size = D // 16
    parts = [v.reshape(16, -1) for v in parts]
    ib = parts[4].reshape(2, place.chips, 2, 2, -1).reshape(2, 8, -1, 2, 2, parts[4].size // (place.wide * 4))
    parts[4] = ib.transpose(0, 1, 3, 4, 2, 5).reshape(16, 4 * 2 * size)
    blocks = [
        with_small(full[i * size : (i + 1) * size], [v[i] for v in parts], size) for i in range(16)
    ]
    blocks = jnp.stack(blocks).reshape(8, 2, 2, size, WIDE)
    even, odd = [blocks[:, core].reshape(4, 4, size, WIDE) for core in range(2)]
    mine = jnp.where(place.core == 0, even, odd)
    other = jnp.where(place.core == 0, odd, even)
    return [mine[m] for m in range(4)] + [other[m] for m in range(4)]


def reduce_attn(keep, give, owned, place):
    mine = jnp.stack(keep).reshape(8, 2, D // 16, WIDE)
    other = give.reshape(8, 2, D // 16, WIDE)
    full = jnp.where(place.core == 0, jnp.stack([mine, other], 1), jnp.stack([other, mine], 1))
    full = full.transpose(0, 1, 3, 2, 4).reshape(place.wide, owned, 2, WIDE)
    full = jnp.swapaxes(full, 1, 2).astype(F32)
    full = lax.psum_scatter(full, "wide", scatter_dimension=0, tiled=True)[0]
    return lax.psum(full, "narrow").astype(BF16)


def body(
    hidden_in,
    masked,
    token_ids,
    token_table,
    qkv_weight,
    qv_bias,
    out_weight,
    out_bias,
    norm1_gain,
    norm1_bias,
    ffn_in_weight,
    ffn_in_bias,
    ffn_out_weight,
    ffn_out_bias,
    norm2_gain,
    norm2_bias,
    out_cotangent,
):
    place = Place(lax.axis_size("narrow"), lax.axis_size("wide"))
    wide = place.wide
    chips = place.chips
    owned = qkv_weight.shape[0]
    units = ffn_out_weight.shape[0]
    rows = hidden_in.shape[0]
    seqs = rows // SEQ

    chosen = (masked > 0)[:, None]
    replaced, ffn_in_weight = tie(jnp.take(token_table, token_ids, axis=0), ffn_in_weight)
    start = jnp.where(chosen, replaced, hidden_in)

    attn_come = jnp.concatenate(
        [place.row_spots(place.core, True), place.row_spots(1 - place.core, True)], 1
    )
    in_come = place.plane_spots(False)
    down_come = place.step_spots()
    leave = place.plane_spots(False)
    attn_leave = jnp.stack([place.row_spots(place.core, False), place.row_spots(1 - place.core, False)])
    quarter_at = (place.core * 2 + place.x).reshape(1).astype(jnp.int32)

    small = (qv_bias, out_bias, norm1_gain, norm1_bias, ffn_in_bias, ffn_out_bias, norm2_gain, norm2_bias)
    attn_own = jnp.concatenate([qkv_weight, out_weight], 1)
    half_units = units // 2
    in_blocks = ffn_in_weight.reshape(owned, 2, chips, 2, 2, half_units)
    in_blocks = by_narrow(place, in_blocks, 4)
    in_mine = by_core(place, in_blocks, 3).reshape(owned, FF // 2)
    in_give = by_core(place, jnp.flip(in_blocks, 3), 3).reshape(owned, FF // 2)
    in_got = place.swap_core(in_give)
    in_piece = jnp.where(
        place.core == 0, jnp.concatenate([in_mine, in_got]), jnp.concatenate([in_got, in_mine])
    )
    down_piece = by_narrow(place, ffn_out_weight.reshape(2, half_units, D), 0)
    if place.direct:
        attn_piece = by_narrow(place, with_small(attn_own, small, owned), 0)
        attn_column = place.column_z(attn_piece)
        down_got = place.swap_y(down_piece)
        held = tie(
            *attn_column, down_got, in_piece, start, attn_come, in_come, down_come, leave, attn_leave
        )
        attn_column, held = held[:4], held[4:]
        down_got, in_piece, start, attn_come, in_come, down_come, leave, attn_leave = held
        in_column = place.spread_z(in_piece)
        blocks = [jnp.stack(attn_column)]
        blocks = blocks + [place.first(blocks[0]), place.second(blocks[0])]
        others = [place.swap_core(values) for values in blocks]
        blocks.append(place.second(blocks[1]))
        *held, in_column, down_got = tie(*blocks, *others, in_column, down_got)
        attn_blocks = held + [place.swap_core(held[3])]
        in_first, in_last = in_column[:2], in_column[2:]
        in_weights = [in_first, in_last, place.swap_y(in_first), place.swap_y(in_last)]
        down_weights = place.column_z(jnp.stack([down_piece, down_got]))
    else:
        attn_blocks = gather_attn(attn_own, small, owned, place)
        whole = plane_all(in_piece, place)
        in_weights = [whole[:2], whole[2:4], whole[4:6], whole[6:]]
        whole = plane_all(down_piece, place)
        down_weights = [whole[:2], whole[2:4], whole[4:6], whole[6:]]
    block_rows, quarter = D // 8, FF // 4
    eight = pltpu.SemaphoreType.DMA((8,))
    sixteen = pltpu.SemaphoreType.DMA((16,))
    thirty_two = pltpu.SemaphoreType.DMA((32,))
    in_hold = pltpu.VMEM((D, 2 * quarter), BF16)
    down_hold = pltpu.VMEM((quarter, D), BF16)
    attn_hold = pltpu.VMEM((D, 2 * WIDE), BF16)
    V, A, S, H, K = VECTORS, ANYWHERE, SCALARS, IN_HBM, KEPT

    context, probs, qkv, unit, scale, hidden, vectors, in_shift = call(
        attn_forward_kernel,
        [V] + [H] * 8 + [S, S],
        [
            (K, (rows, D), BF16),
            (K, (seqs, PAIRS, 2 * SEQ, SEQ), F32),
            (K, (rows, 3 * D), BF16),
            (K, (rows, D), F32),
            (K, (rows, 1), F32),
            (V, (rows, D), BF16),
            (K, (8, D), F32),
            (V, (1, 2 * quarter), F32),
        ],
        [attn_hold, thirty_two],
        rows * D * D * 10,
        10 << 20,
        start,
        *attn_blocks,
        attn_come,
        quarter_at,
    )
    if place.direct:
        hidden, in_weights[2], down_weights[1], down_weights[3] = tie(
            hidden, in_weights[2], down_weights[1], down_weights[3]
        )
    hidden_near = place.swap_narrow(hidden)
    hidden_core = place.swap_core(hidden)
    hidden_near, in_weights[3], down_weights[2] = tie(hidden_near, in_weights[3], down_weights[2])
    hidden_far = place.swap_core(hidden_near)
    inputs = (hidden, hidden_near, hidden_core, hidden_far)
    count = rows // SEQ
    part_shapes = [(V, (SEQ, D), F32), (V, (SEQ, D), F32), (V, (2 * SEQ, D), BF16)]
    act, gelu, slope, in_whole, down_whole, *parts = call(
        ffn_kernel,
        [V, V, V, V, S, H, H, H, H, V, S, H, H, H, H],
        [(V, (4 * rows, quarter), BF16)] * 3
        + [(V, (D, 2 * quarter), BF16), (V, (quarter, D), BF16)]
        + part_shapes * count,
        [eight, eight],
        rows * D * FF * 12,
        16 << 20,
        *inputs,
        in_come,
        *in_weights,
        in_shift,
        down_come,
        *down_weights,
    )
    parts = [parts[3 * i : 3 * i + 3] for i in range(count)]
    turned = []
    for i, (part, near, theirs) in enumerate(parts):
        core_got, got = quarter_sum(near, theirs, SEQ, place)
        row = pl.BlockSpec((SEQ, D), functools.partial(block_at, i))
        turned.append(
            call(
                turn_kernel,
                [V, V, V, row, V, row],
                [(K, (SEQ, D), BF16), (K, (SEQ, D), F32), (V, (SEQ, D), BF16), (K, (3, D), F32)],
                [],
                SEQ * D * 30,
                5 << 20,
                part,
                core_got,
                got,
                hidden,
                vectors,
                out_cotangent,
            )
        )
    layer_out = jnp.concatenate([made[0] for made in turned])

    gradients = []
    for made in turned:
        near = place.swap_narrow(made[2])
        gradients += [made[2], near, place.swap_core(made[2]), place.swap_core(near)]
    back, in_sums, part, near, theirs = call(
        back_kernel,
        [V] * 12,
        [
            (V, (4 * rows, 2 * quarter), BF16),
            (K, (1, 2 * quarter), F32),
            (K, (rows, D), F32),
            (V, (rows, D), F32),
            (V, (2 * rows, D), BF16),
        ],
        [],
        rows * D * FF * 8,
        18 << 20,
        *gradients,
        gelu,
        slope,
        down_whole,
        in_whole,
    )
    theirs, act = tie(theirs, act)
    down_blocks = call(
        down_grad_kernel,
        [V] * 9 + [S],
        [(A, (4, block_rows, D), BF16)] * 2,
        [down_hold, eight],
        rows * D * FF * 2,
        6 << 20,
        act,
        *gradients,
        leave,
    )
    core_got = place.swap_core(theirs)
    near, back = tie((near + core_got[rows:].astype(F32)).astype(BF16), back)
    got = place.swap_narrow(near)
    in_blocks = call(
        in_grad_kernel,
        [V] * 5 + [S],
        [(A, (4, block_rows, 2 * quarter), BF16)] * 2,
        [in_hold, eight],
        rows * D * FF * 8,
        18 << 20,
        *inputs,
        back,
        leave,
    )
    in_far = plane_across(in_blocks, 2 * owned, place)
    down_far = plane_across(down_blocks, half_units, place)
    got, *held = tie(got, *down_far, in_blocks[0])
    down_parts = plane_along(down_blocks[0], held[:-1], place)
    adds = [made[1] for made in turned] + [part, core_got, got]
    turn_sums = [made[3] for made in turned]
    keep_rows = jnp.broadcast_to(jnp.where(chosen, 0.0, 1.0), (rows, 1)).astype(F32)
    input_grad, attn_sums, *blocks = call(
        attn_backward_kernel,
        [K, K, K, V, K, K, K, K, V, K, K, K] + [H] * 8 + [S, K, K, K, K, S, S],
        [(K, (rows, D), F32), (V, (5, D), F32)]
        + [(H, (4, D // 16, WIDE), BF16)] * 4
        + [(H, (16, D // 16, WIDE), BF16)],
        [
            attn_hold,
            pltpu.VMEM((rows, D), BF16),
            pltpu.VMEM((rows, D), BF16),
            pltpu.VMEM((rows, 3 * D), BF16),
            attn_hold,
            thirty_two,
            thirty_two,
        ],
        rows * D * D * 20,
        22 << 20,
        *adds,
        unit,
        scale,
        vectors,
        keep_rows,
        context,
        probs,
        qkv,
        *attn_blocks,
        attn_come,
        start,
        *turn_sums,
        in_sums,
        quarter_at,
        attn_leave,
    )
    give, down_parts, *in_far = tie(blocks[4], down_parts, *in_far)
    if place.direct:
        got = place.swap_core(give)
        keep = [sum_of([blocks[m], got[4 * m : 4 * m + 4]]).astype(BF16) for m in range(4)]
        attn_parts = square_sum(keep, place)
    in_sum = sum_of(plane_along(in_blocks[0], in_far, place)).astype(BF16).reshape(2, owned, 2 * quarter)
    mine = jnp.where(place.core == 0, in_sum[0], in_sum[1])
    give = jnp.where(place.core == 0, in_sum[1], in_sum[0])
    got = place.swap_core(give)
    pair = jnp.where(place.core == 0, jnp.stack([mine, got]), jnp.stack([got, mine]))
    in_rows = halves(place, pair).reshape(2, 2, owned, 2, chips, half_units)
    in_rows = in_rows.transpose(2, 3, 4, 1, 0, 5).reshape(owned, 2 * FF).astype(F32)
    down_rows = halves(place, sum_of(down_parts)).reshape(units, D).astype(F32)

    if place.direct:
        attn_half, in_rows, down_rows = tie(sum_of(attn_parts).astype(BF16), in_rows, down_rows)
        attn_sum = halves(place, attn_half)
        lanes = attn_sum[0, :SMALL_ROWS, HALF:].astype(F32)
        s_qv = lanes[0, : 2 * owned]
        s_ob, s_g1, s_b1, s_db, s_g2, s_b2 = [lanes[i, :owned] for i in range(1, 7)]
        s_ib = lanes[BIAS_ROW : BIAS_ROW + 4, : 2 * owned].reshape(-1)
    else:
        attn_sum = reduce_attn(blocks[:4], blocks[4], owned, place)
        turn_sums = sum_of(turn_sums)
        ib_blocks = in_sums.reshape(2, chips, 1, 1, half_units)
        at_core = (jnp.arange(2) == place.core).astype(F32).reshape(1, 1, 2, 1, 1)
        at_narrow = (jnp.arange(2) == place.x).astype(F32).reshape(1, 1, 1, 2, 1)
        sums = [attn_sums[3:5], attn_sums[2], attn_sums[0], attn_sums[1]]
        sums = sums + [ib_blocks * at_core * at_narrow, turn_sums[0], turn_sums[1], turn_sums[2]]
        widths = [v.size // wide for v in sums]
        sums = jnp.concatenate([v.reshape(wide, -1) for v in sums], 1)
        sums = lax.psum(sums, AXES)[lax.axis_index("wide")]
        ends = [sum(widths[: i + 1]) for i in range(len(widths) - 1)]
        s_qv, s_ob, s_g1, s_b1, s_ib, s_db, s_g2, s_b2 = jnp.split(sums, ends)
    attn_rows = attn_sum[..., :HALF].astype(F32)
    full_qkv = jnp.concatenate([attn_rows[0], attn_rows[1, :, :D]], 1)

    return (
        layer_out,
        input_grad,
        full_qkv,
        s_qv,
        attn_rows[1, :, D:],
        s_ob,
        s_g1,
        s_b1,
        in_rows,
        s_ib,
        down_rows,
        s_db,
        s_g2,
        s_b2,
    )


def solution(mesh):
    rows = P(("narrow", "wide"), None)
    marks = P(("narrow", "wide"))
    matrix = P("wide", None)
    vector = P("wide")
    in_specs = (rows, marks, marks, P(), matrix, vector, matrix, vector, vector, vector)
    in_specs = in_specs + (matrix, vector, matrix, vector, vector, vector, rows)
    out_specs = (rows, rows, matrix, vector, matrix, vector, vector, vector)
    out_specs = out_specs + (matrix, vector, matrix, vector, vector, vector)
    return jax.shard_map(body, mesh=mesh, in_specs=in_specs, out_specs=out_specs, check_vma=False)
```

```python
import functools
import math

import jax
import jax.numpy as jnp
from jax import lax
from jax.experimental import pallas as pl
from jax.experimental.pallas import tpu as pltpu
from jax.sharding import PartitionSpec as P

D = 768
HEADS = 12
HEAD_DIM = 64
FF = 3072
SEQ = 128
EPS = 1e-12
AXES = ("narrow", "wide")
F32 = jnp.float32
BF16 = jnp.bfloat16


def alibi_slopes(count):
    power = 2 ** int(math.floor(math.log2(count)))
    values = [2.0 ** (-8.0 * (number + 1) / power) for number in range(power)]
    extra = [2.0 ** (-8.0 * (number + 1) / (2 * power)) for number in range(2 * power)]
    values = values + extra[0::2][: count - power]
    return values


class Place:
    def __init__(self, narrow, wide):
        self.narrow = narrow
        self.wide = wide
        self.chips = wide // 2
        self.direct = narrow == 2 and wide == 16
        self.ny = 2 if self.direct else 1
        self.nz = self.chips // self.ny
        across = lax.axis_index("narrow")
        along = lax.axis_index("wide")
        self.x = across
        self.core = along % 2
        self.chip = along // 2
        self.y = self.chip % self.ny
        self.z = self.chip // self.ny

    def move(self, values, target):
        pairs = []
        for x in range(self.narrow):
            for z in range(self.nz):
                for y in range(self.ny):
                    for c in range(2):
                        tx, tz, ty, tc = target(x, z, y, c)
                        source = ((x * self.nz + z) * self.ny + y) * 2 + c
                        goal = ((tx * self.nz + tz) * self.ny + ty) * 2 + tc
                        pairs.append((source, goal))
        return lax.ppermute(values, AXES, pairs)

    def swap_core(self, values):
        return self.move(values, lambda x, z, y, c: (x, z, y, 1 - c))

    def swap_narrow(self, values):
        return self.move(values, lambda x, z, y, c: (1 - x, z, y, c))

    def swap_y(self, values):
        return self.move(values, lambda x, z, y, c: (x, z, 1 - y, c))

    def first(self, values):
        return self.move(
            values, lambda x, z, y, c: (1 - x, z, y, c) if c == 0 else (x, z, 1 - y, c)
        )

    def second(self, values):
        return self.move(
            values, lambda x, z, y, c: (x, z, 1 - y, c) if c == 0 else (1 - x, z, y, c)
        )

    def diagonal(self, values):
        return self.move(values, lambda x, z, y, c: (1 - x, z, 1 - y, c))

    def along_z(self, values):
        lines = [
            [(z * self.ny + y) * 2 + c for z in range(self.nz)] for y in range(self.ny) for c in range(2)
        ]
        return lax.all_to_all(
            values, "wide", split_axis=0, concat_axis=0, axis_index_groups=lines, tiled=True
        )

    def column_z(self, values):
        column = [values]
        for step in range(1, self.nz):
            column.append(
                self.move(values, lambda x, z, y, c: (x, (z + step) % self.nz, y, c))
            )
        return column

    def spread_z(self, values):
        return self.along_z(jnp.broadcast_to(values[None], (self.nz,) + values.shape))

    def spots(self, core, steps):
        if not self.direct:
            at = jnp.arange(16, dtype=jnp.int32)
            return at // 2, at % 2
        m = jnp.arange(16) // 4
        z = (self.z - jnp.arange(16)) % 4 if steps else jnp.arange(16) % 4
        on_first = (m == 1) | (m == 3)
        on_second = (m == 2) | (m == 3)
        flip_x = jnp.where(core == 0, on_first, on_second).astype(jnp.int32)
        flip_y = jnp.where(core == 0, on_second, on_first).astype(jnp.int32)
        y = jnp.bitwise_xor(self.y, flip_y)
        x = jnp.bitwise_xor(self.x, flip_x)
        return (z * self.ny + y).astype(jnp.int32), x.astype(jnp.int32)

    def plane_spots(self, y_first):
        if not self.direct:
            return jnp.arange(8, dtype=jnp.int32)
        at = jnp.arange(8)
        flip, z = (at % 2, at // 2) if y_first else (at // 4, at % 4)
        return (z * self.ny + jnp.bitwise_xor(self.y, flip)).astype(jnp.int32)

    def row_spots(self, core, steps):
        chip, half = self.spots(core, steps)
        return jnp.stack([chip * 2 + core, half])


ANYWHERE = pl.BlockSpec(memory_space=pl.ANY)
IN_HBM = pl.BlockSpec(memory_space=pltpu.HBM)
KEPT = pl.BlockSpec(memory_space=pltpu.VMEM)
SCALARS = pl.BlockSpec(memory_space=pltpu.SMEM)
VECTORS = pl.BlockSpec(memory_space=pltpu.VMEM)
PAIRS = HEADS // 2
HALF = 2 * D
LANES = 128
WIDE = HALF + LANES


def dot(a, b, da, db):
    return lax.dot_general(a, b, (((da,), (db,)), ((), ())), preferred_element_type=F32)


BIG, SMALL = 36, 16


def call(kernel, ins, outs, scratch, flops, moved, *operands):
    operands = [
        pltpu.with_memory_space_constraint(operand, pltpu.HBM) if spec is IN_HBM or spec is KEPT else operand
        for spec, operand in zip(ins, operands, strict=True)
    ]
    windows = any(spec.block_shape is not None for spec in ins)
    return pl.pallas_call(
        kernel,
        grid=(1,) if windows else (),
        in_specs=ins,
        out_specs=[spec for spec, _, _ in outs],
        out_shape=[
            pltpu.HBM(shape, dtype)
            if spec is IN_HBM or spec is KEPT
            else jax.ShapeDtypeStruct(shape, dtype)
            for spec, shape, dtype in outs
        ],
        scratch_shapes=scratch,
        cost_estimate=pl.CostEstimate(flops=flops, transcendentals=0, bytes_accessed=moved),
        compiler_params=pltpu.CompilerParams(vmem_limit_bytes=(BIG if kernel is attn_backward_kernel else SMALL) * 1024 * 1024),
    )(*operands)


def normed(values):
    average = jnp.mean(values, -1, keepdims=True)
    center = values - average
    variance = jnp.mean(center * center, -1, keepdims=True)
    scale = lax.rsqrt(variance + EPS)
    return center * scale, scale


def norm_back(grad, unit, scale, gain):
    e = grad * gain
    return scale * (
        e - jnp.mean(e, -1, keepdims=True) - unit * jnp.mean(e * unit, -1, keepdims=True)
    )


def split_heads(pair):
    low = lax.broadcasted_iota(jnp.int32, pair.shape, 1) < HEAD_DIM
    zero = jnp.zeros_like(pair)
    return jnp.concatenate([jnp.where(low, pair, zero), jnp.where(low, zero, pair)], 0)


def join_heads(stacked):
    rows = stacked.shape[0] // 2
    low = lax.broadcasted_iota(jnp.int32, (rows, LANES), 1) < HEAD_DIM
    return jnp.where(low, stacked[:rows], stacked[rows:])


def block_list(arrays):
    blocks = []
    for array in arrays:
        for i in range(array.shape[0]):
            if len(array.shape) == 4:
                blocks += [array.at[i, j] for j in range(array.shape[1])]
            else:
                blocks.append(array.at[i])
    return blocks


def fetch_rows(sources, spots, hold, sems):
    copies = []
    for at, block in enumerate(block_list(sources)):
        size = block.shape[0]
        to = pl.multiple_of(spots[at] * size, size)
        copies.append(pltpu.make_async_copy(block, hold.at[pl.ds(to, size)], sems.at[at]))
    for copy in copies:
        copy.start()
    return copies


def emit_rows(source, outs, spots, sems):
    copies = []
    for at, block in enumerate(block_list(outs)):
        size = block.shape[0]
        start = pl.multiple_of(spots[at] * size, size)
        copies.append(pltpu.make_async_copy(source.at[pl.ds(start, size)], block, sems.at[at]))
    for copy in copies:
        copy.start()
    for copy in copies:
        copy.wait()


def fetch_attn(blocks, spots, hold, sems):
    copies = []
    for at, block in enumerate(block_list(blocks)):
        size = block.shape[0]
        row = pl.multiple_of(spots[0, at] * size, size)
        lane = pl.multiple_of(spots[1, at] * WIDE, LANES)
        copies.append(
            pltpu.make_async_copy(
                block, hold.at[pl.ds(row, size), pl.ds(lane, WIDE)], sems.at[at]
            )
        )
    for copy in copies:
        copy.start()
    return copies


SMALL_ROWS = 16
BIAS_ROW = 8


def read_vectors(hold, quarter, vectors, in_shift):
    owners = 16
    size = D // owners
    tall = lax.broadcasted_iota(jnp.int32, (4, 2 * size), 0) == quarter[0]
    for owner in range(owners):
        at = owner * size
        lane = (owner % (owners // 2)) * 2 * size
        row = owner // (owners // 2)
        region = hold[at : at + SMALL_ROWS, HALF:WIDE].astype(F32)
        vectors[row : row + 1, lane : lane + 2 * size] = region[0:1, : 2 * size]
        vectors[2:8, at : at + size] = region[1:7, :size]
        bias = jnp.where(tall, region[BIAS_ROW : BIAS_ROW + 4, : 2 * size], 0.0)
        in_shift[:, owner * 2 * size : (owner + 1) * 2 * size] = jnp.sum(bias, 0, keepdims=True)


VALUE_AT = WIDE
OUT_AT = WIDE + D


def attn_forward_kernel(
    start, b0, b1, b2, b3, b4, b5, b6, b7, spots, quarter,
    context, probs, qkv, unit, scale, hidden, vectors, in_shift, hold, sems,
):
    for copy in fetch_attn((b0, b1, b2, b3, b4, b5, b6, b7), spots, hold, sems):
        copy.wait()
    read_vectors(hold, quarter, vectors, in_shift)
    rows = start.shape[0]
    begin = start[...]
    for part, at in enumerate((0, D, VALUE_AT)):
        made = dot(begin, hold[:, at : at + D], 1, 0)
        if part != 1:
            made = made + vectors[part // 2 : part // 2 + 1, :]
        qkv[:, part * D : (part + 1) * D] = made.astype(BF16)
    distance = jnp.abs(
        lax.broadcasted_iota(jnp.int32, (SEQ, SEQ), 0) - lax.broadcasted_iota(jnp.int32, (SEQ, SEQ), 1)
    ).astype(F32)
    slopes = alibi_slopes(HEADS)
    for s in range(rows // SEQ):
        span = slice(s * SEQ, (s + 1) * SEQ)
        for pair in range(PAIRS):
            lane = pair * LANES
            queries = qkv[span, lane : lane + LANES]
            keys = qkv[span, D + lane : D + lane + LANES]
            values = qkv[span, 2 * D + lane : 2 * D + lane + LANES]
            raw = dot(split_heads(queries), keys, 1, 1)
            fall = jnp.concatenate([distance * slopes[2 * pair], distance * slopes[2 * pair + 1]], 0)
            scores = raw * HEAD_DIM ** (-0.5) - fall
            expo = jnp.exp(scores - jnp.max(scores, -1, keepdims=True))
            made = expo / jnp.sum(expo, -1, keepdims=True)
            probs[s, pair] = made
            joined = join_heads(dot(made.astype(BF16), values, 1, 0))
            context[span, lane : lane + LANES] = joined.astype(BF16)
    first_sum = begin.astype(F32) + dot(context[...], hold[:, OUT_AT : OUT_AT + D], 1, 0)
    made, factor = normed(first_sum + vectors[2:3, :])
    unit[...] = made
    scale[...] = factor
    hidden[...] = (made * vectors[3:4, :] + vectors[4:5, :]).astype(BF16)


def by_sequence(values):
    return jnp.concatenate(
        [v[i : i + SEQ, :] for i in range(0, values[0].shape[0], SEQ) for v in values], 0
    )


def ffn_kernel(
    h0, h1, h2, h3, spots, w0, w1, w2, w3, shift, down_spots, down,
    act, gelu_out, slope_out, hold, down_hold, part0, near0, theirs0, part1, near1, theirs1,
    sems, down_sems,
):
    copies = fetch_rows((w0, w1, w2, w3), spots, hold, sems)
    down_copies = fetch_rows((down,), down_spots, down_hold, down_sems)
    both = by_sequence((h0, h1, h2, h3))
    for copy in copies:
        copy.wait()
    width = act.shape[1]
    block = 256
    for at in range(0, width, block):
        cols = slice(at, at + block)
        more = slice(width + at, width + at + block)
        gate = dot(both, hold[:, cols], 1, 0) + shift[:, cols]
        up = dot(both, hold[:, more], 1, 0) + shift[:, more]
        cdf = 0.5 + 0.5 * lax.erf(gate * (0.5**0.5))
        gelu = gate * cdf
        slope = cdf + gate * jnp.exp(-0.5 * gate * gate) * ((2 * math.pi) ** -0.5)
        act[:, cols] = (gelu * up).astype(BF16)
        gelu_out[:, cols] = gelu.astype(BF16)
        slope_out[:, cols] = (slope * up).astype(BF16)
    for copy in down_copies:
        copy.wait()
    for i, (part, near, theirs) in enumerate(((part0, near0, theirs0), (part1, near1, theirs1))):
        made = dot(act[i * 4 * SEQ : (i + 1) * 4 * SEQ, :], down_hold[...], 1, 0)
        part[...] = made[:SEQ]
        near[...] = made[SEQ : 2 * SEQ]
        theirs[...] = made[2 * SEQ :].astype(BF16)


def turn_kernel(mine, core, got, hidden, vectors, cotangent, layer_out, second, branch, sums):
    part = mine[...] + core[: mine.shape[0], :].astype(F32) + got[...].astype(F32)
    total = hidden[...].astype(F32) + (part + vectors[5:6, :])
    unit, scale = normed(total)
    layer_out[...] = (unit * vectors[6:7, :] + vectors[7:8, :]).astype(BF16)
    grad = cotangent[...].astype(F32)
    back = norm_back(grad, unit, scale, vectors[6:7, :])
    second[...] = back
    low = back.astype(BF16)
    branch[...] = low
    sums[0:1, :] = jnp.sum(low.astype(F32), 0, keepdims=True)
    sums[1:2, :] = jnp.sum(grad * unit, 0, keepdims=True)
    sums[2:3, :] = jnp.sum(grad, 0, keepdims=True)


def down_grad_kernel(act, g0, g1, g2, g3, g4, g5, g6, g7, spots, p0, p1, hold, sems):
    both = jnp.concatenate([g[...] for g in (g0, g1, g2, g3, g4, g5, g6, g7)], 0)
    hold[...] = dot(act[...], both, 0, 0).astype(BF16)
    emit_rows(hold, (p0, p1), spots, sems)


def back_kernel(
    g0, g1, g2, g3, g4, g5, g6, g7, gelu, slope, hold, in_hold, back, sums, part, near, other
):
    both = jnp.concatenate([g[...] for g in (g0, g1, g2, g3, g4, g5, g6, g7)], 0)
    width = gelu.shape[1]
    block = 256
    for at in range(0, width, block):
        cols = slice(at, at + block)
        more = slice(width + at, width + at + block)
        grad = dot(both, hold[cols, :], 1, 1)
        for cut, factor in ((cols, slope), (more, gelu)):
            low = (grad * factor[:, cols].astype(F32)).astype(BF16)
            back[:, cut] = low
            sums[:, cut] = jnp.sum(low.astype(F32), 0, keepdims=True)
    made = dot(back[...], in_hold[...], 1, 1)
    count = part.shape[0] // SEQ
    for i in range(count):
        at = 4 * SEQ * i
        here, there = slice(i * SEQ, (i + 1) * SEQ), slice((count + i) * SEQ, (count + i + 1) * SEQ)
        part[here, :] = made[at : at + SEQ]
        near[here, :] = made[at + SEQ : at + 2 * SEQ]
        other[here, :] = made[at + 2 * SEQ : at + 3 * SEQ].astype(BF16)
        other[there, :] = made[at + 3 * SEQ : at + 4 * SEQ].astype(BF16)


def in_grad_kernel(h0, h1, h2, h3, back, goal, p0, p1, made, out_sems):
    made[...] = dot(by_sequence((h0, h1, h2, h3)), back[...], 0, 0).astype(BF16)
    emit_rows(made, (p0, p1), goal, out_sems)


def attn_backward_kernel(
    s0, s1, mine, core, near, unit, scale, vectors, keep, context, probs, qkv,
    b0, b1, b2, b3, b4, b5, b6, b7, spots, start, turn0, turn1, in_sums, quarter, goal,
    input_grad, sums, k0, k1, k2, k3, give,
    hold, grad_context, grad_attn, grad_qkv, made_hold, sems, out_sems,
):
    copies = fetch_attn((b0, b1, b2, b3, b4, b5, b6, b7), spots, hold, sems)
    rows = unit.shape[0]
    grad = jnp.concatenate([s0[...], s1[...]], 0) + mine[...]
    grad = grad + core[:rows, :].astype(F32) + near[...].astype(F32)
    made = unit[...]
    sums[0:1, :] = jnp.sum(grad * made, 0, keepdims=True)
    sums[1:2, :] = jnp.sum(grad, 0, keepdims=True)
    first = norm_back(grad, made, scale[...], vectors[3:4, :])
    low = first.astype(BF16)
    grad_attn[...] = low
    sums[2:3, :] = jnp.sum(low.astype(F32), 0, keepdims=True)
    for copy in copies:
        copy.wait()
    grad_context[...] = dot(low, hold[:, OUT_AT : OUT_AT + D], 1, 1).astype(BF16)
    for s in range(rows // SEQ):
        span = slice(s * SEQ, (s + 1) * SEQ)
        for pair in range(PAIRS):
            lane = pair * LANES
            queries = split_heads(qkv[span, lane : lane + LANES])
            keys = qkv[span, D + lane : D + lane + LANES]
            values = qkv[span, 2 * D + lane : 2 * D + lane + LANES]
            outer = split_heads(grad_context[span, lane : lane + LANES])
            weight = probs[s, pair]
            grad_probs = dot(outer, values, 1, 1)
            inner = jnp.sum(weight * grad_probs, -1, keepdims=True)
            grad_raw = (weight * (grad_probs - inner) * HEAD_DIM ** (-0.5)).astype(BF16)
            grad_queries = join_heads(dot(grad_raw, keys, 1, 0))
            grad_keys = dot(grad_raw, queries, 0, 0)
            grad_values = dot(weight.astype(BF16), outer, 0, 0)
            grad_qkv[span, lane : lane + LANES] = grad_queries.astype(BF16)
            grad_qkv[span, D + lane : D + lane + LANES] = grad_keys.astype(BF16)
            grad_qkv[span, 2 * D + lane : 2 * D + lane + LANES] = grad_values.astype(BF16)
    sums[3:4, :] = jnp.sum(grad_qkv[:, :D].astype(F32), 0, keepdims=True)
    sums[4:5, :] = jnp.sum(grad_qkv[:, 2 * D :].astype(F32), 0, keepdims=True)
    total = first
    for part, at in enumerate((0, D, VALUE_AT)):
        total = total + dot(grad_qkv[:, part * D : (part + 1) * D], hold[:, at : at + D], 1, 1)
    input_grad[...] = total * keep[...]
    attn_grad(
        start, grad_qkv, context, grad_attn, sums, turn0, turn1, in_sums, quarter, goal,
        (k0, k1, k2, k3), give, made_hold, out_sems,
    )


def attn_grad(
    start, grad_qkv, context, grad_attn, sums, turn0, turn1, in_sums, quarter, goal, keep, give, hold, sems
):
    begin = start[...]
    size = give.shape[1]
    owners = D // size
    hold[:, HALF:WIDE] = jnp.zeros((D, LANES), BF16)
    hold[:, WIDE + HALF : 2 * WIDE] = jnp.zeros((D, LANES), BF16)
    tall = lax.broadcasted_iota(jnp.int32, (4, 2 * size), 0) == quarter[0]
    for owner in range(owners):
        at = owner * size
        lane = (owner % (owners // 2)) * 2 * size
        row = 3 + owner // (owners // 2)
        bias = in_sums[:, owner * 2 * size : (owner + 1) * 2 * size]
        wide = [sums[row : row + 1, lane : lane + 2 * size]]
        narrow = [sums[i : i + 1, at : at + size] for i in (2, 0, 1)]
        narrow.append(turn0[:, at : at + size] + turn1[:, at : at + size])
        narrow = jnp.concatenate(narrow + [jnp.zeros((1, size), F32)], 0)
        narrow = jnp.concatenate([narrow, jnp.zeros_like(narrow)], 1)
        made = jnp.concatenate(
            wide + [narrow, jnp.where(tall, bias, 0.0), jnp.zeros((4, 2 * size), F32)], 0
        )
        hold[at : at + SMALL_ROWS, HALF : HALF + 2 * size] = made.astype(BF16)
    for part, at in enumerate((0, D, VALUE_AT)):
        hold[:, at : at + D] = dot(begin, grad_qkv[:, part * D : (part + 1) * D], 0, 0).astype(BF16)
    hold[:, OUT_AT : OUT_AT + D] = dot(context[...], grad_attn[...], 0, 0).astype(BF16)
    copies = []
    for side in range(2):
        for at in range(16):
            row = pl.multiple_of(goal[1 - side, 0, at] * size, size)
            lane = pl.multiple_of(goal[1 - side, 1, at] * WIDE, LANES)
            copies.append(
                pltpu.make_async_copy(
                    hold.at[pl.ds(row, size), pl.ds(lane, WIDE)],
                    give.at[at] if side == 0 else keep[at // 4].at[at % 4],
                    sems.at[side * 16 + at],
                )
            )
    for copy in copies:
        copy.start()
    for copy in copies:
        copy.wait()


def block_at(i, step):
    return i, 0


def tie(*values):
    return lax.optimization_barrier(values)


def square_gather(column, place):
    one = place.first(column)
    return column, one, place.second(column), place.second(one)


def halves(place, mine):
    mine = mine.astype(BF16)
    other = place.swap_narrow(mine)
    return jnp.where(place.x == 0, jnp.stack([mine, other]), jnp.stack([other, mine]))


def square_sum(blocks, place):
    zero, one, two, three = blocks
    one = sum_of([one, place.second(three)]).astype(BF16)
    zero = sum_of([zero, place.second(two), place.first(one)]).astype(BF16)
    return place.along_z(zero)


def plane_all(piece, place):
    whole = lax.all_gather(piece, "wide", axis=0, tiled=False)
    whole = whole.reshape((place.chips, 2) + piece.shape)
    return by_core(place, whole, 1).reshape(8, -1, piece.shape[-1])


def plane_across(blocks, size, place):
    if place.direct:
        return [place.swap_y(values) for values in blocks[1:]]
    order = jnp.concatenate(blocks).reshape(place.chips, 1, size, blocks[0].shape[-1])
    zeros = jnp.zeros_like(order)
    order = jnp.where(
        place.core == 0, jnp.concatenate([order, zeros], 1), jnp.concatenate([zeros, order], 1)
    )
    order = order.reshape((-1,) + order.shape[2:]).astype(F32)
    return [lax.psum_scatter(order, "wide", scatter_dimension=0, tiled=True)]


def plane_along(near, far, place):
    if not place.direct:
        return far[0]
    return place.along_z(sum_of([near, far[0]]).astype(BF16))


def sum_of(parts):
    total = parts[0].astype(F32)
    for i in range(1, len(parts)):
        total = total + parts[i].astype(F32)
    return total


def by_core(place, values, axis):
    return jnp.where(
        place.core == 0,
        lax.index_in_dim(values, 0, axis, keepdims=False),
        lax.index_in_dim(values, 1, axis, keepdims=False),
    )


def by_narrow(place, values, axis):
    return jnp.where(
        place.x == 0,
        lax.index_in_dim(values, 0, axis, keepdims=False),
        lax.index_in_dim(values, 1, axis, keepdims=False),
    )


def quarter_sum(near, theirs, rows, place):
    got = place.swap_core(theirs)
    near = (near + got[rows:].astype(F32)).astype(BF16)
    return got, place.swap_narrow(near)


def with_small(rows, vectors, owned):
    both = jnp.swapaxes(rows.reshape(owned, 2, HALF), 0, 1)
    qv, ob, g1, b1, ib, db, g2, b2 = vectors
    width = 2 * owned
    narrow = jnp.stack([ob, g1, b1, db, g2, b2])
    narrow = jnp.pad(narrow, ((0, 1), (0, owned)))
    small = jnp.concatenate([qv[None], narrow, ib.reshape(4, width)])
    small = jnp.pad(small, ((0, owned - small.shape[0]), (0, LANES - width)))
    small = jnp.stack([small, jnp.zeros_like(small)])
    return jnp.concatenate([both, small], 2)


def gather_attn(rows, vectors, owned, place):
    full = lax.all_gather(rows, "wide", axis=0, tiled=True)
    parts = [lax.all_gather(v, "wide", axis=0, tiled=True) for v in vectors]
    size = D // 16
    parts = [v.reshape(16, -1) for v in parts]
    ib = parts[4].reshape(2, place.chips, 2, 2, -1).reshape(2, 8, -1, 2, 2, parts[4].size // (place.wide * 4))
    parts[4] = ib.transpose(0, 1, 3, 4, 2, 5).reshape(16, 4 * 2 * size)
    blocks = [
        with_small(full[i * size : (i + 1) * size], [v[i] for v in parts], size) for i in range(16)
    ]
    blocks = jnp.stack(blocks).reshape(8, 2, 2, size, WIDE)
    even, odd = [blocks[:, core].reshape(4, 4, size, WIDE) for core in range(2)]
    mine = jnp.where(place.core == 0, even, odd)
    other = jnp.where(place.core == 0, odd, even)
    return [mine[m] for m in range(4)] + [other[m] for m in range(4)]


def reduce_attn(keep, give, owned, place):
    mine = jnp.stack(keep).reshape(8, 2, D // 16, WIDE)
    other = give.reshape(8, 2, D // 16, WIDE)
    full = jnp.where(place.core == 0, jnp.stack([mine, other], 1), jnp.stack([other, mine], 1))
    full = full.transpose(0, 1, 3, 2, 4).reshape(place.wide, owned, 2, WIDE)
    full = jnp.swapaxes(full, 1, 2).astype(F32)
    full = lax.psum_scatter(full, "wide", scatter_dimension=0, tiled=True)[0]
    return lax.psum(full, "narrow").astype(BF16)


def body(
    hidden_in,
    masked,
    token_ids,
    token_table,
    qkv_weight,
    qv_bias,
    out_weight,
    out_bias,
    norm1_gain,
    norm1_bias,
    ffn_in_weight,
    ffn_in_bias,
    ffn_out_weight,
    ffn_out_bias,
    norm2_gain,
    norm2_bias,
    out_cotangent,
):
    place = Place(lax.axis_size("narrow"), lax.axis_size("wide"))
    wide = place.wide
    chips = place.chips
    owned = qkv_weight.shape[0]
    units = ffn_out_weight.shape[0]
    rows = hidden_in.shape[0]
    seqs = rows // SEQ

    chosen = (masked > 0)[:, None]
    replaced, ffn_in_weight = tie(jnp.take(token_table, token_ids, axis=0), ffn_in_weight)
    start = jnp.where(chosen, replaced, hidden_in)

    attn_come = jnp.concatenate(
        [place.row_spots(place.core, True), place.row_spots(1 - place.core, True)], 1
    )
    in_come = place.plane_spots(False)
    down_come = place.plane_spots(True)
    leave = place.plane_spots(False)
    attn_leave = jnp.stack([place.row_spots(place.core, False), place.row_spots(1 - place.core, False)])
    quarter_at = (place.core * 2 + place.x).reshape(1).astype(jnp.int32)

    small = (qv_bias, out_bias, norm1_gain, norm1_bias, ffn_in_bias, ffn_out_bias, norm2_gain, norm2_bias)
    attn_own = jnp.concatenate([qkv_weight, out_weight], 1)
    half_units = units // 2
    in_blocks = ffn_in_weight.reshape(owned, 2, chips, 2, 2, half_units)
    in_blocks = by_narrow(place, in_blocks, 4)
    in_mine = by_core(place, in_blocks, 3).reshape(owned, FF // 2)
    in_give = by_core(place, jnp.flip(in_blocks, 3), 3).reshape(owned, FF // 2)
    in_got = place.swap_core(in_give)
    in_piece = jnp.where(
        place.core == 0, jnp.concatenate([in_mine, in_got]), jnp.concatenate([in_got, in_mine])
    )
    down_piece = by_narrow(place, ffn_out_weight.reshape(2, half_units, D), 0)
    if place.direct:
        attn_piece = by_narrow(place, with_small(attn_own, small, owned), 0)
        attn_column = place.column_z(attn_piece)
        down_got = place.swap_y(down_piece)
        held = tie(
            *attn_column, down_got, in_piece, start, attn_come, in_come, down_come, leave, attn_leave
        )
        attn_column, held = held[:4], held[4:]
        down_got, in_piece, start, attn_come, in_come, down_come, leave, attn_leave = held
        in_column = place.spread_z(in_piece)
        blocks = [jnp.stack(attn_column)]
        blocks = blocks + [place.first(blocks[0]), place.second(blocks[0])]
        others = [place.swap_core(values) for values in blocks]
        blocks.append(place.second(blocks[1]))
        *held, in_column, down_got = tie(*blocks, *others, in_column, down_got)
        attn_blocks = held + [place.swap_core(held[3])]
        in_first, in_last = in_column[:2], in_column[2:]
        in_weights = [in_first, in_last, place.swap_y(in_first), place.swap_y(in_last)]
        down_weights = place.spread_z(jnp.stack([down_piece, down_got]))
    else:
        attn_blocks = gather_attn(attn_own, small, owned, place)
        whole = plane_all(in_piece, place)
        in_weights = [whole[:2], whole[2:4], whole[4:6], whole[6:]]
        whole = plane_all(down_piece, place)
        down_weights = whole.reshape(4, 2, -1, D)
    block_rows, quarter = D // 8, FF // 4
    eight = pltpu.SemaphoreType.DMA((8,))
    sixteen = pltpu.SemaphoreType.DMA((16,))
    thirty_two = pltpu.SemaphoreType.DMA((32,))
    in_hold = pltpu.VMEM((D, 2 * quarter), BF16)
    down_hold = pltpu.VMEM((quarter, D), BF16)
    attn_hold = pltpu.VMEM((D, 2 * WIDE), BF16)
    V, A, S, H, K = VECTORS, ANYWHERE, SCALARS, IN_HBM, KEPT

    context, probs, qkv, unit, scale, hidden, vectors, in_shift = call(
        attn_forward_kernel,
        [V] + [H] * 8 + [S, S],
        [
            (K, (rows, D), BF16),
            (K, (seqs, PAIRS, 2 * SEQ, SEQ), F32),
            (K, (rows, 3 * D), BF16),
            (K, (rows, D), F32),
            (K, (rows, 1), F32),
            (V, (rows, D), BF16),
            (K, (8, D), F32),
            (V, (1, 2 * quarter), F32),
        ],
        [attn_hold, thirty_two],
        rows * D * D * 10,
        10 << 20,
        start,
        *attn_blocks,
        attn_come,
        quarter_at,
    )
    hidden, in_weights[2] = tie(hidden, in_weights[2])
    hidden_near = place.swap_narrow(hidden)
    hidden_core = place.swap_core(hidden)
    hidden_near, in_weights[3] = tie(hidden_near, in_weights[3])
    hidden_far = place.swap_core(hidden_near)
    hidden_far, down_weights = tie(hidden_far, down_weights)
    inputs = (hidden, hidden_near, hidden_core, hidden_far)
    count = rows // SEQ
    part_shapes = [(V, (SEQ, D), F32), (V, (SEQ, D), F32), (V, (2 * SEQ, D), BF16)]
    act, gelu, slope, in_whole, down_whole, *parts = call(
        ffn_kernel,
        [V, V, V, V, S, H, H, H, H, V, S, H],
        [(V, (4 * rows, quarter), BF16)] * 3
        + [(V, (D, 2 * quarter), BF16), (V, (quarter, D), BF16)]
        + part_shapes * count,
        [eight, eight],
        rows * D * FF * 12,
        16 << 20,
        *inputs,
        in_come,
        *in_weights,
        in_shift,
        down_come,
        down_weights,
    )
    parts = [parts[3 * i : 3 * i + 3] for i in range(count)]
    turned = []
    for i, (part, near, theirs) in enumerate(parts):
        core_got, got = quarter_sum(near, theirs, SEQ, place)
        row = pl.BlockSpec((SEQ, D), functools.partial(block_at, i))
        turned.append(
            call(
                turn_kernel,
                [V, V, V, row, V, row],
                [(K, (SEQ, D), BF16), (K, (SEQ, D), F32), (V, (SEQ, D), BF16), (K, (3, D), F32)],
                [],
                SEQ * D * 30,
                5 << 20,
                part,
                core_got,
                got,
                hidden,
                vectors,
                out_cotangent,
            )
        )
    layer_out = jnp.concatenate([made[0] for made in turned])

    gradients = []
    for made in turned:
        near = place.swap_narrow(made[2])
        gradients += [made[2], near, place.swap_core(made[2]), place.swap_core(near)]
    down_blocks = call(
        down_grad_kernel,
        [V] * 9 + [S],
        [(A, (4, block_rows, D), BF16)] * 2,
        [down_hold, eight],
        rows * D * FF * 2,
        6 << 20,
        act,
        *gradients,
        leave,
    )
    gelu, *down_blocks = tie(gelu, *down_blocks)
    back, in_sums, part, near, theirs = call(
        back_kernel,
        [V] * 12,
        [
            (V, (4 * rows, 2 * quarter), BF16),
            (K, (1, 2 * quarter), F32),
            (K, (rows, D), F32),
            (V, (rows, D), F32),
            (V, (2 * rows, D), BF16),
        ],
        [],
        rows * D * FF * 8,
        18 << 20,
        *gradients,
        gelu,
        slope,
        down_whole,
        in_whole,
    )
    core_got = place.swap_core(theirs)
    near, back = tie((near + core_got[rows:].astype(F32)).astype(BF16), back)
    got = place.swap_narrow(near)
    in_blocks = call(
        in_grad_kernel,
        [V] * 5 + [S],
        [(A, (4, block_rows, 2 * quarter), BF16)] * 2,
        [in_hold, eight],
        rows * D * FF * 8,
        18 << 20,
        *inputs,
        back,
        leave,
    )
    in_far = plane_across(in_blocks, 2 * owned, place)
    down_far = plane_across(down_blocks, half_units, place)
    got, *held = tie(got, *down_far, in_blocks[0])
    down_parts = plane_along(down_blocks[0], held[:-1], place)
    adds = [made[1] for made in turned] + [part, core_got, got]
    turn_sums = [made[3] for made in turned]
    keep_rows = jnp.broadcast_to(jnp.where(chosen, 0.0, 1.0), (rows, 1)).astype(F32)
    input_grad, attn_sums, *blocks = call(
        attn_backward_kernel,
        [K, K, K, V, K, K, K, K, V, K, K, K] + [H] * 8 + [S, K, K, K, K, S, S],
        [(K, (rows, D), F32), (V, (5, D), F32)]
        + [(H, (4, D // 16, WIDE), BF16)] * 4
        + [(H, (16, D // 16, WIDE), BF16)],
        [
            attn_hold,
            pltpu.VMEM((rows, D), BF16),
            pltpu.VMEM((rows, D), BF16),
            pltpu.VMEM((rows, 3 * D), BF16),
            attn_hold,
            thirty_two,
            thirty_two,
        ],
        rows * D * D * 20,
        22 << 20,
        *adds,
        unit,
        scale,
        vectors,
        keep_rows,
        context,
        probs,
        qkv,
        *attn_blocks,
        attn_come,
        start,
        *turn_sums,
        in_sums,
        quarter_at,
        attn_leave,
    )
    give, down_parts, *in_far = tie(blocks[4], down_parts, *in_far)
    if place.direct:
        got = place.swap_core(give)
        keep = [sum_of([blocks[m], got[4 * m : 4 * m + 4]]).astype(BF16) for m in range(4)]
        attn_parts = square_sum(keep, place)
    in_sum = sum_of(plane_along(in_blocks[0], in_far, place)).astype(BF16).reshape(2, owned, 2 * quarter)
    mine = jnp.where(place.core == 0, in_sum[0], in_sum[1])
    give = jnp.where(place.core == 0, in_sum[1], in_sum[0])
    got = place.swap_core(give)
    pair = jnp.where(place.core == 0, jnp.stack([mine, got]), jnp.stack([got, mine]))
    in_rows = halves(place, pair).reshape(2, 2, owned, 2, chips, half_units)
    in_rows = in_rows.transpose(2, 3, 4, 1, 0, 5).reshape(owned, 2 * FF).astype(F32)
    down_rows = halves(place, sum_of(down_parts)).reshape(units, D).astype(F32)

    if place.direct:
        attn_half, in_rows, down_rows = tie(sum_of(attn_parts).astype(BF16), in_rows, down_rows)
        attn_sum = halves(place, attn_half)
        lanes = attn_sum[0, :SMALL_ROWS, HALF:].astype(F32)
        s_qv = lanes[0, : 2 * owned]
        s_ob, s_g1, s_b1, s_db, s_g2, s_b2 = [lanes[i, :owned] for i in range(1, 7)]
        s_ib = lanes[BIAS_ROW : BIAS_ROW + 4, : 2 * owned].reshape(-1)
    else:
        attn_sum = reduce_attn(blocks[:4], blocks[4], owned, place)
        turn_sums = sum_of(turn_sums)
        ib_blocks = in_sums.reshape(2, chips, 1, 1, half_units)
        at_core = (jnp.arange(2) == place.core).astype(F32).reshape(1, 1, 2, 1, 1)
        at_narrow = (jnp.arange(2) == place.x).astype(F32).reshape(1, 1, 1, 2, 1)
        sums = [attn_sums[3:5], attn_sums[2], attn_sums[0], attn_sums[1]]
        sums = sums + [ib_blocks * at_core * at_narrow, turn_sums[0], turn_sums[1], turn_sums[2]]
        widths = [v.size // wide for v in sums]
        sums = jnp.concatenate([v.reshape(wide, -1) for v in sums], 1)
        sums = lax.psum(sums, AXES)[lax.axis_index("wide")]
        ends = [sum(widths[: i + 1]) for i in range(len(widths) - 1)]
        s_qv, s_ob, s_g1, s_b1, s_ib, s_db, s_g2, s_b2 = jnp.split(sums, ends)
    attn_rows = attn_sum[..., :HALF].astype(F32)
    full_qkv = jnp.concatenate([attn_rows[0], attn_rows[1, :, :D]], 1)

    return (
        layer_out,
        input_grad,
        full_qkv,
        s_qv,
        attn_rows[1, :, D:],
        s_ob,
        s_g1,
        s_b1,
        in_rows,
        s_ib,
        down_rows,
        s_db,
        s_g2,
        s_b2,
    )


def solution(mesh):
    rows = P(("narrow", "wide"), None)
    marks = P(("narrow", "wide"))
    matrix = P("wide", None)
    vector = P("wide")
    in_specs = (rows, marks, marks, P(), matrix, vector, matrix, vector, vector, vector)
    in_specs = in_specs + (matrix, vector, matrix, vector, vector, vector, rows)
    out_specs = (rows, rows, matrix, vector, matrix, vector, vector, vector)
    out_specs = out_specs + (matrix, vector, matrix, vector, vector, vector)
    return jax.shard_map(body, mesh=mesh, in_specs=in_specs, out_specs=out_specs, check_vma=False)
```
